256 devices in a mesh: refl: 8 (over z_hi, y), slab: 32 (over z_lo, x, core).
Axes of the slice: x: 4, y: 4, z: 8 (z_hi: 2, z_lo: 4; z = z_hi * 4 + z_lo), core: 2. Of those that a mesh axis runs over, the one named last changes fastest.
Arguments:
- amplitude: float32 [128, 128, 128], P('slab', 'refl'), may hold values from 1 to 3
- displacement: float32 [3, 128, 128, 128], P(None, 'slab', 'refl'), may hold values from -12 to 12
- support: int32 [128, 128, 128], P('slab'), may hold values from 0 to 1, as said below
- miller: int32 [8, 3], P('refl'), may hold values from -2 to 2, as said below
- shift_kz: int32 [8], P('refl'), may hold values from 0 to 255
- intensity: float32 [8, 256, 256, 256], P('refl', None, 'slab'), may hold values from 0.02 to 0.5
Outputs:
- grad_amplitude: float32 [128, 128, 128], P('slab', 'refl')
- grad_displacement: float32 [3, 128, 128, 128], P(None, 'slab', 'refl')
The draws below stay inside these ranges and needn't reach their ends.
Inputs may be any that keep to these rules, and one draw needn't show every extreme that they name: 1 inside the object's support, 0 outside. `miller`: no index is zero.
All inputs are finite; a program needn't handle non-finite values.
Results may differ from the reference program's by a relative error of at most 0.0003.
Values sent between devices are 32-bit elements; how exact they have to be, the bound alone decides.
A program may use at most 64 MiB of HBM per device.

```python
import math
import jax
import jax.numpy as jnp
from jax import lax

SUP = 128
GRID = 256
REFLS = 8


def draw_support(key, part):
    keys = jax.random.split(jax.random.fold_in(key, 11), 2)
    offset = jnp.arange(SUP, dtype=jnp.int32) - SUP // 2
    square = offset * offset
    factors = jax.random.randint(keys[0], (3,), 3, 6)
    value = factors[0] * square[:, None, None] + factors[1] * square[None, :, None] + factors[2] * square[None, None, :]
    limit = 3 * (SUP // 2) * (SUP // 2)
    spread = SUP // 2 * (SUP // 2) // 2
    noise = jax.random.randint(keys[1], (SUP, SUP, SUP), -spread, spread)
    return jnp.where(value + noise < limit, 1, 0).astype(jnp.int32)


def draw_miller(key, part):
    keys = jax.random.split(jax.random.fold_in(key, 23), 2)
    magnitude = jax.random.randint(keys[0], (REFLS, 3), 1, 3)
    polarity = 2 * jax.random.randint(keys[1], (REFLS, 3), 0, 2) - 1
    drawn = (magnitude * polarity).astype(jnp.int32)
    drawn = drawn.at[0, 0].set(2)
    drawn = drawn.at[0, 1].set(-2)
    return drawn.astype(jnp.int32)


def touch_ends(entries, own_key, smallest, top_value):
    longest = entries.shape.index(max(entries.shape))
    spots = []
    for shift in (0, 1):
        where = [jax.random.randint(jax.random.fold_in(own_key, axis), (), 0, length) for axis, length in enumerate(entries.shape)]
        where[longest] = (where[longest] + shift) % entries.shape[longest]
        spots.append(tuple(where))
    return entries.at[spots[0]].set(smallest).at[spots[1]].set(top_value)


def block_levels(rng, dims, cuts, least, top_value):
    factor_of = 1.0
    for axis_at, parts in cuts:
        steps = jax.random.uniform(jax.random.fold_in(jax.random.fold_in(rng, 6), axis_at), (parts,), jnp.float32, least / len(cuts), top_value / len(cuts))
        factor_of = factor_of * jnp.repeat(jnp.exp(steps), dims[axis_at] // parts).reshape((-1,) + (1,) * (len(dims) - 1 - axis_at))
    return factor_of


def centred(rng, shape, width, most, cuts=(), kind=jnp.bfloat16):
    result = width * jax.random.normal(rng, shape, jnp.float32)
    if cuts:
        result = result * block_levels(rng, shape, cuts, -0.22, 0.18)
    return jnp.clip(result, -most, most).astype(kind)


def setup_inputs(seed: int = 0) -> dict:
    key_of = jax.random.split(jax.random.key(seed), 7)
    amplitude = jnp.clip(1.0 + 2.0 * jax.random.uniform(key_of[0], (SUP, SUP, SUP), jnp.float32) ** block_levels(key_of[0], (SUP, SUP, SUP), ((0, 32), (1, 8)), -0.2, 0.2), 1.0, 3.0)
    displacement = centred(key_of[1], (3, SUP, SUP, SUP), 2.0, 12.0, ((1, 32), (2, 8)), jnp.float32)
    support = draw_support(jax.random.fold_in(key_of[6], 71), 0)
    miller = draw_miller(jax.random.fold_in(key_of[6], 71), 0)
    shift_kz = touch_ends(jax.random.randint(key_of[4], (REFLS,), 0, GRID), jax.random.fold_in(key_of[4], 1), 0, GRID - 1).astype(jnp.int32)
    intensity = jnp.clip(jnp.exp(math.log(0.5) - 3.218876 * jax.random.uniform(key_of[5], (REFLS, GRID, GRID, GRID), jnp.float32) ** block_levels(key_of[5], (REFLS, GRID, GRID, GRID), ((0, 8), (2, 32)), -0.2, 0.2)), 0.02, 0.5)
    return {"amplitude": amplitude, "displacement": displacement, "support": support, "miller": miller, "shift_kz": shift_kz, "intensity": intensity}


STRAIN_WEIGHT = 0.05
EDGE_WEIGHT = 0.05


def laplace(field):
    padded = jnp.pad(field, 1)
    beside = padded[2:, 1:-1, 1:-1] + padded[:-2, 1:-1, 1:-1]
    beside = beside + padded[1:-1, 2:, 1:-1] + padded[1:-1, :-2, 1:-1]
    beside = beside + padded[1:-1, 1:-1, 2:] + padded[1:-1, 1:-1, :-2]
    return 6.0 * field - beside


def reference(amplitude, displacement, support, miller, shift_kz, intensity):
    mask = support.astype(amplitude.dtype)
    weight = mask * amplitude

    def one_reflection(carry, index):
        row = miller[index].astype(amplitude.dtype)
        phase = row[0] * displacement[0] + row[1] * displacement[1] + row[2] * displacement[2]
        cosine = jnp.cos(phase)
        sine = jnp.sin(phase)
        target = weight * cosine + 1j * (weight * sine)
        padded = jnp.zeros((GRID, GRID, GRID), target.dtype).at[:SUP, :SUP, :SUP].set(target)
        spectrum = jnp.fft.fftn(padded, norm="ortho")
        measured = jnp.roll(intensity[index], -shift_kz[index], axis=2)
        power = jnp.real(spectrum) ** 2 + jnp.imag(spectrum) ** 2
        residual = 4.0 * (power - measured) * spectrum
        back = jnp.fft.ifftn(residual, norm="ortho")[:SUP, :SUP, :SUP]
        along = jnp.real(back) * cosine + jnp.imag(back) * sine
        across = weight * (jnp.imag(back) * cosine - jnp.real(back) * sine)
        grad_amp = carry[0] + mask * along
        grad_disp = carry[1] + row[:, None, None, None] * across[None]
        return (grad_amp, grad_disp), None

    start = (jnp.zeros_like(amplitude), jnp.zeros_like(displacement))
    (grad_amp, grad_disp), unused = lax.scan(one_reflection, start, jnp.arange(REFLS, dtype=jnp.int32))
    grad_amp = grad_amp + 2.0 * EDGE_WEIGHT * mask * laplace(weight)
    strain = jnp.stack([laplace(displacement[comp]) for comp in range(3)])
    grad_disp = grad_disp + 2.0 * STRAIN_WEIGHT * strain
    return grad_amp, grad_disp
```

```python
import jax
import jax.numpy as jnp
from jax import lax
from jax.sharding import PartitionSpec as P

STRAIN_WEIGHT = 0.05
EDGE_WEIGHT = 0.05


def cut_along(x, dim, count):
    before, after = (x.shape[:dim], x.shape[dim + 1 :])
    return jnp.moveaxis(x.reshape(*before, count, -1, *after), dim, 0)


def extended_2(x, sides, width):
    edges = {}
    for axis, dim in sides:
        count, length = (lax.axis_size(axis), x.shape[dim])
        up = [(i, (i + 1) % count) for i in range(count - 1)]
        last = lax.slice_in_dim(x, length - width, length, axis=dim)
        leading = lax.slice_in_dim(x, 0, width, axis=dim)
        edges[dim] = (
            lax.ppermute(last, axis, up),
            lax.ppermute(leading, axis, [(b, a) for a, b in up]),
        )
    done = []
    for _, dim in sides:
        low, high = edges[dim]
        around = [(width, width) if d in done else (0, 0) for d in range(x.ndim)]
        x = jnp.concatenate([jnp.pad(low, around), x, jnp.pad(high, around)], axis=dim)
        done.append(dim)
    return x


def tables(freqs, places, length):
    product = freqs[:, None] * places[None, :] % length
    angle = 2.0 * jnp.pi / length * product.astype(jnp.float32)
    factor = length ** (-0.5)
    return (jnp.cos(angle) * factor, jnp.sin(angle) * factor)


def transform(parts, matrices, pattern, forward):
    cosine, sine = matrices

    def multiply(matrix, operand):
        return jnp.einsum(
            pattern,
            operand,
            matrix,
            precision=lax.Precision.HIGH,
            preferred_element_type=jnp.float32,
        )

    cos_real = multiply(cosine, parts[0])
    cos_imag = multiply(cosine, parts[1])
    sin_real = multiply(sine, parts[0])
    sin_imag = multiply(sine, parts[1])
    if forward:
        return (cos_real + sin_imag, cos_imag - sin_real)
    return (cos_real - sin_imag, cos_imag + sin_real)


def everyone(x, axis):
    count = lax.axis_size(axis)
    spread = jnp.broadcast_to(x[None], (count, *x.shape))
    return lax.all_to_all(spread, axis, 0, 0, tiled=True)


def body(amplitude, displacement, support, miller, shift_kz, intensity):
    owned = amplitude.shape[1]
    edge = amplitude.shape[2]
    grid = 2 * edge
    refl_index = lax.axis_index("refl")
    mask = support.astype(jnp.float32)
    mask_own = lax.dynamic_slice_in_dim(mask, refl_index * owned, owned, 1)
    fields = jnp.concatenate([(mask_own * amplitude)[None], displacement], axis=0)
    whole = everyone(fields, "refl")
    weight, d0, d1, d2 = [
        jnp.moveaxis(whole[:, c], 0, 1).reshape(amplitude.shape[0], edge, edge) for c in range(4)
    ]
    millers = everyone(miller[0].astype(jnp.float32), "refl")
    miller_row = miller[0].astype(jnp.float32)
    every = jnp.arange(grid, dtype=jnp.int32)
    inner = jnp.arange(edge, dtype=jnp.int32)
    turn = (shift_kz[0] * inner % grid).astype(jnp.float32) * (2.0 * jnp.pi / grid)
    phase = miller_row[0] * d0 + miller_row[1] * d1 + miller_row[2] * d2 + turn
    cosine = jnp.cos(phase)
    sine = jnp.sin(phase)
    target = (weight * cosine, weight * sine)
    half_mats = tables(every, inner, grid)
    why_done = transform(target, half_mats, "anz,kn->akz", True)
    both = jnp.stack(why_done)
    moved = lax.all_to_all(both, "slab", 2, 1, tiled=True)
    zed_done = transform(moved, half_mats, "xyn,kn->xyk", True)
    spectrum = transform(zed_done, half_mats, "nyk,xn->xyk", True)
    power = spectrum[0] * spectrum[0] + spectrum[1] * spectrum[1]
    excess = 4.0 * (power - intensity[0])
    residual = (excess * spectrum[0], excess * spectrum[1])
    back_x = transform(residual, half_mats, "xyk,xn->nyk", False)
    back_z = transform(back_x, half_mats, "xyk,kn->xyn", False)
    returned = lax.all_to_all(jnp.stack(back_z), "slab", 1, 2, tiled=True)
    adjoint = transform(returned, half_mats, "akz,kn->anz", False)
    along = adjoint[0] * cosine + adjoint[1] * sine
    across = weight * (adjoint[1] * cosine - adjoint[0] * sine)
    pair = jnp.stack([along, across])
    parts = lax.all_to_all(cut_along(pair, 2, lax.axis_size("refl")), "refl", 0, 0, tiled=True)
    summed_amp = mask_own * jnp.sum(parts[:, 0], axis=0)
    summed_disp = jnp.sum(millers[:, :, None, None, None] * parts[:, 1][:, None], axis=0)
    extended = extended_2(fields, (("refl", 2), ("slab", 1)), 1)
    extended = jnp.pad(extended, ((0, 0), (0, 0), (0, 0), (1, 1)))
    centre = extended[:, 1:-1, 1:-1, 1:-1]
    beside = extended[:, 2:, 1:-1, 1:-1] + extended[:, :-2, 1:-1, 1:-1]
    beside = beside + extended[:, 1:-1, 2:, 1:-1] + extended[:, 1:-1, :-2, 1:-1]
    beside = beside + extended[:, 1:-1, 1:-1, 2:] + extended[:, 1:-1, 1:-1, :-2]
    lapped = 6.0 * centre - beside
    amp_total = summed_amp + 2.0 * EDGE_WEIGHT * mask_own * lapped[0]
    disp_total = summed_disp + 2.0 * STRAIN_WEIGHT * lapped[1:]
    return (amp_total, disp_total)


def solution(mesh):
    placed = (
        P("slab", "refl", None),
        P(None, "slab", "refl", None),
        P("slab", None, None),
        P("refl", None),
        P("refl"),
        P("refl", None, "slab", None),
    )
    return jax.shard_map(
        body,
        mesh=mesh,
        in_specs=placed,
        out_specs=(P("slab", "refl", None), P(None, "slab", "refl", None)),
        check_vma=False,
    )
```

```python
import math

import jax
import jax.numpy as jnp
from jax import lax
from jax.experimental import pallas as pl
from jax.experimental.pallas import tpu as pltpu
from jax.sharding import PartitionSpec as P

MESH = pl.DeviceIdType.MESH
F32 = jnp.float32
BF16 = jnp.bfloat16
STRAIN_WEIGHT = 0.05
EDGE_WEIGHT = 0.05
SLABS = 32
ROWS = 4
HALF = SLABS * 32


def sine_turns(v):
    w = v * v
    total = jnp.full_like(v, -((2 * math.pi) ** 11) / math.factorial(11))
    for power in (9, 7, 5, 3, 1):
        sign = 1.0 if power % 4 == 1 else -1.0
        total = total * w + sign * (2 * math.pi) ** power / math.factorial(power)
    return total * v


def cos_sin_turns(t):
    t = t - jnp.floor(t + 0.5)
    size = jnp.abs(t)
    cosine = sine_turns(0.25 - size)
    sine = sine_turns(0.25 - jnp.abs(size - 0.25))
    return cosine, jnp.where(t < 0.0, -sine, sine)


def split(x):
    high = x.astype(BF16)
    low = (x - high.astype(F32)).astype(BF16)
    return high, low


def stacked(x):
    high, low = split(x)
    return jnp.concatenate([high, low, high], axis=0)


def abreast(x):
    high, low = split(x)
    return jnp.concatenate([high, low, high], axis=1)


def dot(a, b):
    return jnp.dot(a, b, preferred_element_type=F32)


def freq_y(i):
    return 8 * ((i >> 1) & 31) + 4 * (i >> 8) + ((i >> 6) & 3), i & 1


def freq_plain(i):
    return i & 255, i >> 8


def place_plain(i):
    return i & 127, i >> 7


def place_x(i):
    return 4 * (i & 31) + ((i >> 5) & 3), i >> 7


def fill_table(ref, shape, row_is_freq, freq, place, on_left):
    rows, cols = shape
    chunk = 32

    def step(j, carry):
        start = pl.multiple_of(j * chunk, chunk)
        row = lax.broadcasted_iota(jnp.int32, (chunk, cols), 0) + start
        col = lax.broadcasted_iota(jnp.int32, (chunk, cols), 1)
        if row_is_freq:
            k, kc = freq(row)
            n, nc = place(col)
        else:
            k, kc = freq(col)
            n, nc = place(row)
        turns = ((k * n + 64 * (kc - nc) + 128) & 255) - 128
        t = turns.astype(F32) * (1.0 / 256.0)
        high, low = split(sine_turns(0.25 - jnp.abs(t)) * (1.0 / 16.0))
        if on_left:
            ref[pl.ds(start, chunk), 0:cols] = high
            ref[pl.ds(start, chunk), cols : 2 * cols] = high
            ref[pl.ds(start, chunk), 2 * cols : 3 * cols] = low
        else:
            ref[pl.ds(start, chunk), :] = high
            ref[pl.ds(pl.multiple_of(rows + start, chunk), chunk), :] = high
            ref[pl.ds(pl.multiple_of(2 * rows + start, chunk), chunk), :] = low
        return carry

    lax.fori_loop(0, rows // chunk, step, 0)


def kernel(
    amp_ref, disp_ref, sup_hbm, miller_ref, shift_ref, int_hbm,
    amp_out, disp_out,
    sup, inten, own, mate, mill, ey_send, ey_recv, ex_recv, trig, obj, obj_all, bcat,
    fwd_send, fwd_recv, back_send, back_recv, ydone, ydone_all, part, part_recv,
    y_fwd, y_back, x_fwd, x_back, z_fwd, z_back,
    load_sem, mate_sem, mill_sem, edge_sem, peer_sem, peer_back_sem, slab_sem, slab_back_sem, part_sem,
):
    refl = lax.axis_index("refl")
    me = lax.axis_index("slab")
    zh = refl // 4
    yy = lax.rem(refl, 4)
    mate_id = lax.rem(refl + 4, 8)

    def peer_of(t):
        return zh * 4 + lax.rem(yy + t, 4)

    sup_copy = pltpu.make_async_copy(
        sup_hbm.at[:, pl.ds(pl.multiple_of(refl * 16, 16), 16), :], sup, load_sem.at[0]
    )
    sup_copy.start()
    int_copies = [
        pltpu.make_async_copy(int_hbm.at[:, pl.ds(128 * j, 128)], inten.at[j], load_sem.at[1 + j])
        for j in range(2)
    ]
    for copy in int_copies:
        copy.start()

    barrier = pltpu.get_barrier_semaphore()

    def greet_slab(j, carry):
        pl.semaphore_signal(
            barrier, inc=1, device_id={"slab": lax.rem(me + j, SLABS)}, device_id_type=MESH
        )
        return carry

    def greet_refl(j, carry):
        pl.semaphore_signal(
            barrier, inc=1, device_id={"refl": lax.rem(refl + j, 8)}, device_id_type=MESH
        )
        return carry

    lax.fori_loop(1, 8, greet_refl, 0)
    lax.fori_loop(1, SLABS, greet_slab, 0)

    own[1:4] = disp_ref[...]
    lane_row = lax.broadcasted_iota(jnp.int32, (8, 128), 0)
    tile = jnp.where(
        lane_row == 0,
        miller_ref[0, 0].astype(F32),
        jnp.where(
            lane_row == 1,
            miller_ref[0, 1].astype(F32),
            jnp.where(lane_row == 2, miller_ref[0, 2].astype(F32), shift_ref[0].astype(F32)),
        ),
    )
    mill[yy] = tile
    sup_copy.wait()
    mask = sup[...].astype(F32)
    own[0] = mask * amp_ref[...]
    for f in range(4):
        for x in range(ROWS):
            at = f * 4 + x
            ey_send[0, at : at + 1, :] = own[f, x, 0:1, :]
            ey_send[1, at : at + 1, :] = own[f, x, 15:16, :]

    pl.semaphore_wait(barrier, 38)

    def remote(src, dst, sems, axis, target):
        return pltpu.make_async_remote_copy(
            src_ref=src,
            dst_ref=dst,
            send_sem=sems.at[0],
            recv_sem=sems.at[1],
            device_id={axis: target},
            device_id_type=MESH,
        )

    mate_copy = remote(own, mate, mate_sem, "refl", mate_id)
    mate_copy.start()
    mill_copies = [
        remote(mill.at[yy], mill.at[yy], mill_sem.at[t], "refl", peer_of(t)) for t in (1, 2, 3)
    ]
    for copy in mill_copies:
        copy.start()

    has = (refl > 0, refl < 7, me > 0, me < SLABS - 1)
    down_y = remote(ey_send.at[0], ey_recv.at[1], edge_sem.at[0], "refl", lax.rem(refl + 7, 8))
    up_y = remote(ey_send.at[1], ey_recv.at[0], edge_sem.at[1], "refl", lax.rem(refl + 1, 8))
    down_x = remote(own.at[:, 0], ex_recv.at[1], edge_sem.at[2], "slab", lax.rem(me + SLABS - 1, SLABS))
    up_x = remote(own.at[:, 3], ex_recv.at[0], edge_sem.at[3], "slab", lax.rem(me + 1, SLABS))
    edges = (down_y, up_y, down_x, up_x)
    for there, copy in zip(has, edges):
        pl.when(there)(copy.start)

    def nothing(ref, at):
        def fill():
            ref[at] = jnp.zeros(ref.shape[1:], F32)
        return fill

    for there, ref, at in zip(has, (ey_recv, ey_recv, ex_recv, ex_recv), (0, 1, 0, 1)):
        pl.when(jnp.logical_not(there))(nothing(ref, at))

    def place_y(i):
        side = ((i >> 4) & 1) + zh
        return ((side & 1) * 4 + (i >> 6)) * 16 + (i & 15), (i >> 5) & 1

    fill_table(y_fwd, (512, 256), True, freq_y, place_y, True)
    fill_table(y_back, (256, 512), False, freq_y, place_y, True)
    fill_table(x_fwd, (512, 256), True, freq_plain, place_x, True)
    fill_table(x_back, (256, 512), False, freq_plain, place_x, True)
    fill_table(z_fwd, (256, 512), False, freq_plain, place_plain, False)
    fill_table(z_back, (512, 256), True, freq_plain, place_plain, False)

    for t in (1, 2, 3):
        remote(mill.at[yy], mill.at[yy], mill_sem.at[t], "refl", peer_of(t)).wait_recv()
    mate_copy.wait_recv()
    lane = lax.broadcasted_iota(jnp.int32, (1, 1, 128), 2).astype(F32)

    def objects(t, store):
        coef = mill[lax.rem(yy + t, 4)]
        m0, m1, m2, s = [coef[j : j + 1][None] for j in range(4)]
        turn = s * lane * (1.0 / 256.0)
        turn = turn - jnp.floor(turn)
        for b, fields in enumerate((own, mate)):
            phase = m0 * fields[1] + m1 * fields[2] + m2 * fields[3]
            cosine, sine = cos_sin_turns(phase * (1.0 / (2 * math.pi)) + turn)
            trig[t, 0, b] = cosine
            trig[t, 1, b] = sine
            weight = fields[0]
            store(0, b, weight * cosine)
            store(1, b, weight * sine)

    def keep(t):
        def store(c, b, value):
            obj[t, c, b] = value
        return store

    def keep_own(c, b, value):
        obj_all[yy, c, b] = value

    obj_copies = {}
    for t in (2, 1, 3):
        objects(t, keep(t))
        obj_copies[t] = remote(obj.at[t], obj_all.at[yy], peer_sem.at[t], "refl", peer_of(t))
        obj_copies[t].start()
    objects(0, keep_own)
    for t in (2, 1, 3):
        obj_copies[t].wait_recv()

    for pair in range(2):
        columns = [
            obj_all[:, :, :, 2 * pair + j].reshape(256, 128) for j in range(2)
        ]
        bcat[pair] = stacked(jnp.concatenate(columns, axis=1))

    def slab_sends(src, dst, sems, h):
        def send(j, carry):
            to = lax.rem(me + j, SLABS)
            pltpu.make_async_remote_copy(
                src_ref=src.at[h, pl.ds(pl.multiple_of(to * 32, 32), 32)],
                dst_ref=dst.at[h, pl.ds(pl.multiple_of(me * 32, 32), 32)],
                send_sem=sems.at[0, h],
                recv_sem=sems.at[1, h],
                device_id={"slab": to},
                device_id_type=MESH,
            ).start()
            return carry

        lax.fori_loop(16, SLABS, send, 0)
        lax.fori_loop(1, 16, send, 0)
        mine = pl.ds(pl.multiple_of(me * 32, 32), 32)
        pltpu.make_async_copy(src.at[h, mine], dst.at[h, mine], sems.at[1, h]).start()

    def wait_sent(src, dst, sems, h):
        most = pl.ds(0, HALF - 32)
        pltpu.make_async_copy(src.at[h, most], dst.at[h, most], sems.at[0, h]).wait()

    def wait_arrived(dst, sems, h):
        pltpu.make_async_copy(dst.at[h], dst.at[h], sems.at[1, h]).wait()

    for h in range(2):
        for pair in range(2):
            out = dot(y_fwd[256 * h : 256 * (h + 1), :], bcat[pair])
            for k in range(4):
                for j in range(2):
                    fwd_send[h, pl.ds((2 * pair + j) * 4 + k, 64, stride=16), :] = out[
                        64 * k : 64 * (k + 1), 128 * j : 128 * (j + 1)
                    ]
        slab_sends(fwd_send, fwd_recv, slab_sem, h)

    for copy in int_copies:
        copy.wait()

    for h in range(2):
        wait_arrived(fwd_recv, slab_sem, h)

        def row(k, carry):
            sides = [
                jnp.concatenate(
                    [
                        fwd_recv[h, pl.ds(c * 16 + x * 4 + k, 32, stride=32), :]
                        for x in range(ROWS)
                    ],
                    axis=0,
                )
                for c in range(2)
            ]
            zed = dot(abreast(jnp.concatenate(sides, axis=1)), z_fwd[...])
            spec = dot(
                x_fwd[...], stacked(jnp.concatenate([zed[:, :256], zed[:, 256:]], axis=0))
            )
            real, imag = spec[:256], spec[256:]
            measured = jnp.concatenate(
                [inten[j, pl.ds(4 * h + k, 256, stride=8), :] for j in range(2)], axis=1
            )
            excess = 4.0 * (real * real + imag * imag - measured)
            residual = jnp.concatenate([excess * real, excess * imag], axis=0)
            back = dot(x_back[...], stacked(residual))
            out = dot(abreast(jnp.concatenate([back[:128], back[128:]], axis=1)), z_back[...])
            for c in range(2):
                for x in range(ROWS):
                    back_send[h, pl.ds(c * 16 + x * 4 + k, 32, stride=32), :] = out[
                        32 * x : 32 * (x + 1), 128 * c : 128 * (c + 1)
                    ]
            return carry

        lax.fori_loop(0, 4, row, 0)
        slab_sends(back_send, back_recv, slab_back_sem, h)

    for h in range(2):
        wait_arrived(back_recv, slab_back_sem, h)

    for pair in range(2):
        columns = [
            jnp.concatenate(
                [
                    back_recv[h, pl.ds((2 * pair + j) * 4 + k, 64, stride=16), :]
                    for h in range(2)
                    for k in range(4)
                ],
                axis=0,
            )
            for j in range(2)
        ]
        out = dot(y_back[...], stacked(jnp.concatenate(columns, axis=1)))
        for j in range(2):
            ydone[:, :, :, 2 * pair + j] = out[:, 128 * j : 128 * (j + 1)].reshape(4, 2, 2, 16, 128)
    done_copies = {}
    for t in (2, 1, 3):
        done_copies[t] = remote(
            ydone.at[lax.rem(yy + t, 4)], ydone_all.at[4 - t], peer_back_sem.at[t], "refl", peer_of(t)
        )
        done_copies[t].start()
    for t in (2, 1, 3):
        done_copies[t].wait_recv()

    def summed(b):
        totals = [jnp.zeros((ROWS, 16, 128), F32) for _ in range(4)]
        for t in range(4):
            if t == 0:
                real, imag = ydone[yy, 0, b], ydone[yy, 1, b]
            else:
                real, imag = ydone_all[t, 0, b], ydone_all[t, 1, b]
            cosine, sine = trig[t, 0, b], trig[t, 1, b]
            coef = mill[lax.rem(yy + t, 4)]
            across = imag * cosine - real * sine
            totals[0] = totals[0] + real * cosine + imag * sine
            for c in range(3):
                totals[1 + c] = totals[1 + c] + coef[c : c + 1][None] * across
        return totals

    for f, total in enumerate(summed(1)):
        part[f] = total
    part_copy = remote(part, part_recv, part_sem, "refl", mate_id)
    part_copy.start()
    totals = summed(0)

    came = ((has[1], up_y), (has[0], down_y), (has[3], up_x), (has[2], down_x))
    for (there, copy) in ((has[0], up_y), (has[1], down_y), (has[2], up_x), (has[3], down_x)):
        pl.when(there)(copy.wait_recv)
    sub = lax.broadcasted_iota(jnp.int32, (ROWS, 16, 128), 1)
    last = lax.broadcasted_iota(jnp.int32, (ROWS, 16, 128), 2)
    lapped = []
    for f in range(4):
        x = own[f]
        beside = jnp.concatenate([ex_recv[0, f][None], x[:3]], axis=0)
        beside = beside + jnp.concatenate([x[1:], ex_recv[1, f][None]], axis=0)
        low = ey_recv[0, 4 * f : 4 * f + 4, :][:, None, :]
        high = ey_recv[1, 4 * f : 4 * f + 4, :][:, None, :]
        beside = beside + jnp.where(sub == 0, low, pltpu.roll(x, 1, 1))
        beside = beside + jnp.where(sub == 15, high, pltpu.roll(x, 15, 1))
        beside = beside + jnp.where(last == 0, 0.0, pltpu.roll(x, 1, 2))
        beside = beside + jnp.where(last == 127, 0.0, pltpu.roll(x, 127, 2))
        lapped.append(6.0 * x - beside)

    part_copy.wait_recv()
    mask = sup[...].astype(F32)
    amp_out[...] = mask * (totals[0] + part_recv[0]) + 2.0 * EDGE_WEIGHT * mask * lapped[0]
    for c in range(3):
        disp_out[c] = (
            own[0] * (totals[1 + c] + part_recv[1 + c]) + 2.0 * STRAIN_WEIGHT * lapped[1 + c]
        )

    mate_copy.wait_send()
    for copy in mill_copies:
        copy.wait_send()
    for there, copy in zip(has, edges):
        pl.when(there)(copy.wait_send)
    for t in (1, 2, 3):
        obj_copies[t].wait_send()
        done_copies[t].wait_send()
    for h in range(2):
        wait_sent(fwd_send, fwd_recv, slab_sem, h)
        wait_sent(back_send, back_recv, slab_back_sem, h)
    part_copy.wait_send()


def body(amplitude, displacement, support, miller, shift_kz, intensity):
    vmem = pl.BlockSpec(memory_space=pltpu.VMEM)
    smem = pl.BlockSpec(memory_space=pltpu.SMEM)
    anywhere = pl.BlockSpec(memory_space=pl.ANY)
    block = (ROWS, 16, 128)
    sems = pltpu.SemaphoreType.DMA
    return pl.pallas_call(
        kernel,
        out_shape=(
            jax.ShapeDtypeStruct(block, F32),
            jax.ShapeDtypeStruct((3, *block), F32),
        ),
        in_specs=[vmem, vmem, anywhere, smem, smem, anywhere],
        out_specs=(vmem, vmem),
        scratch_shapes=[
            pltpu.VMEM(block, jnp.int32),
            pltpu.VMEM((2, 2048, 128), F32),
            pltpu.VMEM((4, *block), F32),
            pltpu.VMEM((4, *block), F32),
            pltpu.VMEM((4, 8, 128), F32),
            pltpu.VMEM((2, 16, 128), F32),
            pltpu.VMEM((2, 16, 128), F32),
            pltpu.VMEM((2, 4, 16, 128), F32),
            pltpu.VMEM((4, 2, 2, *block), F32),
            pltpu.VMEM((4, 2, 2, *block), F32),
            pltpu.VMEM((4, 2, 2, *block), F32),
            pltpu.VMEM((2, 768, 256), BF16),
            pltpu.VMEM((2, HALF, 128), F32),
            pltpu.VMEM((2, HALF, 128), F32),
            pltpu.VMEM((2, HALF, 128), F32),
            pltpu.VMEM((2, HALF, 128), F32),
            pltpu.VMEM((4, 2, 2, *block), F32),
            pltpu.VMEM((4, 2, 2, *block), F32),
            pltpu.VMEM((4, *block), F32),
            pltpu.VMEM((4, *block), F32),
            pltpu.VMEM((512, 768), BF16),
            pltpu.VMEM((256, 1536), BF16),
            pltpu.VMEM((512, 768), BF16),
            pltpu.VMEM((256, 1536), BF16),
            pltpu.VMEM((768, 512), BF16),
            pltpu.VMEM((1536, 256), BF16),
            sems((3,)),
            sems((2,)),
            sems((4, 2)),
            sems((4, 2)),
            sems((4, 2)),
            sems((4, 2)),
            sems((2, 2)),
            sems((2, 2)),
            sems((2,)),
        ],
        compiler_params=pltpu.CompilerParams(
            collective_id=0, has_side_effects=True, vmem_limit_bytes=56 * 1024 * 1024
        ),
        name="gradient",
    )(amplitude, displacement, support, miller, shift_kz, intensity.reshape(2048, 256))


def solution(mesh):
    placed = (
        P("slab", "refl", None),
        P(None, "slab", "refl", None),
        P("slab", None, None),
        P("refl", None),
        P("refl"),
        P("refl", None, "slab", None),
    )
    return jax.shard_map(
        body,
        mesh=mesh,
        in_specs=placed,
        out_specs=(P("slab", "refl", None), P(None, "slab", "refl", None)),
        check_vma=False,
    )
```

```python
import math

import jax
import jax.numpy as jnp
from jax import lax
from jax.experimental import pallas as pl
from jax.experimental.pallas import tpu as pltpu
from jax.sharding import PartitionSpec as P

MESH = pl.DeviceIdType.MESH
F32 = jnp.float32
BF16 = jnp.bfloat16
STRAIN_WEIGHT = 0.05
EDGE_WEIGHT = 0.05
SLABS = 32
ROWS = 4
WIDTH = 2
LINES = SLABS * 16


def sine_turns(v):
    w = v * v
    total = jnp.full_like(v, -((2 * math.pi) ** 11) / math.factorial(11))
    for power in (9, 7, 5, 3, 1):
        sign = 1.0 if power % 4 == 1 else -1.0
        total = total * w + sign * (2 * math.pi) ** power / math.factorial(power)
    return total * v


def cos_sin_turns(t):
    t = t - jnp.floor(t + 0.5)
    size = jnp.abs(t)
    cosine = sine_turns(0.25 - size)
    sine = sine_turns(0.25 - jnp.abs(size - 0.25))
    return cosine, jnp.where(t < 0.0, -sine, sine)


def split(x):
    high = x.astype(BF16)
    low = (x - high.astype(F32)).astype(BF16)
    return high, low


def stacked(x):
    high, low = split(x)
    return jnp.concatenate([high, low, high], axis=0)


def abreast(x):
    high, low = split(x)
    return jnp.concatenate([high, low, high], axis=1)


def dot(a, b):
    return jnp.dot(a, b, preferred_element_type=F32)


def freq_y(i):
    return 8 * ((i >> 1) & 31) + 4 * (i >> 8) + ((i >> 6) & 3), i & 1


def freq_plain(i):
    return i & 255, i >> 8


def place_plain(i):
    return i & 127, i >> 7


def place_x(i):
    return 4 * (i & 31) + ((i >> 5) & 3), i >> 7


def fill_table(ref, shape, row_is_freq, freq, place, on_left):
    rows, cols = shape
    chunk = 32

    def step(j, carry):
        start = pl.multiple_of(j * chunk, chunk)
        row = lax.broadcasted_iota(jnp.int32, (chunk, cols), 0) + start
        col = lax.broadcasted_iota(jnp.int32, (chunk, cols), 1)
        if row_is_freq:
            k, kc = freq(row)
            n, nc = place(col)
        else:
            k, kc = freq(col)
            n, nc = place(row)
        turns = ((k * n + 64 * (kc - nc) + 128) & 255) - 128
        t = turns.astype(F32) * (1.0 / 256.0)
        high, low = split(sine_turns(0.25 - jnp.abs(t)) * (1.0 / 16.0))
        if on_left:
            ref[pl.ds(start, chunk), 0:cols] = high
            ref[pl.ds(start, chunk), cols : 2 * cols] = high
            ref[pl.ds(start, chunk), 2 * cols : 3 * cols] = low
        else:
            ref[pl.ds(start, chunk), :] = high
            ref[pl.ds(pl.multiple_of(rows + start, chunk), chunk), :] = high
            ref[pl.ds(pl.multiple_of(2 * rows + start, chunk), chunk), :] = low
        return carry

    lax.fori_loop(0, rows // chunk, step, 0)


def kernel(
    amp_ref, disp_ref, sup_hbm, miller_ref, shift_ref, int_hbm,
    amp_out, disp_out,
    sup, inten, own, mate, mill, ey_send, ey_recv, ex_recv, trig, obj, obj_all, bcat,
    fwd_send, fwd_recv, back_send, back_recv, ydone, ydone_all, part, part_own, part_recv, lapped,
    y_fwd, y_back, x_fwd, x_back, z_fwd, z_back,
    load_sem, mate_sem, mill_sem, edge_sem, peer_sem, peer_back_sem, slab_sem, slab_back_sem, part_sem,
):
    refl = lax.axis_index("refl")
    me = lax.axis_index("slab")
    zh = refl // 4
    yy = lax.rem(refl, 4)
    mate_id = lax.rem(refl + 4, 8)

    def peer_of(t):
        return zh * 4 + lax.rem(yy + t, 4)

    sup_copy = pltpu.make_async_copy(
        sup_hbm.at[:, pl.ds(pl.multiple_of(refl * 16, 16), 16), :], sup, load_sem.at[0]
    )
    sup_copy.start()
    int_copies = [
        pltpu.make_async_copy(int_hbm.at[:, pl.ds(128 * j, 128)], inten.at[j], load_sem.at[1 + j])
        for j in range(2)
    ]
    for copy in int_copies:
        copy.start()

    barrier = pltpu.get_barrier_semaphore()

    def greet_slab(j, carry):
        pl.semaphore_signal(
            barrier, inc=1, device_id={"slab": lax.rem(me + j, SLABS)}, device_id_type=MESH
        )
        return carry

    def greet_refl(j, carry):
        pl.semaphore_signal(
            barrier, inc=1, device_id={"refl": lax.rem(refl + j, 8)}, device_id_type=MESH
        )
        return carry

    lax.fori_loop(1, 8, greet_refl, 0)
    lax.fori_loop(1, SLABS, greet_slab, 0)

    own[1:4] = disp_ref[...]
    lane_row = lax.broadcasted_iota(jnp.int32, (8, 128), 0)
    tile = jnp.where(
        lane_row == 0,
        miller_ref[0, 0].astype(F32),
        jnp.where(
            lane_row == 1,
            miller_ref[0, 1].astype(F32),
            jnp.where(lane_row == 2, miller_ref[0, 2].astype(F32), shift_ref[0].astype(F32)),
        ),
    )
    mill[yy] = tile
    sup_copy.wait()
    mask = sup[...].astype(F32)
    own[0] = mask * amp_ref[...]
    for f in range(4):
        for x in range(ROWS):
            at = f * 4 + x
            ey_send[0, at : at + 1, :] = own[f, x, 0:1, :]
            ey_send[1, at : at + 1, :] = own[f, x, 15:16, :]

    pl.semaphore_wait(barrier, 38)

    def remote(src, dst, sems, axis, target):
        return pltpu.make_async_remote_copy(
            src_ref=src,
            dst_ref=dst,
            send_sem=sems.at[0],
            recv_sem=sems.at[1],
            device_id={axis: target},
            device_id_type=MESH,
        )

    def planes(p):
        return pl.ds(WIDTH * p, WIDTH)

    mate_copies = [
        remote(own.at[:, planes(p)], mate.at[:, planes(p)], mate_sem.at[p], "refl", mate_id)
        for p in range(2)
    ]
    mill_copies = [
        remote(mill.at[yy], mill.at[yy], mill_sem.at[t], "refl", peer_of(t)) for t in (1, 2, 3)
    ]
    for copy in mill_copies + mate_copies:
        copy.start()

    has = (refl > 0, refl < 7, me > 0, me < SLABS - 1)
    down_y = remote(ey_send.at[0], ey_recv.at[1], edge_sem.at[0], "refl", lax.rem(refl + 7, 8))
    up_y = remote(ey_send.at[1], ey_recv.at[0], edge_sem.at[1], "refl", lax.rem(refl + 1, 8))
    down_x = remote(own.at[:, 0], ex_recv.at[1], edge_sem.at[2], "slab", lax.rem(me + SLABS - 1, SLABS))
    up_x = remote(own.at[:, 3], ex_recv.at[0], edge_sem.at[3], "slab", lax.rem(me + 1, SLABS))
    edges = (down_y, up_y, down_x, up_x)
    for there, copy in zip(has, edges):
        pl.when(there)(copy.start)

    def nothing(ref, at):
        def fill():
            ref[at] = jnp.zeros(ref.shape[1:], F32)
        return fill

    for there, ref, at in zip(has, (ey_recv, ey_recv, ex_recv, ex_recv), (0, 1, 0, 1)):
        pl.when(jnp.logical_not(there))(nothing(ref, at))

    def place_y(i):
        side = ((i >> 4) & 1) + zh
        return ((side & 1) * 4 + (i >> 6)) * 16 + (i & 15), (i >> 5) & 1

    fill_table(y_fwd, (512, 256), True, freq_y, place_y, True)
    for copy in mill_copies:
        copy.wait_recv()
    lane = lax.broadcasted_iota(jnp.int32, (1, 1, 128), 2).astype(F32)

    def objects(t, p, ref):
        coef = mill[lax.rem(yy + t, 4)]
        m0, m1, m2, s = [coef[j : j + 1][None] for j in range(4)]
        turn = s * lane * (1.0 / 256.0)
        turn = turn - jnp.floor(turn)
        for b, fields in enumerate((own, mate)):
            weight, d0, d1, d2 = [fields[f, planes(p)] for f in range(4)]
            phase = m0 * d0 + m1 * d1 + m2 * d2
            cosine, sine = cos_sin_turns(phase * (1.0 / (2 * math.pi)) + turn)
            trig[t, 0, b, planes(p)] = cosine
            trig[t, 1, b, planes(p)] = sine
            ref[0, b] = weight * cosine
            ref[1, b] = weight * sine

    obj_copies = [{}, {}]
    for p in range(2):
        mate_copies[p].wait_recv()
        for t in (2, 1, 3):
            objects(t, p, obj.at[t, p])
            copy = remote(obj.at[t, p], obj_all.at[p, yy], peer_sem.at[p, t], "refl", peer_of(t))
            copy.start()
            obj_copies[p][t] = copy
        objects(0, p, obj_all.at[p, yy])

    def slab_sends(src, dst, sems, at, g):
        def lines(i):
            return (*at, pl.ds(pl.multiple_of(i * 16, 16), 16))

        def send(j, carry):
            to = lax.rem(me + j, SLABS)
            pltpu.make_async_remote_copy(
                src_ref=src.at[lines(to)],
                dst_ref=dst.at[lines(me)],
                send_sem=sems.at[0, g],
                recv_sem=sems.at[1, g],
                device_id={"slab": to},
                device_id_type=MESH,
            ).start()
            return carry

        lax.fori_loop(16, SLABS, send, 0)
        lax.fori_loop(1, 16, send, 0)
        pltpu.make_async_copy(src.at[lines(me)], dst.at[lines(me)], sems.at[1, g]).start()

    def wait_sent(src, dst, sems, at, g):
        most = (*at, pl.ds(0, LINES - 16))
        pltpu.make_async_copy(src.at[most], dst.at[most], sems.at[0, g]).wait()

    def wait_arrived(dst, sems, at, g):
        pltpu.make_async_copy(dst.at[at], dst.at[at], sems.at[1, g]).wait()

    whole = slice(None)
    fwd_groups = ((0, whole), (1, 0), (1, 1))
    back_groups = ((0, whole), (1, 0), (1, 1))

    for p in range(2):
        for t in (1, 3, 2):
            obj_copies[p][t].wait_recv()
        columns = [obj_all[p, :, :, :, j].reshape(256, 128) for j in range(WIDTH)]
        bcat[...] = stacked(jnp.concatenate(columns, axis=1))
        for h in range(2):
            out = dot(y_fwd[256 * h : 256 * (h + 1), :], bcat[...])
            for k in range(4):
                for j in range(WIDTH):
                    fwd_send[p, h, pl.ds(4 * j + k, 64, stride=8), :] = out[
                        64 * k : 64 * (k + 1), 128 * j : 128 * (j + 1)
                    ]
            if p == 1:
                slab_sends(fwd_send, fwd_recv, slab_sem, fwd_groups[1 + h], 1 + h)
        if p == 0:
            slab_sends(fwd_send, fwd_recv, slab_sem, fwd_groups[0], 0)

    fill_table(x_fwd, (512, 256), True, freq_plain, place_x, True)
    fill_table(z_fwd, (256, 512), False, freq_plain, place_plain, False)
    fill_table(x_back, (256, 512), False, freq_plain, place_x, True)
    fill_table(z_back, (512, 256), True, freq_plain, place_plain, False)
    fill_table(y_back, (256, 512), False, freq_y, place_y, True)
    for copy in int_copies:
        copy.wait()

    for h in range(2):
        for g in ((0, 1), (2,))[h]:
            wait_arrived(fwd_recv, slab_sem, fwd_groups[g], g)

        def row(k, carry):
            sides = [
                jnp.concatenate(
                    [
                        fwd_recv[x // 2, h, pl.ds(c * 8 + (x % 2) * 4 + k, 32, stride=16), :]
                        for x in range(ROWS)
                    ],
                    axis=0,
                )
                for c in range(2)
            ]
            zed = dot(abreast(jnp.concatenate(sides, axis=1)), z_fwd[...])
            spec = dot(
                x_fwd[...], stacked(jnp.concatenate([zed[:, :256], zed[:, 256:]], axis=0))
            )
            real, imag = spec[:256], spec[256:]
            measured = jnp.concatenate(
                [inten[j, pl.ds(4 * h + k, 256, stride=8), :] for j in range(2)], axis=1
            )
            excess = 4.0 * (real * real + imag * imag - measured)
            residual = jnp.concatenate([excess * real, excess * imag], axis=0)
            back = dot(x_back[...], stacked(residual))
            out = dot(abreast(jnp.concatenate([back[:128], back[128:]], axis=1)), z_back[...])
            for c in range(2):
                for x in range(ROWS):
                    back_send[h, x // 2, pl.ds(c * 8 + (x % 2) * 4 + k, 32, stride=16), :] = out[
                        32 * x : 32 * (x + 1), 128 * c : 128 * (c + 1)
                    ]
            return carry

        lax.fori_loop(0, 4, row, 0)
        for g in ((0,), (1, 2))[h]:
            slab_sends(back_send, back_recv, slab_back_sem, back_groups[g], g)

    for there, copy in ((has[0], up_y), (has[1], down_y), (has[2], up_x), (has[3], down_x)):
        pl.when(there)(copy.wait_recv)
    sub = lax.broadcasted_iota(jnp.int32, (ROWS, 16, 128), 1)
    last = lax.broadcasted_iota(jnp.int32, (ROWS, 16, 128), 2)
    for f in range(4):
        x = own[f]
        beside = jnp.concatenate([ex_recv[0, f][None], x[:3]], axis=0)
        beside = beside + jnp.concatenate([x[1:], ex_recv[1, f][None]], axis=0)
        low = ey_recv[0, 4 * f : 4 * f + 4, :][:, None, :]
        high = ey_recv[1, 4 * f : 4 * f + 4, :][:, None, :]
        beside = beside + jnp.where(sub == 0, low, pltpu.roll(x, 1, 1))
        beside = beside + jnp.where(sub == 15, high, pltpu.roll(x, 15, 1))
        beside = beside + jnp.where(last == 0, 0.0, pltpu.roll(x, 1, 2))
        beside = beside + jnp.where(last == 127, 0.0, pltpu.roll(x, 127, 2))
        lapped[f] = 2.0 * (EDGE_WEIGHT if f == 0 else STRAIN_WEIGHT) * (6.0 * x - beside)

    done_copies = [{}, {}]
    for p in range(2):
        for g in ((0, 1), (2,))[p]:
            wait_arrived(back_recv, slab_back_sem, back_groups[g], g)
        columns = [
            jnp.concatenate(
                [
                    back_recv[h, p, pl.ds(4 * j + k, 64, stride=8), :]
                    for h in range(2)
                    for k in range(4)
                ],
                axis=0,
            )
            for j in range(WIDTH)
        ]
        out = dot(y_back[...], stacked(jnp.concatenate(columns, axis=1)))
        for j in range(WIDTH):
            ydone[p, :, :, :, j] = out[:, 128 * j : 128 * (j + 1)].reshape(4, 2, 2, 16, 128)
        for t in (2, 1, 3):
            copy = remote(
                ydone.at[p, lax.rem(yy + t, 4)],
                ydone_all.at[p, 4 - t],
                peer_back_sem.at[p, t],
                "refl",
                peer_of(t),
            )
            copy.start()
            done_copies[p][t] = copy

    def summed(b, p):
        totals = [jnp.zeros((WIDTH, 16, 128), F32) for _ in range(4)]
        for t in range(4):
            if t == 0:
                real, imag = ydone[p, yy, 0, b], ydone[p, yy, 1, b]
            else:
                real, imag = ydone_all[p, t, 0, b], ydone_all[p, t, 1, b]
            cosine, sine = trig[t, 0, b, planes(p)], trig[t, 1, b, planes(p)]
            coef = mill[lax.rem(yy + t, 4)]
            across = imag * cosine - real * sine
            totals[0] = totals[0] + real * cosine + imag * sine
            for c in range(3):
                totals[1 + c] = totals[1 + c] + coef[c : c + 1][None] * across
        return totals

    part_copies = []
    for p in range(2):
        for t in (1, 3, 2):
            done_copies[p][t].wait_recv()
        for f, total in enumerate(summed(1, p)):
            part[p, f] = total
        copy = remote(part.at[p], part_recv.at[p], part_sem.at[p], "refl", mate_id)
        copy.start()
        part_copies.append(copy)
        for f, total in enumerate(summed(0, p)):
            part_own[p, f] = total

    for p in range(2):
        part_copies[p].wait_recv()
        mask = sup[planes(p)].astype(F32)
        amp_out[planes(p)] = mask * (part_own[p, 0] + part_recv[p, 0] + lapped[0, planes(p)])
        for c in range(3):
            disp_out[c, planes(p)] = (
                own[0, planes(p)] * (part_own[p, 1 + c] + part_recv[p, 1 + c])
                + lapped[1 + c, planes(p)]
            )

    for copy in mill_copies + mate_copies + part_copies:
        copy.wait_send()
    for there, copy in zip(has, edges):
        pl.when(there)(copy.wait_send)
    for p in range(2):
        for t in (1, 2, 3):
            obj_copies[p][t].wait_send()
            done_copies[p][t].wait_send()
    for g in range(3):
        wait_sent(fwd_send, fwd_recv, slab_sem, fwd_groups[g], g)
        wait_sent(back_send, back_recv, slab_back_sem, back_groups[g], g)


def body(amplitude, displacement, support, miller, shift_kz, intensity):
    vmem = pl.BlockSpec(memory_space=pltpu.VMEM)
    smem = pl.BlockSpec(memory_space=pltpu.SMEM)
    anywhere = pl.BlockSpec(memory_space=pl.ANY)
    block = (ROWS, 16, 128)
    chunk = (WIDTH, 16, 128)
    sems = pltpu.SemaphoreType.DMA
    return pl.pallas_call(
        kernel,
        out_shape=(
            jax.ShapeDtypeStruct(block, F32),
            jax.ShapeDtypeStruct((3, *block), F32),
        ),
        in_specs=[vmem, vmem, anywhere, smem, smem, anywhere],
        out_specs=(vmem, vmem),
        scratch_shapes=[
            pltpu.VMEM(block, jnp.int32),
            pltpu.VMEM((2, 2048, 128), F32),
            pltpu.VMEM((4, *block), F32),
            pltpu.VMEM((4, *block), F32),
            pltpu.VMEM((4, 8, 128), F32),
            pltpu.VMEM((2, 16, 128), F32),
            pltpu.VMEM((2, 16, 128), F32),
            pltpu.VMEM((2, 4, 16, 128), F32),
            pltpu.VMEM((4, 2, 2, *block), F32),
            pltpu.VMEM((4, 2, 2, 2, *chunk), F32),
            pltpu.VMEM((2, 4, 2, 2, *chunk), F32),
            pltpu.VMEM((768, 256), BF16),
            pltpu.VMEM((2, 2, LINES, 128), F32),
            pltpu.VMEM((2, 2, LINES, 128), F32),
            pltpu.VMEM((2, 2, LINES, 128), F32),
            pltpu.VMEM((2, 2, LINES, 128), F32),
            pltpu.VMEM((2, 4, 2, 2, *chunk), F32),
            pltpu.VMEM((2, 4, 2, 2, *chunk), F32),
            pltpu.VMEM((2, 4, *chunk), F32),
            pltpu.VMEM((2, 4, *chunk), F32),
            pltpu.VMEM((2, 4, *chunk), F32),
            pltpu.VMEM((4, *block), F32),
            pltpu.VMEM((512, 768), BF16),
            pltpu.VMEM((256, 1536), BF16),
            pltpu.VMEM((512, 768), BF16),
            pltpu.VMEM((256, 1536), BF16),
            pltpu.VMEM((768, 512), BF16),
            pltpu.VMEM((1536, 256), BF16),
            sems((3,)),
            sems((2, 2)),
            sems((4, 2)),
            sems((4, 2)),
            sems((2, 4, 2)),
            sems((2, 4, 2)),
            sems((2, 3)),
            sems((2, 3)),
            sems((2, 2)),
        ],
        compiler_params=pltpu.CompilerParams(
            collective_id=0, has_side_effects=True, vmem_limit_bytes=56 * 1024 * 1024
        ),
        name="gradient",
    )(amplitude, displacement, support, miller, shift_kz, intensity.reshape(2048, 256))


def solution(mesh):
    placed = (
        P("slab", "refl", None),
        P(None, "slab", "refl", None),
        P("slab", None, None),
        P("refl", None),
        P("refl"),
        P("refl", None, "slab", None),
    )
    return jax.shard_map(
        body,
        mesh=mesh,
        in_specs=placed,
        out_specs=(P("slab", "refl", None), P(None, "slab", "refl", None)),
        check_vma=False,
    )
```

```python
import math

import jax
import jax.numpy as jnp
from jax import lax
from jax.experimental import pallas as pl
from jax.experimental.pallas import tpu as pltpu
from jax.sharding import PartitionSpec as P

MESH = pl.DeviceIdType.MESH
F32 = jnp.float32
BF16 = jnp.bfloat16
STRAIN_WEIGHT = 0.05
EDGE_WEIGHT = 0.05
SLABS = 32
ROWS = 4
WIDTH = 2
LINES = SLABS * 16


def sine_turns(v):
    w = v * v
    total = jnp.full_like(v, -((2 * math.pi) ** 11) / math.factorial(11))
    for power in (9, 7, 5, 3, 1):
        sign = 1.0 if power % 4 == 1 else -1.0
        total = total * w + sign * (2 * math.pi) ** power / math.factorial(power)
    return total * v


def cos_sin_turns(t):
    t = t - jnp.floor(t + 0.5)
    size = jnp.abs(t)
    cosine = sine_turns(0.25 - size)
    sine = sine_turns(0.25 - jnp.abs(size - 0.25))
    return cosine, jnp.where(t < 0.0, -sine, sine)


def split(x):
    high = x.astype(BF16)
    low = (x - high.astype(F32)).astype(BF16)
    return high, low


def stacked(x):
    high, low = split(x)
    return jnp.concatenate([high, low, high], axis=0)


def abreast(x):
    high, low = split(x)
    return jnp.concatenate([high, low, high], axis=1)


def dot(a, b):
    return jnp.dot(a, b, preferred_element_type=F32)


def freq_y(i):
    return 8 * ((i >> 1) & 31) + 4 * (i >> 8) + ((i >> 6) & 3), i & 1


def freq_plain(i):
    return i & 255, i >> 8


def place_plain(i):
    return i & 127, i >> 7


def place_x(i):
    return 4 * (i & 31) + ((i >> 5) & 3), i >> 7


def fill_table(ref, shape, row_is_freq, freq, place, on_left):
    rows, cols = shape
    chunk = 32

    def step(j, carry):
        start = pl.multiple_of(j * chunk, chunk)
        row = lax.broadcasted_iota(jnp.int32, (chunk, cols), 0) + start
        col = lax.broadcasted_iota(jnp.int32, (chunk, cols), 1)
        if row_is_freq:
            k, kc = freq(row)
            n, nc = place(col)
        else:
            k, kc = freq(col)
            n, nc = place(row)
        turns = ((k * n + 64 * (kc - nc) + 128) & 255) - 128
        t = turns.astype(F32) * (1.0 / 256.0)
        high, low = split(sine_turns(0.25 - jnp.abs(t)) * (1.0 / 16.0))
        if on_left:
            ref[pl.ds(start, chunk), 0:cols] = high
            ref[pl.ds(start, chunk), cols : 2 * cols] = high
            ref[pl.ds(start, chunk), 2 * cols : 3 * cols] = low
        else:
            ref[pl.ds(start, chunk), :] = high
            ref[pl.ds(pl.multiple_of(rows + start, chunk), chunk), :] = high
            ref[pl.ds(pl.multiple_of(2 * rows + start, chunk), chunk), :] = low
        return carry

    lax.fori_loop(0, rows // chunk, step, 0)


def kernel(
    amp_ref, disp_ref, sup_hbm, miller_ref, shift_ref, int_hbm,
    amp_out, disp_out,
    sup, inten, own, mate, mill, ey_send, ey_recv, ex_recv, trig, obj, obj_all, bcat,
    fwd_send, fwd_recv, back_send, back_recv, ydone, ydone_all, part, part_own, part_recv, lapped,
    y_fwd, y_back, x_fwd, x_back, z_fwd, z_back,
    load_sem, mate_sem, mill_sem, edge_sem, peer_sem, peer_back_sem, slab_sem, slab_back_sem, part_sem,
):
    refl = lax.axis_index("refl")
    me = lax.axis_index("slab")
    zh = refl // 4
    yy = lax.rem(refl, 4)
    mate_id = lax.rem(refl + 4, 8)

    def peer_of(t):
        return zh * 4 + lax.rem(yy + t, 4)

    sup_copy = pltpu.make_async_copy(
        sup_hbm.at[:, pl.ds(pl.multiple_of(refl * 16, 16), 16), :], sup, load_sem.at[0]
    )
    sup_copy.start()
    int_copies = [
        pltpu.make_async_copy(int_hbm.at[:, pl.ds(128 * j, 128)], inten.at[j], load_sem.at[1 + j])
        for j in range(2)
    ]
    for copy in int_copies:
        copy.start()

    barrier = pltpu.get_barrier_semaphore()

    def greet_slab(j, carry):
        pl.semaphore_signal(
            barrier, inc=1, device_id={"slab": lax.rem(me + j, SLABS)}, device_id_type=MESH
        )
        return carry

    def greet_refl(j, carry):
        pl.semaphore_signal(
            barrier, inc=1, device_id={"refl": lax.rem(refl + j, 8)}, device_id_type=MESH
        )
        return carry

    lax.fori_loop(1, 8, greet_refl, 0)
    lax.fori_loop(1, SLABS, greet_slab, 0)

    own[1:4] = disp_ref[...]
    lane_row = lax.broadcasted_iota(jnp.int32, (8, 128), 0)
    tile = jnp.where(
        lane_row == 0,
        miller_ref[0, 0].astype(F32),
        jnp.where(
            lane_row == 1,
            miller_ref[0, 1].astype(F32),
            jnp.where(lane_row == 2, miller_ref[0, 2].astype(F32), shift_ref[0].astype(F32)),
        ),
    )
    mill[yy] = tile
    sup_copy.wait()
    mask = sup[...].astype(F32)
    own[0] = mask * amp_ref[...]
    for f in range(4):
        for x in range(ROWS):
            at = f * 4 + x
            ey_send[0, at : at + 1, :] = own[f, x, 0:1, :]
            ey_send[1, at : at + 1, :] = own[f, x, 15:16, :]

    pl.semaphore_wait(barrier, 38)

    def remote(src, dst, sems, axis, target):
        return pltpu.make_async_remote_copy(
            src_ref=src,
            dst_ref=dst,
            send_sem=sems.at[0],
            recv_sem=sems.at[1],
            device_id={axis: target},
            device_id_type=MESH,
        )

    def planes(p):
        return pl.ds(WIDTH * p, WIDTH)

    mate_copies = [
        remote(own.at[:, planes(p)], mate.at[:, planes(p)], mate_sem.at[p], "refl", mate_id)
        for p in range(2)
    ]
    mill_copies = [
        remote(mill.at[yy], mill.at[yy], mill_sem.at[t], "refl", peer_of(t)) for t in (1, 2, 3)
    ]
    for copy in mill_copies + mate_copies:
        copy.start()

    has = (refl > 0, refl < 7, me > 0, me < SLABS - 1)
    down_y = remote(ey_send.at[0], ey_recv.at[1], edge_sem.at[0], "refl", lax.rem(refl + 7, 8))
    up_y = remote(ey_send.at[1], ey_recv.at[0], edge_sem.at[1], "refl", lax.rem(refl + 1, 8))
    down_x = remote(own.at[:, 0], ex_recv.at[1], edge_sem.at[2], "slab", lax.rem(me + SLABS - 1, SLABS))
    up_x = remote(own.at[:, 3], ex_recv.at[0], edge_sem.at[3], "slab", lax.rem(me + 1, SLABS))
    edges = (down_y, up_y, down_x, up_x)
    for there, copy in zip(has, edges):
        pl.when(there)(copy.start)

    def nothing(ref, at):
        def fill():
            ref[at] = jnp.zeros(ref.shape[1:], F32)
        return fill

    for there, ref, at in zip(has, (ey_recv, ey_recv, ex_recv, ex_recv), (0, 1, 0, 1)):
        pl.when(jnp.logical_not(there))(nothing(ref, at))

    def place_y(i):
        side = ((i >> 5) & 1) + zh
        return ((side & 1) * 4 + (i >> 6)) * 16 + (i & 15), (i >> 4) & 1

    fill_table(y_fwd, (512, 256), True, freq_y, place_y, True)
    for copy in mill_copies:
        copy.wait_recv()
    lane = lax.broadcasted_iota(jnp.int32, (1, 1, 128), 2).astype(F32)

    def objects(t, p, b, ref):
        coef = mill[lax.rem(yy + t, 4)]
        m0, m1, m2, s = [coef[j : j + 1][None] for j in range(4)]
        turn = s * lane * (1.0 / 256.0)
        turn = turn - jnp.floor(turn)
        weight, d0, d1, d2 = [(own, mate)[b][f, planes(p)] for f in range(4)]
        phase = m0 * d0 + m1 * d1 + m2 * d2
        cosine, sine = cos_sin_turns(phase * (1.0 / (2 * math.pi)) + turn)
        trig[t, 0, b, planes(p)] = cosine
        trig[t, 1, b, planes(p)] = sine
        ref[0] = weight * cosine
        ref[1] = weight * sine

    obj_copies = {}
    for b in range(2):
        for p in range(2):
            if b == 1:
                mate_copies[p].wait_recv()
            for t in (2, 1, 3):
                objects(t, p, b, obj.at[t, p, b])
                copy = remote(
                    obj.at[t, p, b], obj_all.at[p, yy, b], peer_sem.at[p, b, t], "refl", peer_of(t)
                )
                copy.start()
                obj_copies[p, b, t] = copy
            objects(0, p, b, obj_all.at[p, yy, b])

    def slab_sends(src, dst, sems, at, g):
        def lines(i):
            return (*at, pl.ds(pl.multiple_of(i * 16, 16), 16))

        def send(j, carry):
            to = lax.rem(me + j, SLABS)
            pltpu.make_async_remote_copy(
                src_ref=src.at[lines(to)],
                dst_ref=dst.at[lines(me)],
                send_sem=sems.at[0, g],
                recv_sem=sems.at[1, g],
                device_id={"slab": to},
                device_id_type=MESH,
            ).start()
            return carry

        lax.fori_loop(16, SLABS, send, 0)
        lax.fori_loop(1, 16, send, 0)
        pltpu.make_async_copy(src.at[lines(me)], dst.at[lines(me)], sems.at[1, g]).start()

    def wait_sent(src, dst, sems, at, g):
        most = (*at, pl.ds(0, LINES - 16))
        pltpu.make_async_copy(src.at[most], dst.at[most], sems.at[0, g]).wait()

    def wait_arrived(dst, sems, at, g):
        pltpu.make_async_copy(dst.at[at], dst.at[at], sems.at[1, g]).wait()

    whole = slice(None)
    fwd_groups = ((0, 0), (0, 1), (1, whole))
    back_groups = ((0, whole), (1, 0), (1, 1))

    def why(h, p):
        out = dot(y_fwd[256 * h : 256 * (h + 1), :], bcat[p])
        for k in range(4):
            for j in range(WIDTH):
                fwd_send[h, p, pl.ds(4 * j + k, 64, stride=8), :] = out[
                    64 * k : 64 * (k + 1), 128 * j : 128 * (j + 1)
                ]

    for p in range(2):
        for b in range(2):
            for t in (1, 3, 2):
                obj_copies[p, b, t].wait_recv()
        columns = [obj_all[p, :, :, :, j].reshape(256, 128) for j in range(WIDTH)]
        bcat[p] = stacked(jnp.concatenate(columns, axis=1))
        why(0, p)
        slab_sends(fwd_send, fwd_recv, slab_sem, fwd_groups[p], p)
    for p in range(2):
        why(1, p)
    slab_sends(fwd_send, fwd_recv, slab_sem, fwd_groups[2], 2)

    fill_table(x_fwd, (512, 256), True, freq_plain, place_x, True)
    fill_table(z_fwd, (256, 512), False, freq_plain, place_plain, False)
    fill_table(x_back, (256, 512), False, freq_plain, place_x, True)
    fill_table(z_back, (512, 256), True, freq_plain, place_plain, False)
    fill_table(y_back, (256, 512), False, freq_y, place_y, True)
    for copy in int_copies:
        copy.wait()

    for h in range(2):
        for g in ((0, 1), (2,))[h]:
            wait_arrived(fwd_recv, slab_sem, fwd_groups[g], g)

        def row(k, carry):
            sides = [
                jnp.concatenate(
                    [
                        fwd_recv[h, x // 2, pl.ds(c * 8 + (x % 2) * 4 + k, 32, stride=16), :]
                        for x in range(ROWS)
                    ],
                    axis=0,
                )
                for c in range(2)
            ]
            zed = dot(abreast(jnp.concatenate(sides, axis=1)), z_fwd[...])
            spec = dot(
                x_fwd[...], stacked(jnp.concatenate([zed[:, :256], zed[:, 256:]], axis=0))
            )
            real, imag = spec[:256], spec[256:]
            measured = jnp.concatenate(
                [inten[j, pl.ds(4 * h + k, 256, stride=8), :] for j in range(2)], axis=1
            )
            excess = 4.0 * (real * real + imag * imag - measured)
            residual = jnp.concatenate([excess * real, excess * imag], axis=0)
            back = dot(x_back[...], stacked(residual))
            out = dot(abreast(jnp.concatenate([back[:128], back[128:]], axis=1)), z_back[...])
            for c in range(2):
                for x in range(ROWS):
                    back_send[h, x // 2, pl.ds(c * 8 + (x % 2) * 4 + k, 32, stride=16), :] = out[
                        32 * x : 32 * (x + 1), 128 * c : 128 * (c + 1)
                    ]
            return carry

        lax.fori_loop(0, 4, row, 0)
        for g in ((0,), (1, 2))[h]:
            slab_sends(back_send, back_recv, slab_back_sem, back_groups[g], g)

    for there, copy in ((has[0], up_y), (has[1], down_y), (has[2], up_x), (has[3], down_x)):
        pl.when(there)(copy.wait_recv)
    sub = lax.broadcasted_iota(jnp.int32, (ROWS, 16, 128), 1)
    last = lax.broadcasted_iota(jnp.int32, (ROWS, 16, 128), 2)
    for f in range(4):
        x = own[f]
        beside = jnp.concatenate([ex_recv[0, f][None], x[:3]], axis=0)
        beside = beside + jnp.concatenate([x[1:], ex_recv[1, f][None]], axis=0)
        low = ey_recv[0, 4 * f : 4 * f + 4, :][:, None, :]
        high = ey_recv[1, 4 * f : 4 * f + 4, :][:, None, :]
        beside = beside + jnp.where(sub == 0, low, pltpu.roll(x, 1, 1))
        beside = beside + jnp.where(sub == 15, high, pltpu.roll(x, 15, 1))
        beside = beside + jnp.where(last == 0, 0.0, pltpu.roll(x, 1, 2))
        beside = beside + jnp.where(last == 127, 0.0, pltpu.roll(x, 127, 2))
        lapped[f] = 2.0 * (EDGE_WEIGHT if f == 0 else STRAIN_WEIGHT) * (6.0 * x - beside)

    done_copies = {}
    for p in range(2):
        for g in ((0, 1), (2,))[p]:
            wait_arrived(back_recv, slab_back_sem, back_groups[g], g)
        columns = [
            jnp.concatenate(
                [
                    back_recv[h, p, pl.ds(4 * j + k, 64, stride=8), :]
                    for h in range(2)
                    for k in range(4)
                ],
                axis=0,
            )
            for j in range(WIDTH)
        ]
        out = dot(y_back[...], stacked(jnp.concatenate(columns, axis=1)))
        for j in range(WIDTH):
            ydone[p, :, :, :, j] = out[:, 128 * j : 128 * (j + 1)].reshape(4, 2, 2, 16, 128)
        for b in (1, 0):
            for t in (2, 1, 3):
                copy = remote(
                    ydone.at[p, lax.rem(yy + t, 4), b],
                    ydone_all.at[p, 4 - t, b],
                    peer_back_sem.at[p, b, t],
                    "refl",
                    peer_of(t),
                )
                copy.start()
                done_copies[p, b, t] = copy

    def summed(b, p):
        for t in (1, 3, 2):
            done_copies[p, b, t].wait_recv()
        totals = [jnp.zeros((WIDTH, 16, 128), F32) for _ in range(4)]
        for t in range(4):
            if t == 0:
                real, imag = ydone[p, yy, b, 0], ydone[p, yy, b, 1]
            else:
                real, imag = ydone_all[p, t, b, 0], ydone_all[p, t, b, 1]
            cosine, sine = trig[t, 0, b, planes(p)], trig[t, 1, b, planes(p)]
            coef = mill[lax.rem(yy + t, 4)]
            across = imag * cosine - real * sine
            totals[0] = totals[0] + real * cosine + imag * sine
            for c in range(3):
                totals[1 + c] = totals[1 + c] + coef[c : c + 1][None] * across
        return totals

    part_copies = []
    for p in range(2):
        for f, total in enumerate(summed(1, p)):
            part[p, f] = total
        copy = remote(part.at[p], part_recv.at[p], part_sem.at[p], "refl", mate_id)
        copy.start()
        part_copies.append(copy)
    for p in range(2):
        for f, total in enumerate(summed(0, p)):
            part_own[p, f] = total

    for p in range(2):
        part_copies[p].wait_recv()
        mask = sup[planes(p)].astype(F32)
        amp_out[planes(p)] = mask * (part_own[p, 0] + part_recv[p, 0] + lapped[0, planes(p)])
        for c in range(3):
            disp_out[c, planes(p)] = (
                own[0, planes(p)] * (part_own[p, 1 + c] + part_recv[p, 1 + c])
                + lapped[1 + c, planes(p)]
            )

    for copy in mill_copies + mate_copies + part_copies:
        copy.wait_send()
    for there, copy in zip(has, edges):
        pl.when(there)(copy.wait_send)
    for at in obj_copies:
        obj_copies[at].wait_send()
        done_copies[at].wait_send()
    for g in range(3):
        wait_sent(fwd_send, fwd_recv, slab_sem, fwd_groups[g], g)
        wait_sent(back_send, back_recv, slab_back_sem, back_groups[g], g)


def body(amplitude, displacement, support, miller, shift_kz, intensity):
    vmem = pl.BlockSpec(memory_space=pltpu.VMEM)
    smem = pl.BlockSpec(memory_space=pltpu.SMEM)
    anywhere = pl.BlockSpec(memory_space=pl.ANY)
    block = (ROWS, 16, 128)
    chunk = (WIDTH, 16, 128)
    sems = pltpu.SemaphoreType.DMA
    return pl.pallas_call(
        kernel,
        out_shape=(
            jax.ShapeDtypeStruct(block, F32),
            jax.ShapeDtypeStruct((3, *block), F32),
        ),
        in_specs=[vmem, vmem, anywhere, smem, smem, anywhere],
        out_specs=(vmem, vmem),
        scratch_shapes=[
            pltpu.VMEM(block, jnp.int32),
            pltpu.VMEM((2, 2048, 128), F32),
            pltpu.VMEM((4, *block), F32),
            pltpu.VMEM((4, *block), F32),
            pltpu.VMEM((4, 8, 128), F32),
            pltpu.VMEM((2, 16, 128), F32),
            pltpu.VMEM((2, 16, 128), F32),
            pltpu.VMEM((2, 4, 16, 128), F32),
            pltpu.VMEM((4, 2, 2, *block), F32),
            pltpu.VMEM((4, 2, 2, 2, *chunk), F32),
            pltpu.VMEM((2, 4, 2, 2, *chunk), F32),
            pltpu.VMEM((2, 768, 256), BF16),
            pltpu.VMEM((2, 2, LINES, 128), F32),
            pltpu.VMEM((2, 2, LINES, 128), F32),
            pltpu.VMEM((2, 2, LINES, 128), F32),
            pltpu.VMEM((2, 2, LINES, 128), F32),
            pltpu.VMEM((2, 4, 2, 2, *chunk), F32),
            pltpu.VMEM((2, 4, 2, 2, *chunk), F32),
            pltpu.VMEM((2, 4, *chunk), F32),
            pltpu.VMEM((2, 4, *chunk), F32),
            pltpu.VMEM((2, 4, *chunk), F32),
            pltpu.VMEM((4, *block), F32),
            pltpu.VMEM((512, 768), BF16),
            pltpu.VMEM((256, 1536), BF16),
            pltpu.VMEM((512, 768), BF16),
            pltpu.VMEM((256, 1536), BF16),
            pltpu.VMEM((768, 512), BF16),
            pltpu.VMEM((1536, 256), BF16),
            sems((3,)),
            sems((2, 2)),
            sems((4, 2)),
            sems((4, 2)),
            sems((2, 2, 4, 2)),
            sems((2, 2, 4, 2)),
            sems((2, 3)),
            sems((2, 3)),
            sems((2, 2)),
        ],
        compiler_params=pltpu.CompilerParams(
            collective_id=0, has_side_effects=True, vmem_limit_bytes=56 * 1024 * 1024
        ),
        name="gradient",
    )(amplitude, displacement, support, miller, shift_kz, intensity.reshape(2048, 256))


def solution(mesh):
    placed = (
        P("slab", "refl", None),
        P(None, "slab", "refl", None),
        P("slab", None, None),
        P("refl", None),
        P("refl"),
        P("refl", None, "slab", None),
    )
    return jax.shard_map(
        body,
        mesh=mesh,
        in_specs=placed,
        out_specs=(P("slab", "refl", None), P(None, "slab", "refl", None)),
        check_vma=False,
    )
```

```python
import math

import jax
import jax.numpy as jnp
from jax import lax
from jax.experimental import pallas as pl
from jax.experimental.pallas import tpu as pltpu
from jax.sharding import PartitionSpec as P

MESH = pl.DeviceIdType.MESH
F32 = jnp.float32
BF16 = jnp.bfloat16
STRAIN_WEIGHT = 0.05
EDGE_WEIGHT = 0.05
SLABS = 32
ROWS = 4
WIDTH = 2
TEAM = SLABS // 2
LINES = TEAM * 16
BLOCKS = ((0, 1), (1, 1), (1, 0))


def sine_turns(v):
    w = v * v
    total = jnp.full_like(v, -((2 * math.pi) ** 11) / math.factorial(11))
    for power in (9, 7, 5, 3, 1):
        sign = 1.0 if power % 4 == 1 else -1.0
        total = total * w + sign * (2 * math.pi) ** power / math.factorial(power)
    return total * v


def cos_sin_turns(t):
    t = t - jnp.floor(t + 0.5)
    size = jnp.abs(t)
    cosine = sine_turns(0.25 - size)
    sine = sine_turns(0.25 - jnp.abs(size - 0.25))
    return cosine, jnp.where(t < 0.0, -sine, sine)


def split(x):
    high = x.astype(BF16)
    low = (x - high.astype(F32)).astype(BF16)
    return high, low


def stacked(x):
    high, low = split(x)
    return jnp.concatenate([high, low, high], axis=0)


def abreast(x):
    high, low = split(x)
    return jnp.concatenate([high, low, high], axis=1)


def dot(a, b):
    return jnp.dot(a, b, preferred_element_type=F32)


def freq_plain(i):
    return i & 255, i >> 8


def place_plain(i):
    return i & 127, i >> 7


def fill_table(ref, shape, row_is_freq, freq, place, on_left):
    rows, cols = shape
    chunk = 32

    def step(j, carry):
        start = pl.multiple_of(j * chunk, chunk)
        row = lax.broadcasted_iota(jnp.int32, (chunk, cols), 0) + start
        col = lax.broadcasted_iota(jnp.int32, (chunk, cols), 1)
        if row_is_freq:
            k, kc = freq(row)
            n, nc = place(col)
        else:
            k, kc = freq(col)
            n, nc = place(row)
        turns = ((k * n + 64 * (kc - nc) + 128) & 255) - 128
        t = turns.astype(F32) * (1.0 / 256.0)
        high, low = split(sine_turns(0.25 - jnp.abs(t)) * (1.0 / 16.0))
        if on_left:
            ref[pl.ds(start, chunk), 0:cols] = high
            ref[pl.ds(start, chunk), cols : 2 * cols] = high
            ref[pl.ds(start, chunk), 2 * cols : 3 * cols] = low
        else:
            ref[pl.ds(start, chunk), :] = high
            ref[pl.ds(pl.multiple_of(rows + start, chunk), chunk), :] = high
            ref[pl.ds(pl.multiple_of(2 * rows + start, chunk), chunk), :] = low
        return carry

    lax.fori_loop(0, rows // chunk, step, 0)


def kernel(
    amp_ref, disp_ref, sup_hbm, miller_ref, shift_ref, int_hbm,
    amp_out, disp_out,
    sup, inten, raw, mill, ey_send, ey_recv, ex_recv, trig, obj, obj_all, bcat,
    fwd_send, fwd_recv, back_send, back_recv, ydone, ydone_all, part, part_recv, lapped,
    y_fwd, y_back, x_fwd, x_back, z_fwd, z_back,
    load_sem, raw_sem, mill_sem, edge_sem, peer_sem, peer_back_sem, slab_sem, slab_back_sem, part_sem,
):
    refl = lax.axis_index("refl")
    me = lax.axis_index("slab")
    zh = refl // 4
    yy = lax.rem(refl, 4)
    team = me // TEAM
    own = raw.at[0, 0]

    def peer_of(t):
        return {"refl": zh * 4 + lax.rem(yy + t, 4)}

    def across(b, q):
        return {"refl": lax.rem(refl + 4 * b, 8), "slab": lax.rem(me + TEAM * q, SLABS)}

    sup_copy = pltpu.make_async_copy(
        sup_hbm.at[:, pl.ds(pl.multiple_of(refl * 16, 16), 16), :], sup, load_sem.at[0]
    )
    sup_copy.start()
    int_copies = [
        pltpu.make_async_copy(int_hbm.at[:, pl.ds(128 * j, 128)], inten.at[j], load_sem.at[1 + j])
        for j in range(2)
    ]
    for copy in int_copies:
        copy.start()

    barrier = pltpu.get_barrier_semaphore()

    def greet_slab(j, carry):
        pl.semaphore_signal(
            barrier, inc=1, device_id={"slab": lax.rem(me + j, SLABS)}, device_id_type=MESH
        )
        return carry

    def greet_refl(j, carry):
        pl.semaphore_signal(
            barrier, inc=1, device_id={"refl": lax.rem(refl + j, 8)}, device_id_type=MESH
        )
        return carry

    lax.fori_loop(1, 8, greet_refl, 0)
    lax.fori_loop(1, SLABS, greet_slab, 0)
    pl.semaphore_signal(barrier, inc=1, device_id=across(1, 1), device_id_type=MESH)

    own[1:4] = disp_ref[...]
    lane_row = lax.broadcasted_iota(jnp.int32, (8, 128), 0)
    tile = jnp.where(
        lane_row == 0,
        miller_ref[0, 0].astype(F32),
        jnp.where(
            lane_row == 1,
            miller_ref[0, 1].astype(F32),
            jnp.where(lane_row == 2, miller_ref[0, 2].astype(F32), shift_ref[0].astype(F32)),
        ),
    )
    mill[yy] = tile
    sup_copy.wait()
    mask = sup[...].astype(F32)
    own[0] = mask * amp_ref[...]
    for f in range(4):
        for x in range(ROWS):
            at = f * 4 + x
            ey_send[0, at : at + 1, :] = own[f, x, 0:1, :]
            ey_send[1, at : at + 1, :] = own[f, x, 15:16, :]

    pl.semaphore_wait(barrier, 39)

    def remote(src, dst, sems, target):
        return pltpu.make_async_remote_copy(
            src_ref=src,
            dst_ref=dst,
            send_sem=sems.at[0],
            recv_sem=sems.at[1],
            device_id=target,
            device_id_type=MESH,
        )

    def planes(p):
        return pl.ds(WIDTH * p, WIDTH)

    raw_copies = {
        (b, q, p): remote(
            raw.at[0, 0, :, planes(p)], raw.at[b, q, :, planes(p)], raw_sem.at[b, q, p], across(b, q)
        )
        for p in range(2)
        for b, q in BLOCKS
    }
    mill_copies = [
        remote(mill.at[yy], mill.at[yy], mill_sem.at[t], peer_of(t)) for t in (1, 2, 3)
    ]
    for copy in mill_copies + list(raw_copies.values()):
        copy.start()

    has = (refl > 0, refl < 7, me > 0, me < SLABS - 1)
    down_y = remote(ey_send.at[0], ey_recv.at[1], edge_sem.at[0], {"refl": lax.rem(refl + 7, 8)})
    up_y = remote(ey_send.at[1], ey_recv.at[0], edge_sem.at[1], {"refl": lax.rem(refl + 1, 8)})
    down_x = remote(own.at[:, 0], ex_recv.at[1], edge_sem.at[2], {"slab": lax.rem(me + SLABS - 1, SLABS)})
    up_x = remote(own.at[:, 3], ex_recv.at[0], edge_sem.at[3], {"slab": lax.rem(me + 1, SLABS)})
    edges = (down_y, up_y, down_x, up_x)
    for there, copy in zip(has, edges):
        pl.when(there)(copy.start)

    def nothing(ref, at):
        def fill():
            ref[at] = jnp.zeros(ref.shape[1:], F32)
        return fill

    for there, ref, at in zip(has, (ey_recv, ey_recv, ex_recv, ex_recv), (0, 1, 0, 1)):
        pl.when(jnp.logical_not(there))(nothing(ref, at))

    def place_y(i):
        side = ((i >> 5) & 1) + zh
        return ((side & 1) * 4 + (i >> 6)) * 16 + (i & 15), (i >> 4) & 1

    def freq_y(i):
        return 8 * (TEAM * team + ((i >> 1) & 15)) + 4 * (i >> 7) + ((i >> 5) & 3), i & 1

    def place_x(i):
        side = ((i >> 6) & 1) + team
        return 64 * (side & 1) + 4 * (i & 15) + 2 * ((i >> 5) & 1) + ((i >> 4) & 1), i >> 7

    fill_table(y_fwd, (256, 256), True, freq_y, place_y, True)
    for copy in mill_copies:
        copy.wait_recv()
    lane = lax.broadcasted_iota(jnp.int32, (1, 1, 128), 2).astype(F32)

    def objects(t, p, b, q, ref):
        coef = mill[lax.rem(yy + t, 4)]
        m0, m1, m2, s = [coef[j : j + 1][None] for j in range(4)]
        turn = s * lane * (1.0 / 256.0)
        turn = turn - jnp.floor(turn)
        weight, d0, d1, d2 = [raw[b, q, f, planes(p)] for f in range(4)]
        phase = m0 * d0 + m1 * d1 + m2 * d2
        cosine, sine = cos_sin_turns(phase * (1.0 / (2 * math.pi)) + turn)
        trig[t, 0, b, q, planes(p)] = cosine
        trig[t, 1, b, q, planes(p)] = sine
        ref[0] = weight * cosine
        ref[1] = weight * sine

    obj_copies = {}

    def object_block(p, b, q):
        for t in (2, 1, 3):
            objects(t, p, b, q, obj.at[t, p, q, b])
            copy = remote(
                obj.at[t, p, q, b], obj_all.at[p, q, yy, b], peer_sem.at[p, q, b, t], peer_of(t)
            )
            copy.start()
            obj_copies[p, q, b, t] = copy
        objects(0, p, b, q, obj_all.at[p, q, yy, b])

    for p in range(2):
        object_block(p, 0, 0)
    for p in range(2):
        for b, q in BLOCKS:
            raw_copies[b, q, p].wait_recv()
            object_block(p, b, q)

    def slab_sends(src, dst, sems, h, p):
        def lines(i):
            return (h, p, slice(None), pl.ds(pl.multiple_of(lax.rem(i, TEAM) * 16, 16), 16))

        def send(j, carry):
            to = TEAM * team + lax.rem(me + j, TEAM)
            pltpu.make_async_remote_copy(
                src_ref=src.at[lines(to)],
                dst_ref=dst.at[lines(me)],
                send_sem=sems.at[0, h, p],
                recv_sem=sems.at[1, h, p],
                device_id={"slab": to},
                device_id_type=MESH,
            ).start()
            return carry

        lax.fori_loop(1, TEAM, send, 0)
        pltpu.make_async_copy(src.at[lines(me)], dst.at[lines(me)], sems.at[1, h, p]).start()

    def wait_sent(src, dst, sems, h, p):
        most = (h, p, slice(None), pl.ds(0, LINES - 16))
        pltpu.make_async_copy(src.at[most], dst.at[most], sems.at[0, h, p]).wait()

    def wait_arrived(dst, sems, h, p):
        pltpu.make_async_copy(dst.at[h, p], dst.at[h, p], sems.at[1, h, p]).wait()

    for p in range(2):
        for b, q in ((0, 0), *BLOCKS):
            for t in (1, 3, 2):
                obj_copies[p, q, b, t].wait_recv()
        for q in range(2):
            columns = [obj_all[p, q, :, :, :, j].reshape(256, 128) for j in range(WIDTH)]
            bcat[q] = stacked(jnp.concatenate(columns, axis=1))
        for h in range(2):
            for q in range(2):
                out = dot(y_fwd[128 * h : 128 * (h + 1), :], bcat[q])
                for k in range(4):
                    for j in range(WIDTH):
                        fwd_send[h, p, q, pl.ds(4 * j + k, 32, stride=8), :] = out[
                            32 * k : 32 * (k + 1), 128 * j : 128 * (j + 1)
                        ]
            slab_sends(fwd_send, fwd_recv, slab_sem, h, p)

    fill_table(x_fwd, (512, 256), True, freq_plain, place_x, True)
    fill_table(z_fwd, (256, 512), False, freq_plain, place_plain, False)
    fill_table(x_back, (256, 512), False, freq_plain, place_x, True)
    fill_table(z_back, (512, 256), True, freq_plain, place_plain, False)
    fill_table(y_back, (256, 256), False, freq_y, place_y, True)
    for copy in int_copies:
        copy.wait()

    for h in range(2):
        for p in range(2):
            wait_arrived(fwd_recv, slab_sem, h, p)

        def row(k, carry):
            sides = [
                jnp.concatenate(
                    [
                        fwd_recv[h, p, q, pl.ds(c * 8 + 4 * j + k, 16, stride=16), :]
                        for q in range(2)
                        for p in range(2)
                        for j in range(WIDTH)
                    ],
                    axis=0,
                )
                for c in range(2)
            ]
            zed = dot(abreast(jnp.concatenate(sides, axis=1)), z_fwd[...])
            spec = dot(
                x_fwd[...], stacked(jnp.concatenate([zed[:, :256], zed[:, 256:]], axis=0))
            )
            real, imag = spec[:256], spec[256:]
            measured = jnp.concatenate(
                [inten[j, pl.ds(4 * h + k, 256, stride=8), :] for j in range(2)], axis=1
            )
            excess = 4.0 * (real * real + imag * imag - measured)
            residual = jnp.concatenate([excess * real, excess * imag], axis=0)
            back = dot(x_back[...], stacked(residual))
            out = dot(abreast(jnp.concatenate([back[:128], back[128:]], axis=1)), z_back[...])
            for c in range(2):
                for at in range(8):
                    q, p, j = at // 4, at // 2 % 2, at % 2
                    back_send[h, p, q, pl.ds(c * 8 + 4 * j + k, 16, stride=16), :] = out[
                        16 * at : 16 * (at + 1), 128 * c : 128 * (c + 1)
                    ]
            return carry

        lax.fori_loop(0, 4, row, 0)
        for p in range(2):
            slab_sends(back_send, back_recv, slab_back_sem, h, p)

    for there, copy in ((has[0], up_y), (has[1], down_y), (has[2], up_x), (has[3], down_x)):
        pl.when(there)(copy.wait_recv)
    sub = lax.broadcasted_iota(jnp.int32, (ROWS, 16, 128), 1)
    last = lax.broadcasted_iota(jnp.int32, (ROWS, 16, 128), 2)
    for f in range(4):
        x = own[f]
        beside = jnp.concatenate([ex_recv[0, f][None], x[:3]], axis=0)
        beside = beside + jnp.concatenate([x[1:], ex_recv[1, f][None]], axis=0)
        low = ey_recv[0, 4 * f : 4 * f + 4, :][:, None, :]
        high = ey_recv[1, 4 * f : 4 * f + 4, :][:, None, :]
        beside = beside + jnp.where(sub == 0, low, pltpu.roll(x, 1, 1))
        beside = beside + jnp.where(sub == 15, high, pltpu.roll(x, 15, 1))
        beside = beside + jnp.where(last == 0, 0.0, pltpu.roll(x, 1, 2))
        beside = beside + jnp.where(last == 127, 0.0, pltpu.roll(x, 127, 2))
        lapped[f] = 2.0 * (EDGE_WEIGHT if f == 0 else STRAIN_WEIGHT) * (6.0 * x - beside)

    done_copies = {}
    for p in range(2):
        for h in range(2):
            wait_arrived(back_recv, slab_back_sem, h, p)
        for q in range(2):
            columns = [
                jnp.concatenate(
                    [
                        back_recv[h, p, q, pl.ds(4 * j + k, 32, stride=8), :]
                        for h in range(2)
                        for k in range(4)
                    ],
                    axis=0,
                )
                for j in range(WIDTH)
            ]
            out = dot(y_back[...], stacked(jnp.concatenate(columns, axis=1)))
            for j in range(WIDTH):
                ydone[p, q, :, :, :, j] = out[:, 128 * j : 128 * (j + 1)].reshape(4, 2, 2, 16, 128)
        for b, q in ((1, 0), (1, 1), (0, 1), (0, 0)):
            for t in (2, 1, 3):
                copy = remote(
                    ydone.at[p, q, lax.rem(yy + t, 4), b],
                    ydone_all.at[p, q, 4 - t, b],
                    peer_back_sem.at[p, q, b, t],
                    peer_of(t),
                )
                copy.start()
                done_copies[p, q, b, t] = copy

    def summed(b, q, p):
        for t in (1, 3, 2):
            done_copies[p, q, b, t].wait_recv()
        totals = [jnp.zeros((WIDTH, 16, 128), F32) for _ in range(4)]
        for t in range(4):
            if t == 0:
                real, imag = ydone[p, q, yy, b, 0], ydone[p, q, yy, b, 1]
            else:
                real, imag = ydone_all[p, q, t, b, 0], ydone_all[p, q, t, b, 1]
            cosine, sine = trig[t, 0, b, q, planes(p)], trig[t, 1, b, q, planes(p)]
            coef = mill[lax.rem(yy + t, 4)]
            across = imag * cosine - real * sine
            totals[0] = totals[0] + real * cosine + imag * sine
            for c in range(3):
                totals[1 + c] = totals[1 + c] + coef[c : c + 1][None] * across
        return totals

    part_copies = {}
    for p in range(2):
        for b, q in ((1, 0), (1, 1), (0, 1), (0, 0)):
            for f, total in enumerate(summed(b, q, p)):
                part[b, q, p, f] = total
            if (b, q) != (0, 0):
                copy = remote(
                    part.at[b, q, p], part_recv.at[b, q, p], part_sem.at[b, q, p], across(b, q)
                )
                copy.start()
                part_copies[b, q, p] = copy

    for p in range(2):
        sums = [part[0, 0, p, f] for f in range(4)]
        for b, q in BLOCKS:
            part_copies[b, q, p].wait_recv()
            sums = [sums[f] + part_recv[b, q, p, f] for f in range(4)]
        mask = sup[planes(p)].astype(F32)
        amp_out[planes(p)] = mask * (sums[0] + lapped[0, planes(p)])
        for c in range(3):
            disp_out[c, planes(p)] = (
                own[0, planes(p)] * sums[1 + c] + lapped[1 + c, planes(p)]
            )

    for copy in (*mill_copies, *raw_copies.values(), *part_copies.values()):
        copy.wait_send()
    for there, copy in zip(has, edges):
        pl.when(there)(copy.wait_send)
    for at in obj_copies:
        obj_copies[at].wait_send()
        done_copies[at].wait_send()
    for h in range(2):
        for p in range(2):
            wait_sent(fwd_send, fwd_recv, slab_sem, h, p)
            wait_sent(back_send, back_recv, slab_back_sem, h, p)


def body(amplitude, displacement, support, miller, shift_kz, intensity):
    vmem = pl.BlockSpec(memory_space=pltpu.VMEM)
    smem = pl.BlockSpec(memory_space=pltpu.SMEM)
    anywhere = pl.BlockSpec(memory_space=pl.ANY)
    block = (ROWS, 16, 128)
    chunk = (WIDTH, 16, 128)
    sems = pltpu.SemaphoreType.DMA
    return pl.pallas_call(
        kernel,
        out_shape=(
            jax.ShapeDtypeStruct(block, F32),
            jax.ShapeDtypeStruct((3, *block), F32),
        ),
        in_specs=[vmem, vmem, anywhere, smem, smem, anywhere],
        out_specs=(vmem, vmem),
        scratch_shapes=[
            pltpu.VMEM(block, jnp.int32),
            pltpu.VMEM((2, 2048, 128), F32),
            pltpu.VMEM((2, 2, 4, *block), F32),
            pltpu.VMEM((4, 8, 128), F32),
            pltpu.VMEM((2, 16, 128), F32),
            pltpu.VMEM((2, 16, 128), F32),
            pltpu.VMEM((2, 4, 16, 128), F32),
            pltpu.VMEM((4, 2, 2, 2, *block), F32),
            pltpu.VMEM((4, 2, 2, 2, 2, *chunk), F32),
            pltpu.VMEM((2, 2, 4, 2, 2, *chunk), F32),
            pltpu.VMEM((2, 768, 256), BF16),
            pltpu.VMEM((2, 2, 2, LINES, 128), F32),
            pltpu.VMEM((2, 2, 2, LINES, 128), F32),
            pltpu.VMEM((2, 2, 2, LINES, 128), F32),
            pltpu.VMEM((2, 2, 2, LINES, 128), F32),
            pltpu.VMEM((2, 2, 4, 2, 2, *chunk), F32),
            pltpu.VMEM((2, 2, 4, 2, 2, *chunk), F32),
            pltpu.VMEM((2, 2, 2, 4, *chunk), F32),
            pltpu.VMEM((2, 2, 2, 4, *chunk), F32),
            pltpu.VMEM((4, *block), F32),
            pltpu.VMEM((256, 768), BF16),
            pltpu.VMEM((256, 768), BF16),
            pltpu.VMEM((512, 768), BF16),
            pltpu.VMEM((256, 1536), BF16),
            pltpu.VMEM((768, 512), BF16),
            pltpu.VMEM((1536, 256), BF16),
            sems((3,)),
            sems((2, 2, 2, 2)),
            sems((4, 2)),
            sems((4, 2)),
            sems((2, 2, 2, 4, 2)),
            sems((2, 2, 2, 4, 2)),
            sems((2, 2, 2)),
            sems((2, 2, 2)),
            sems((2, 2, 2, 2)),
        ],
        compiler_params=pltpu.CompilerParams(
            collective_id=0, has_side_effects=True, vmem_limit_bytes=56 * 1024 * 1024
        ),
        name="gradient",
    )(amplitude, displacement, support, miller, shift_kz, intensity.reshape(2048, 256))


def solution(mesh):
    placed = (
        P("slab", "refl", None),
        P(None, "slab", "refl", None),
        P("slab", None, None),
        P("refl", None),
        P("refl"),
        P("refl", None, "slab", None),
    )
    return jax.shard_map(
        body,
        mesh=mesh,
        in_specs=placed,
        out_specs=(P("slab", "refl", None), P(None, "slab", "refl", None)),
        check_vma=False,
    )
```

```python
import math

import jax
import jax.numpy as jnp
from jax import lax
from jax.experimental import pallas as pl
from jax.experimental.pallas import tpu as pltpu
from jax.sharding import PartitionSpec as P

MESH = pl.DeviceIdType.MESH
F32 = jnp.float32
BF16 = jnp.bfloat16
STRAIN_WEIGHT = 0.05
EDGE_WEIGHT = 0.05
SLABS = 32
ROWS = 4
WIDTH = 2
TEAM = SLABS // 2
LINES = TEAM * 16
BLOCKS = ((0, 1), (1, 1), (1, 0))


def sine_turns(v):
    w = v * v
    total = jnp.full_like(v, -((2 * math.pi) ** 11) / math.factorial(11))
    for power in (9, 7, 5, 3, 1):
        sign = 1.0 if power % 4 == 1 else -1.0
        total = total * w + sign * (2 * math.pi) ** power / math.factorial(power)
    return total * v


def cos_sin_turns(t):
    t = t - jnp.floor(t + 0.5)
    size = jnp.abs(t)
    cosine = sine_turns(0.25 - size)
    sine = sine_turns(0.25 - jnp.abs(size - 0.25))
    return cosine, jnp.where(t < 0.0, -sine, sine)


def split(x):
    high = x.astype(BF16)
    low = (x - high.astype(F32)).astype(BF16)
    return high, low


def stacked(x):
    high, low = split(x)
    return jnp.concatenate([high, low, high], axis=0)


def abreast(x):
    high, low = split(x)
    return jnp.concatenate([high, low, high], axis=1)


def dot(a, b):
    return jnp.dot(a, b, preferred_element_type=F32)


def freq_plain(i):
    return i & 255, i >> 8


def place_plain(i):
    return i & 127, i >> 7


def fill_table(ref, shape, row_is_freq, freq, place, on_left):
    rows, cols = shape
    chunk = 32

    def step(j, carry):
        start = pl.multiple_of(j * chunk, chunk)
        row = lax.broadcasted_iota(jnp.int32, (chunk, cols), 0) + start
        col = lax.broadcasted_iota(jnp.int32, (chunk, cols), 1)
        if row_is_freq:
            k, kc = freq(row)
            n, nc = place(col)
        else:
            k, kc = freq(col)
            n, nc = place(row)
        turns = ((k * n + 64 * (kc - nc) + 128) & 255) - 128
        t = turns.astype(F32) * (1.0 / 256.0)
        high, low = split(sine_turns(0.25 - jnp.abs(t)) * (1.0 / 16.0))
        if on_left:
            ref[pl.ds(start, chunk), 0:cols] = high
            ref[pl.ds(start, chunk), cols : 2 * cols] = high
            ref[pl.ds(start, chunk), 2 * cols : 3 * cols] = low
        else:
            ref[pl.ds(start, chunk), :] = high
            ref[pl.ds(pl.multiple_of(rows + start, chunk), chunk), :] = high
            ref[pl.ds(pl.multiple_of(2 * rows + start, chunk), chunk), :] = low
        return carry

    lax.fori_loop(0, rows // chunk, step, 0)


def kernel(
    amp_ref, disp_ref, sup_hbm, miller_ref, shift_ref, int_hbm,
    amp_out, disp_out,
    sup, inten, raw, mill, ey_send, ey_recv, ex_recv, trig, obj, obj_all, bcat,
    fwd_send, fwd_recv, back_send, back_recv, ydone, ydone_all, part, part_own, part_recv, lapped,
    y_fwd, y_back, x_fwd, x_back, z_fwd, z_back,
    load_sem, raw_sem, mill_sem, edge_sem, peer_sem, peer_back_sem, slab_sem, slab_back_sem, part_sem,
):
    refl = lax.axis_index("refl")
    me = lax.axis_index("slab")
    zh = refl // 4
    yy = lax.rem(refl, 4)
    team = me // TEAM
    own = raw.at[0, 0]

    def peer_of(t):
        return {"refl": zh * 4 + lax.rem(yy + t, 4)}

    def across(b, q):
        return {"refl": lax.rem(refl + 4 * b, 8), "slab": lax.rem(me + TEAM * q, SLABS)}

    sup_copy = pltpu.make_async_copy(
        sup_hbm.at[:, pl.ds(pl.multiple_of(refl * 16, 16), 16), :], sup, load_sem.at[0]
    )
    sup_copy.start()
    int_copies = [
        pltpu.make_async_copy(int_hbm.at[:, pl.ds(128 * j, 128)], inten.at[j], load_sem.at[1 + j])
        for j in range(2)
    ]
    for copy in int_copies:
        copy.start()

    barrier = pltpu.get_barrier_semaphore()

    def greet_slab(j, carry):
        pl.semaphore_signal(
            barrier, inc=1, device_id={"slab": lax.rem(me + j, SLABS)}, device_id_type=MESH
        )
        return carry

    def greet_refl(j, carry):
        pl.semaphore_signal(
            barrier, inc=1, device_id={"refl": lax.rem(refl + j, 8)}, device_id_type=MESH
        )
        return carry

    lax.fori_loop(1, 8, greet_refl, 0)
    lax.fori_loop(1, SLABS, greet_slab, 0)
    pl.semaphore_signal(barrier, inc=1, device_id=across(1, 1), device_id_type=MESH)

    own[1:4] = disp_ref[...]
    lane_row = lax.broadcasted_iota(jnp.int32, (8, 128), 0)
    tile = jnp.where(
        lane_row == 0,
        miller_ref[0, 0].astype(F32),
        jnp.where(
            lane_row == 1,
            miller_ref[0, 1].astype(F32),
            jnp.where(lane_row == 2, miller_ref[0, 2].astype(F32), shift_ref[0].astype(F32)),
        ),
    )
    mill[yy] = tile
    sup_copy.wait()
    mask = sup[...].astype(F32)
    own[0] = mask * amp_ref[...]
    for f in range(4):
        for x in range(ROWS):
            at = f * 4 + x
            ey_send[0, at : at + 1, :] = own[f, x, 0:1, :]
            ey_send[1, at : at + 1, :] = own[f, x, 15:16, :]

    pl.semaphore_wait(barrier, 39)

    def remote(src, dst, sems, target):
        return pltpu.make_async_remote_copy(
            src_ref=src,
            dst_ref=dst,
            send_sem=sems.at[0],
            recv_sem=sems.at[1],
            device_id=target,
            device_id_type=MESH,
        )

    def planes(p):
        return pl.ds(WIDTH * p, WIDTH)

    raw_copies = {
        (b, q, p): remote(
            raw.at[0, 0, :, planes(p)], raw.at[b, q, :, planes(p)], raw_sem.at[b, q, p], across(b, q)
        )
        for p in range(2)
        for b, q in BLOCKS
    }
    mill_copies = [
        remote(mill.at[yy], mill.at[yy], mill_sem.at[t], peer_of(t)) for t in (1, 2, 3)
    ]
    for copy in mill_copies + list(raw_copies.values()):
        copy.start()

    has = (refl > 0, refl < 7, me > 0, me < SLABS - 1)
    down_y = remote(ey_send.at[0], ey_recv.at[1], edge_sem.at[0], {"refl": lax.rem(refl + 7, 8)})
    up_y = remote(ey_send.at[1], ey_recv.at[0], edge_sem.at[1], {"refl": lax.rem(refl + 1, 8)})
    down_x = remote(own.at[:, 0], ex_recv.at[1], edge_sem.at[2], {"slab": lax.rem(me + SLABS - 1, SLABS)})
    up_x = remote(own.at[:, 3], ex_recv.at[0], edge_sem.at[3], {"slab": lax.rem(me + 1, SLABS)})
    edges = (down_y, up_y, down_x, up_x)
    for there, copy in zip(has, edges):
        pl.when(there)(copy.start)

    def nothing(ref, at):
        def fill():
            ref[at] = jnp.zeros(ref.shape[1:], F32)
        return fill

    for there, ref, at in zip(has, (ey_recv, ey_recv, ex_recv, ex_recv), (0, 1, 0, 1)):
        pl.when(jnp.logical_not(there))(nothing(ref, at))

    def place_y(i):
        side = ((i >> 5) & 1) + zh
        return ((side & 1) * 4 + (i >> 6)) * 16 + (i & 15), (i >> 4) & 1

    def freq_y(i):
        return 8 * (TEAM * team + ((i >> 1) & 15)) + 4 * (i >> 7) + ((i >> 5) & 3), i & 1

    def freq_y_all(i):
        return 8 * ((i >> 1) & 31) + 4 * (i >> 8) + ((i >> 6) & 3), i & 1

    def place_x(i):
        side = ((i >> 6) & 1) + team
        return 64 * (side & 1) + 4 * (i & 15) + 2 * ((i >> 5) & 1) + ((i >> 4) & 1), i >> 7

    fill_table(y_fwd, (256, 256), True, freq_y, place_y, True)
    for copy in mill_copies:
        copy.wait_recv()
    lane = lax.broadcasted_iota(jnp.int32, (1, 1, 128), 2).astype(F32)

    def objects(t, p, b, q, ref):
        coef = mill[lax.rem(yy + t, 4)]
        m0, m1, m2, s = [coef[j : j + 1][None] for j in range(4)]
        turn = s * lane * (1.0 / 256.0)
        turn = turn - jnp.floor(turn)
        weight, d0, d1, d2 = [raw[b, q, f, planes(p)] for f in range(4)]
        phase = m0 * d0 + m1 * d1 + m2 * d2
        cosine, sine = cos_sin_turns(phase * (1.0 / (2 * math.pi)) + turn)
        if q == 0:
            trig[t, 0, b, planes(p)] = cosine
            trig[t, 1, b, planes(p)] = sine
        ref[0] = weight * cosine
        ref[1] = weight * sine

    obj_copies = {}

    def object_block(p, b, q):
        for t in (2, 1, 3):
            objects(t, p, b, q, obj.at[t, p, q, b])
            copy = remote(
                obj.at[t, p, q, b], obj_all.at[p, q, yy, b], peer_sem.at[p, q, b, t], peer_of(t)
            )
            copy.start()
            obj_copies[p, q, b, t] = copy
        objects(0, p, b, q, obj_all.at[p, q, yy, b])

    for p in range(2):
        object_block(p, 0, 0)
    for p in range(2):
        for b, q in BLOCKS:
            raw_copies[b, q, p].wait_recv()
            object_block(p, b, q)

    def team_sends(h, p):
        def lines(i):
            return (h, p, slice(None), pl.ds(pl.multiple_of(lax.rem(i, TEAM) * 16, 16), 16))

        def send(j, carry):
            to = TEAM * team + lax.rem(me + j, TEAM)
            pltpu.make_async_remote_copy(
                src_ref=fwd_send.at[lines(to)],
                dst_ref=fwd_recv.at[lines(me)],
                send_sem=slab_sem.at[0, h, p],
                recv_sem=slab_sem.at[1, h, p],
                device_id={"slab": to},
                device_id_type=MESH,
            ).start()
            return carry

        lax.fori_loop(1, TEAM, send, 0)
        pltpu.make_async_copy(
            fwd_send.at[lines(me)], fwd_recv.at[lines(me)], slab_sem.at[1, h, p]
        ).start()

    whole = slice(None)
    back_groups = ((0, whole), (1, 0), (1, 1))

    def slab_sends(g):
        def lines(i):
            return (*back_groups[g], pl.ds(pl.multiple_of(i * 16, 16), 16))

        def send(j, carry):
            to = lax.rem(me + j, SLABS)
            pltpu.make_async_remote_copy(
                src_ref=back_send.at[lines(to)],
                dst_ref=back_recv.at[lines(me)],
                send_sem=slab_back_sem.at[0, g],
                recv_sem=slab_back_sem.at[1, g],
                device_id={"slab": to},
                device_id_type=MESH,
            ).start()
            return carry

        lax.fori_loop(1, SLABS, send, 0)
        pltpu.make_async_copy(
            back_send.at[lines(me)], back_recv.at[lines(me)], slab_back_sem.at[1, g]
        ).start()

    def wait_all(ref, at, sem):
        pltpu.make_async_copy(ref.at[at], ref.at[at], sem).wait()

    for p in range(2):
        for b, q in ((0, 0), *BLOCKS):
            for t in (1, 3, 2):
                obj_copies[p, q, b, t].wait_recv()
        for q in range(2):
            columns = [obj_all[p, q, :, :, :, j].reshape(256, 128) for j in range(WIDTH)]
            bcat[q] = stacked(jnp.concatenate(columns, axis=1))
        for h in range(2):
            for q in range(2):
                out = dot(y_fwd[128 * h : 128 * (h + 1), :], bcat[q])
                for k in range(4):
                    for j in range(WIDTH):
                        fwd_send[h, p, q, pl.ds(4 * j + k, 32, stride=8), :] = out[
                            32 * k : 32 * (k + 1), 128 * j : 128 * (j + 1)
                        ]
            team_sends(h, p)

    fill_table(x_fwd, (512, 256), True, freq_plain, place_x, True)
    fill_table(z_fwd, (256, 512), False, freq_plain, place_plain, False)
    fill_table(x_back, (256, 512), False, freq_plain, place_x, True)
    fill_table(z_back, (512, 256), True, freq_plain, place_plain, False)
    fill_table(y_back, (256, 512), False, freq_y_all, place_y, True)
    for copy in int_copies:
        copy.wait()

    for h in range(2):
        for p in range(2):
            wait_all(fwd_recv, (h, p), slab_sem.at[1, h, p])

        def row(k, carry):
            sides = [
                jnp.concatenate(
                    [
                        fwd_recv[h, p, q, pl.ds(c * 8 + 4 * j + k, 16, stride=16), :]
                        for q in range(2)
                        for p in range(2)
                        for j in range(WIDTH)
                    ],
                    axis=0,
                )
                for c in range(2)
            ]
            zed = dot(abreast(jnp.concatenate(sides, axis=1)), z_fwd[...])
            spec = dot(
                x_fwd[...], stacked(jnp.concatenate([zed[:, :256], zed[:, 256:]], axis=0))
            )
            real, imag = spec[:256], spec[256:]
            measured = jnp.concatenate(
                [inten[j, pl.ds(4 * h + k, 256, stride=8), :] for j in range(2)], axis=1
            )
            excess = 4.0 * (real * real + imag * imag - measured)
            residual = jnp.concatenate([excess * real, excess * imag], axis=0)
            back = dot(x_back[...], stacked(residual))
            out = dot(abreast(jnp.concatenate([back[:128], back[128:]], axis=1)), z_back[...])
            for c in range(2):
                for at in range(8):
                    q, p, j = at // 4, at // 2 % 2, at % 2
                    first = LINES * lax.rem(q + team, 2) + c * 8 + 4 * j + k
                    back_send[h, p, pl.ds(first, 16, stride=16), :] = out[
                        16 * at : 16 * (at + 1), 128 * c : 128 * (c + 1)
                    ]
            return carry

        lax.fori_loop(0, 4, row, 0)
        for g in ((0,), (1, 2))[h]:
            slab_sends(g)

    for there, copy in ((has[0], up_y), (has[1], down_y), (has[2], up_x), (has[3], down_x)):
        pl.when(there)(copy.wait_recv)
    sub = lax.broadcasted_iota(jnp.int32, (ROWS, 16, 128), 1)
    last = lax.broadcasted_iota(jnp.int32, (ROWS, 16, 128), 2)
    for f in range(4):
        x = own[f]
        beside = jnp.concatenate([ex_recv[0, f][None], x[:3]], axis=0)
        beside = beside + jnp.concatenate([x[1:], ex_recv[1, f][None]], axis=0)
        low = ey_recv[0, 4 * f : 4 * f + 4, :][:, None, :]
        high = ey_recv[1, 4 * f : 4 * f + 4, :][:, None, :]
        beside = beside + jnp.where(sub == 0, low, pltpu.roll(x, 1, 1))
        beside = beside + jnp.where(sub == 15, high, pltpu.roll(x, 15, 1))
        beside = beside + jnp.where(last == 0, 0.0, pltpu.roll(x, 1, 2))
        beside = beside + jnp.where(last == 127, 0.0, pltpu.roll(x, 127, 2))
        lapped[f] = 2.0 * (EDGE_WEIGHT if f == 0 else STRAIN_WEIGHT) * (6.0 * x - beside)

    done_copies = {}
    for p in range(2):
        for g in ((0, 1), (2,))[p]:
            wait_all(back_recv, back_groups[g], slab_back_sem.at[1, g])
        columns = [
            jnp.concatenate(
                [
                    back_recv[h, p, pl.ds(4 * j + k, 64, stride=8), :]
                    for h in range(2)
                    for k in range(4)
                ],
                axis=0,
            )
            for j in range(WIDTH)
        ]
        out = dot(y_back[...], stacked(jnp.concatenate(columns, axis=1)))
        for j in range(WIDTH):
            ydone[p, :, :, :, j] = out[:, 128 * j : 128 * (j + 1)].reshape(4, 2, 2, 16, 128)
        for b in (1, 0):
            for t in (2, 1, 3):
                copy = remote(
                    ydone.at[p, lax.rem(yy + t, 4), b],
                    ydone_all.at[p, 4 - t, b],
                    peer_back_sem.at[p, b, t],
                    peer_of(t),
                )
                copy.start()
                done_copies[p, b, t] = copy

    def summed(b, p):
        for t in (1, 3, 2):
            done_copies[p, b, t].wait_recv()
        totals = [jnp.zeros((WIDTH, 16, 128), F32) for _ in range(4)]
        for t in range(4):
            if t == 0:
                real, imag = ydone[p, yy, b, 0], ydone[p, yy, b, 1]
            else:
                real, imag = ydone_all[p, t, b, 0], ydone_all[p, t, b, 1]
            cosine, sine = trig[t, 0, b, planes(p)], trig[t, 1, b, planes(p)]
            coef = mill[lax.rem(yy + t, 4)]
            across = imag * cosine - real * sine
            totals[0] = totals[0] + real * cosine + imag * sine
            for c in range(3):
                totals[1 + c] = totals[1 + c] + coef[c : c + 1][None] * across
        return totals

    part_copies = []
    for p in range(2):
        for f, total in enumerate(summed(1, p)):
            part[p, f] = total
        copy = remote(part.at[p], part_recv.at[p], part_sem.at[p], across(1, 0))
        copy.start()
        part_copies.append(copy)
    for p in range(2):
        for f, total in enumerate(summed(0, p)):
            part_own[p, f] = total

    for p in range(2):
        part_copies[p].wait_recv()
        mask = sup[planes(p)].astype(F32)
        amp_out[planes(p)] = mask * (part_own[p, 0] + part_recv[p, 0] + lapped[0, planes(p)])
        for c in range(3):
            disp_out[c, planes(p)] = (
                own[0, planes(p)] * (part_own[p, 1 + c] + part_recv[p, 1 + c])
                + lapped[1 + c, planes(p)]
            )

    for copy in (*mill_copies, *raw_copies.values(), *part_copies):
        copy.wait_send()
    for there, copy in zip(has, edges):
        pl.when(there)(copy.wait_send)
    for copy in (*obj_copies.values(), *done_copies.values()):
        copy.wait_send()
    for h in range(2):
        for p in range(2):
            wait_all(fwd_send, (h, p, whole, pl.ds(0, LINES - 16)), slab_sem.at[0, h, p])
    for g in range(3):
        wait_all(back_send, (*back_groups[g], pl.ds(0, 2 * LINES - 16)), slab_back_sem.at[0, g])


def body(amplitude, displacement, support, miller, shift_kz, intensity):
    vmem = pl.BlockSpec(memory_space=pltpu.VMEM)
    smem = pl.BlockSpec(memory_space=pltpu.SMEM)
    anywhere = pl.BlockSpec(memory_space=pl.ANY)
    block = (ROWS, 16, 128)
    chunk = (WIDTH, 16, 128)
    sems = pltpu.SemaphoreType.DMA
    return pl.pallas_call(
        kernel,
        out_shape=(
            jax.ShapeDtypeStruct(block, F32),
            jax.ShapeDtypeStruct((3, *block), F32),
        ),
        in_specs=[vmem, vmem, anywhere, smem, smem, anywhere],
        out_specs=(vmem, vmem),
        scratch_shapes=[
            pltpu.VMEM(block, jnp.int32),
            pltpu.VMEM((2, 2048, 128), F32),
            pltpu.VMEM((2, 2, 4, *block), F32),
            pltpu.VMEM((4, 8, 128), F32),
            pltpu.VMEM((2, 16, 128), F32),
            pltpu.VMEM((2, 16, 128), F32),
            pltpu.VMEM((2, 4, 16, 128), F32),
            pltpu.VMEM((4, 2, 2, *block), F32),
            pltpu.VMEM((4, 2, 2, 2, 2, *chunk), F32),
            pltpu.VMEM((2, 2, 4, 2, 2, *chunk), F32),
            pltpu.VMEM((2, 768, 256), BF16),
            pltpu.VMEM((2, 2, 2, LINES, 128), F32),
            pltpu.VMEM((2, 2, 2, LINES, 128), F32),
            pltpu.VMEM((2, 2, 2 * LINES, 128), F32),
            pltpu.VMEM((2, 2, 2 * LINES, 128), F32),
            pltpu.VMEM((2, 4, 2, 2, *chunk), F32),
            pltpu.VMEM((2, 4, 2, 2, *chunk), F32),
            pltpu.VMEM((2, 4, *chunk), F32),
            pltpu.VMEM((2, 4, *chunk), F32),
            pltpu.VMEM((2, 4, *chunk), F32),
            pltpu.VMEM((4, *block), F32),
            pltpu.VMEM((256, 768), BF16),
            pltpu.VMEM((256, 1536), BF16),
            pltpu.VMEM((512, 768), BF16),
            pltpu.VMEM((256, 1536), BF16),
            pltpu.VMEM((768, 512), BF16),
            pltpu.VMEM((1536, 256), BF16),
            sems((3,)),
            sems((2, 2, 2, 2)),
            sems((4, 2)),
            sems((4, 2)),
            sems((2, 2, 2, 4, 2)),
            sems((2, 2, 4, 2)),
            sems((2, 2, 2)),
            sems((2, 3)),
            sems((2, 2)),
        ],
        compiler_params=pltpu.CompilerParams(
            collective_id=0, has_side_effects=True, vmem_limit_bytes=56 * 1024 * 1024
        ),
        name="gradient",
    )(amplitude, displacement, support, miller, shift_kz, intensity.reshape(2048, 256))


def solution(mesh):
    placed = (
        P("slab", "refl", None),
        P(None, "slab", "refl", None),
        P("slab", None, None),
        P("refl", None),
        P("refl"),
        P("refl", None, "slab", None),
    )
    return jax.shard_map(
        body,
        mesh=mesh,
        in_specs=placed,
        out_specs=(P("slab", "refl", None), P(None, "slab", "refl", None)),
        check_vma=False,
    )
```

```python
import math

import jax
import jax.numpy as jnp
from jax import lax
from jax.experimental import pallas as pl
from jax.experimental.pallas import tpu as pltpu
from jax.sharding import PartitionSpec as P

MESH = pl.DeviceIdType.MESH
F32 = jnp.float32
BF16 = jnp.bfloat16
STRAIN_WEIGHT = 0.05
EDGE_WEIGHT = 0.05
SLABS = 32
ROWS = 4
WIDTH = 2
TEAM = SLABS // 2
LINES = TEAM * 16
UNROLL = 4
BLOCKS = ((0, 1), (1, 1), (1, 0))


def sine_turns(v):
    w = v * v
    total = jnp.full_like(v, -((2 * math.pi) ** 11) / math.factorial(11))
    for power in (9, 7, 5, 3, 1):
        sign = 1.0 if power % 4 == 1 else -1.0
        total = total * w + sign * (2 * math.pi) ** power / math.factorial(power)
    return total * v


def cos_sin_turns(t):
    t = t - jnp.floor(t + 0.5)
    size = jnp.abs(t)
    cosine = sine_turns(0.25 - size)
    sine = sine_turns(0.25 - jnp.abs(size - 0.25))
    return cosine, jnp.where(t < 0.0, -sine, sine)


def split(x):
    high = x.astype(BF16)
    low = (x - high.astype(F32)).astype(BF16)
    return high, low


def stacked(x):
    high, low = split(x)
    return jnp.concatenate([high, low, high], axis=0)


def abreast(x):
    high, low = split(x)
    return jnp.concatenate([high, low, high], axis=1)


def dot(a, b):
    return jnp.dot(a, b, preferred_element_type=F32)


def freq_plain(i):
    return i & 255, i >> 8


def place_plain(i):
    return i & 127, i >> 7


def fill_table(ref, shape, row_is_freq, freq, place, on_left):
    rows, cols = shape
    chunk = 32

    def step(j, carry):
        start = pl.multiple_of(j * chunk, chunk)
        row = lax.broadcasted_iota(jnp.int32, (chunk, cols), 0) + start
        col = lax.broadcasted_iota(jnp.int32, (chunk, cols), 1)
        if row_is_freq:
            k, kc = freq(row)
            n, nc = place(col)
        else:
            k, kc = freq(col)
            n, nc = place(row)
        turns = ((k * n + 64 * (kc - nc) + 128) & 255) - 128
        t = turns.astype(F32) * (1.0 / 256.0)
        high, low = split(sine_turns(0.25 - jnp.abs(t)) * (1.0 / 16.0))
        if on_left:
            ref[pl.ds(start, chunk), 0:cols] = high
            ref[pl.ds(start, chunk), cols : 2 * cols] = high
            ref[pl.ds(start, chunk), 2 * cols : 3 * cols] = low
        else:
            ref[pl.ds(start, chunk), :] = high
            ref[pl.ds(pl.multiple_of(rows + start, chunk), chunk), :] = high
            ref[pl.ds(pl.multiple_of(2 * rows + start, chunk), chunk), :] = low
        return carry

    lax.fori_loop(0, rows // chunk, step, 0)


def kernel(
    amp_ref, disp_ref, sup_hbm, miller_ref, shift_ref, int_hbm,
    amp_out, disp_out,
    sup, inten, raw, mill, ey_send, ey_recv, ex_recv, trig, obj, obj_all, bcat,
    fwd_send, fwd_recv, zed, zedb, back_send, back_recv, ydone, ydone_all, part, part_recv, lapped,
    y_fwd, y_back, x_fwd, x_back, z_fwd, z_back,
    load_sem, raw_sem, mill_sem, edge_sem, peer_sem, peer_back_sem, slab_sem, slab_back_sem, part_sem,
):
    refl = lax.axis_index("refl")
    me = lax.axis_index("slab")
    zh = refl // 4
    yy = lax.rem(refl, 4)
    team = me // TEAM
    own = raw.at[0, 0]

    def peer_of(t):
        return {"refl": zh * 4 + lax.rem(yy + t, 4)}

    def across(b, q):
        return {"refl": lax.rem(refl + 4 * b, 8), "slab": lax.rem(me + TEAM * q, SLABS)}

    sup_copy = pltpu.make_async_copy(
        sup_hbm.at[:, pl.ds(pl.multiple_of(refl * 16, 16), 16), :], sup, load_sem.at[0]
    )
    sup_copy.start()
    int_copies = [
        pltpu.make_async_copy(int_hbm.at[:, pl.ds(128 * j, 128)], inten.at[j], load_sem.at[1 + j])
        for j in range(2)
    ]
    for copy in int_copies:
        copy.start()

    barrier = pltpu.get_barrier_semaphore()

    def greet_slab(j, carry):
        pl.semaphore_signal(
            barrier, inc=1, device_id={"slab": lax.rem(me + j, SLABS)}, device_id_type=MESH
        )
        return carry

    def greet_refl(j, carry):
        pl.semaphore_signal(
            barrier, inc=1, device_id={"refl": lax.rem(refl + j, 8)}, device_id_type=MESH
        )
        return carry

    lax.fori_loop(1, 8, greet_refl, 0)
    lax.fori_loop(1, SLABS, greet_slab, 0)
    pl.semaphore_signal(barrier, inc=1, device_id=across(1, 1), device_id_type=MESH)

    own[1:4] = disp_ref[...]
    lane_row = lax.broadcasted_iota(jnp.int32, (8, 128), 0)
    tile = jnp.where(
        lane_row == 0,
        miller_ref[0, 0].astype(F32),
        jnp.where(
            lane_row == 1,
            miller_ref[0, 1].astype(F32),
            jnp.where(lane_row == 2, miller_ref[0, 2].astype(F32), shift_ref[0].astype(F32)),
        ),
    )
    mill[yy] = tile
    sup_copy.wait()
    mask = sup[...].astype(F32)
    own[0] = mask * amp_ref[...]
    for f in range(4):
        for x in range(ROWS):
            at = f * 4 + x
            ey_send[0, at : at + 1, :] = own[f, x, 0:1, :]
            ey_send[1, at : at + 1, :] = own[f, x, 15:16, :]

    pl.semaphore_wait(barrier, 39)

    def remote(src, dst, sems, target):
        return pltpu.make_async_remote_copy(
            src_ref=src,
            dst_ref=dst,
            send_sem=sems.at[0],
            recv_sem=sems.at[1],
            device_id=target,
            device_id_type=MESH,
        )

    def planes(p):
        return pl.ds(WIDTH * p, WIDTH)

    raw_copies = {
        (b, q, p): remote(
            raw.at[0, 0, :, planes(p)], raw.at[b, q, :, planes(p)], raw_sem.at[b, q, p], across(b, q)
        )
        for p in range(2)
        for b, q in BLOCKS
    }

    mill_copies = [
        remote(mill.at[yy], mill.at[yy], mill_sem.at[t], peer_of(t)) for t in (1, 2, 3)
    ]
    for copy in mill_copies + list(raw_copies.values()):
        copy.start()

    has = (refl > 0, refl < 7, me > 0, me < SLABS - 1)
    down_y = remote(ey_send.at[0], ey_recv.at[1], edge_sem.at[0], {"refl": lax.rem(refl + 7, 8)})
    up_y = remote(ey_send.at[1], ey_recv.at[0], edge_sem.at[1], {"refl": lax.rem(refl + 1, 8)})
    down_x = remote(own.at[:, 0], ex_recv.at[1], edge_sem.at[2], {"slab": lax.rem(me + SLABS - 1, SLABS)})
    up_x = remote(own.at[:, 3], ex_recv.at[0], edge_sem.at[3], {"slab": lax.rem(me + 1, SLABS)})
    edges = (down_y, up_y, down_x, up_x)
    for there, copy in zip(has, edges):
        pl.when(there)(copy.start)

    def nothing(ref, at):
        def fill():
            ref[at] = jnp.zeros(ref.shape[1:], F32)
        return fill

    for there, ref, at in zip(has, (ey_recv, ey_recv, ex_recv, ex_recv), (0, 1, 0, 1)):
        pl.when(jnp.logical_not(there))(nothing(ref, at))

    def place_y(i):
        side = ((i >> 5) & 1) + zh
        return ((side & 1) * 4 + (i >> 6)) * 16 + (i & 15), (i >> 4) & 1

    def freq_y(i):
        return 8 * (TEAM * team + ((i >> 1) & 15)) + 4 * (i >> 7) + ((i >> 5) & 3), i & 1

    def place_x(i):
        side = ((i >> 6) & 1) + team
        return 64 * (side & 1) + 4 * (i & 15) + 2 * ((i >> 5) & 1) + ((i >> 4) & 1), i >> 7

    fill_table(y_fwd, (256, 256), True, freq_y, place_y, True)
    for copy in mill_copies:
        copy.wait_recv()
    lane = lax.broadcasted_iota(jnp.int32, (1, 1, 128), 2).astype(F32)

    def objects(t, p, b, q, ref):
        coef = mill[lax.rem(yy + t, 4)]
        m0, m1, m2, s = [coef[j : j + 1][None] for j in range(4)]
        turn = s * lane * (1.0 / 256.0)
        turn = turn - jnp.floor(turn)
        weight, d0, d1, d2 = [raw[b, q, f, planes(p)] for f in range(4)]
        phase = m0 * d0 + m1 * d1 + m2 * d2
        cosine, sine = cos_sin_turns(phase * (1.0 / (2 * math.pi)) + turn)
        trig[t, 0, b, q, planes(p)] = cosine
        trig[t, 1, b, q, planes(p)] = sine
        ref[0] = weight * cosine
        ref[1] = weight * sine

    obj_copies = {}

    def object_block(p, b, q):
        for t in (2, 1, 3):
            objects(t, p, b, q, obj.at[t, p, q, b])
            copy = remote(
                obj.at[t, p, q, b], obj_all.at[p, q, yy, b], peer_sem.at[p, q, b, t], peer_of(t)
            )
            copy.start()
            obj_copies[p, q, b, t] = copy
        objects(0, p, b, q, obj_all.at[p, q, yy, b])

    for p in range(2):
        object_block(p, 0, 0)
    for p in range(2):
        for b, q in BLOCKS:
            raw_copies[b, q, p].wait_recv()
            object_block(p, b, q)

    def slab_sends(src, dst, sems, h, p):
        def lines(i):
            return (h, p, slice(None), pl.ds(pl.multiple_of(lax.rem(i, TEAM) * 16, 16), 16))

        def send(j, carry):
            to = TEAM * team + lax.rem(me + j, TEAM)
            pltpu.make_async_remote_copy(
                src_ref=src.at[lines(to)],
                dst_ref=dst.at[lines(me)],
                send_sem=sems.at[0, h, p],
                recv_sem=sems.at[1, h, p],
                device_id={"slab": to},
                device_id_type=MESH,
            ).start()
            return carry

        lax.fori_loop(1, TEAM, send, 0)
        pltpu.make_async_copy(src.at[lines(me)], dst.at[lines(me)], sems.at[1, h, p]).start()

    def wait_sent(src, dst, sems, h, p):
        most = (h, p, slice(None), pl.ds(0, LINES - 16))
        pltpu.make_async_copy(src.at[most], dst.at[most], sems.at[0, h, p]).wait()

    def wait_arrived(dst, sems, h, p):
        pltpu.make_async_copy(dst.at[h, p], dst.at[h, p], sems.at[1, h, p]).wait()

    for p in range(2):
        for b, q in ((0, 0), *BLOCKS):
            for t in (1, 3, 2):
                obj_copies[p, q, b, t].wait_recv()
        for q in range(2):
            columns = [obj_all[p, q, :, :, :, j].reshape(256, 128) for j in range(WIDTH)]
            bcat[q] = stacked(jnp.concatenate(columns, axis=1))
        for h in range(2):
            for q in range(2):
                out = dot(y_fwd[128 * h : 128 * (h + 1), :], bcat[q])
                for k in range(4):
                    for j in range(WIDTH):
                        fwd_send[h, p, q, pl.ds(4 * j + k, 32, stride=8), :] = out[
                            32 * k : 32 * (k + 1), 128 * j : 128 * (j + 1)
                        ]
            slab_sends(fwd_send, fwd_recv, slab_sem, h, p)

    fill_table(x_fwd, (512, 256), True, freq_plain, place_x, True)
    fill_table(z_fwd, (256, 512), False, freq_plain, place_plain, False)
    fill_table(x_back, (256, 512), False, freq_plain, place_x, True)
    fill_table(z_back, (512, 256), True, freq_plain, place_plain, False)
    fill_table(y_back, (256, 256), False, freq_y, place_y, True)
    for copy in int_copies:
        copy.wait()

    for h in range(2):
        for p in range(2):
            wait_arrived(fwd_recv, slab_sem, h, p)

        sides = [
            jnp.concatenate(
                [
                    fwd_recv[h, p, q, pl.ds(c * 8 + 4 * j + k, 16, stride=16), :]
                    for k in range(4)
                    for q in range(2)
                    for p in range(2)
                    for j in range(WIDTH)
                ],
                axis=0,
            )
            for c in range(2)
        ]
        zed[...] = dot(abreast(jnp.concatenate(sides, axis=1)), z_fwd[...])

        def row(k, carry):
            lines = pl.ds(pl.multiple_of(128 * k, 128), 128)
            spec = dot(
                x_fwd[...], stacked(jnp.concatenate([zed[lines, :256], zed[lines, 256:]], axis=0))
            )
            real, imag = spec[:256], spec[256:]
            measured = jnp.concatenate(
                [inten[j, pl.ds(4 * h + k, 256, stride=8), :] for j in range(2)], axis=1
            )
            excess = 4.0 * (real * real + imag * imag - measured)
            residual = jnp.concatenate([excess * real, excess * imag], axis=0)
            back = dot(x_back[...], stacked(residual))
            for c in range(2):
                high, low = split(back[128 * c : 128 * (c + 1)])
                zedb[lines, 256 * c : 256 * (c + 1)] = high
                zedb[lines, 512 + 256 * c : 512 + 256 * (c + 1)] = low
                zedb[lines, 1024 + 256 * c : 1024 + 256 * (c + 1)] = high
            return carry

        lax.fori_loop(0, 4, row, 0, unroll=UNROLL)
        out = dot(zedb[...], z_back[...])
        for k in range(4):
            for c in range(2):
                for at in range(8):
                    q, p, j = at // 4, at // 2 % 2, at % 2
                    first = 128 * k + 16 * at
                    back_send[h, p, q, pl.ds(c * 8 + 4 * j + k, 16, stride=16), :] = out[
                        first : first + 16, 128 * c : 128 * (c + 1)
                    ]
        for p in range(2):
            slab_sends(back_send, back_recv, slab_back_sem, h, p)

    for there, copy in ((has[0], up_y), (has[1], down_y), (has[2], up_x), (has[3], down_x)):
        pl.when(there)(copy.wait_recv)
    sub = lax.broadcasted_iota(jnp.int32, (ROWS, 16, 128), 1)
    last = lax.broadcasted_iota(jnp.int32, (ROWS, 16, 128), 2)
    for f in range(4):
        x = own[f]
        beside = jnp.concatenate([ex_recv[0, f][None], x[:3]], axis=0)
        beside = beside + jnp.concatenate([x[1:], ex_recv[1, f][None]], axis=0)
        low = ey_recv[0, 4 * f : 4 * f + 4, :][:, None, :]
        high = ey_recv[1, 4 * f : 4 * f + 4, :][:, None, :]
        beside = beside + jnp.where(sub == 0, low, pltpu.roll(x, 1, 1))
        beside = beside + jnp.where(sub == 15, high, pltpu.roll(x, 15, 1))
        beside = beside + jnp.where(last == 0, 0.0, pltpu.roll(x, 1, 2))
        beside = beside + jnp.where(last == 127, 0.0, pltpu.roll(x, 127, 2))
        lapped[f] = 2.0 * (EDGE_WEIGHT if f == 0 else STRAIN_WEIGHT) * (6.0 * x - beside)

    done_copies = {}

    def done_send(p, q, b):
        for t in (2, 1, 3):
            copy = remote(
                ydone.at[p, q, lax.rem(yy + t, 4), b],
                ydone_all.at[p, q, 4 - t, b],
                peer_back_sem.at[p, q, b, t],
                peer_of(t),
            )
            copy.start()
            done_copies[p, q, b, t] = copy

    for p in range(2):
        for h in range(2):
            wait_arrived(back_recv, slab_back_sem, h, p)
        for q in range(2):
            columns = [
                jnp.concatenate(
                    [
                        back_recv[h, p, q, pl.ds(4 * j + k, 32, stride=8), :]
                        for h in range(2)
                        for k in range(4)
                    ],
                    axis=0,
                )
                for j in range(WIDTH)
            ]
            out = dot(y_back[...], stacked(jnp.concatenate(columns, axis=1)))
            for j in range(WIDTH):
                ydone[p, q, :, :, :, j] = out[:, 128 * j : 128 * (j + 1)].reshape(4, 2, 2, 16, 128)
        for b, q in ((1, 0), (1, 1), (0, 1)):
            done_send(p, q, b)
    for p in range(2):
        done_send(p, 0, 0)

    def summed(b, q, p):
        for t in (1, 3, 2):
            done_copies[p, q, b, t].wait_recv()
        totals = [jnp.zeros((WIDTH, 16, 128), F32) for _ in range(4)]
        for t in range(4):
            if t == 0:
                real, imag = ydone[p, q, yy, b, 0], ydone[p, q, yy, b, 1]
            else:
                real, imag = ydone_all[p, q, t, b, 0], ydone_all[p, q, t, b, 1]
            cosine, sine = trig[t, 0, b, q, planes(p)], trig[t, 1, b, q, planes(p)]
            coef = mill[lax.rem(yy + t, 4)]
            across = imag * cosine - real * sine
            totals[0] = totals[0] + real * cosine + imag * sine
            for c in range(3):
                totals[1 + c] = totals[1 + c] + coef[c : c + 1][None] * across
        return totals

    part_copies = {}
    for p in range(2):
        for b, q in ((1, 0), (1, 1), (0, 1)):
            for f, total in enumerate(summed(b, q, p)):
                part[b, q, p, f] = total
            copy = remote(
                part.at[b, q, p], part_recv.at[b, q, p], part_sem.at[b, q, p], across(b, q)
            )
            copy.start()
            part_copies[b, q, p] = copy

    for p in range(2):
        sums = summed(0, 0, p)
        for b, q in BLOCKS:
            part_copies[b, q, p].wait_recv()
            sums = [sums[f] + part_recv[b, q, p, f] for f in range(4)]
        mask = sup[planes(p)].astype(F32)
        amp_out[planes(p)] = mask * (sums[0] + lapped[0, planes(p)])
        for c in range(3):
            disp_out[c, planes(p)] = (
                own[0, planes(p)] * sums[1 + c] + lapped[1 + c, planes(p)]
            )

    for copy in (*mill_copies, *raw_copies.values(), *part_copies.values()):
        copy.wait_send()
    for there, copy in zip(has, edges):
        pl.when(there)(copy.wait_send)
    for at in obj_copies:
        obj_copies[at].wait_send()
        done_copies[at].wait_send()
    for h in range(2):
        for p in range(2):
            wait_sent(fwd_send, fwd_recv, slab_sem, h, p)
            wait_sent(back_send, back_recv, slab_back_sem, h, p)


def body(amplitude, displacement, support, miller, shift_kz, intensity):
    vmem = pl.BlockSpec(memory_space=pltpu.VMEM)
    smem = pl.BlockSpec(memory_space=pltpu.SMEM)
    anywhere = pl.BlockSpec(memory_space=pl.ANY)
    block = (ROWS, 16, 128)
    chunk = (WIDTH, 16, 128)
    sems = pltpu.SemaphoreType.DMA
    return pl.pallas_call(
        kernel,
        out_shape=(
            jax.ShapeDtypeStruct(block, F32),
            jax.ShapeDtypeStruct((3, *block), F32),
        ),
        in_specs=[vmem, vmem, anywhere, smem, smem, anywhere],
        out_specs=(vmem, vmem),
        scratch_shapes=[
            pltpu.VMEM(block, jnp.int32),
            pltpu.VMEM((2, 2048, 128), F32),
            pltpu.VMEM((2, 2, 4, *block), F32),
            pltpu.VMEM((4, 8, 128), F32),
            pltpu.VMEM((2, 16, 128), F32),
            pltpu.VMEM((2, 16, 128), F32),
            pltpu.VMEM((2, 4, 16, 128), F32),
            pltpu.VMEM((4, 2, 2, 2, *block), F32),
            pltpu.VMEM((4, 2, 2, 2, 2, *chunk), F32),
            pltpu.VMEM((2, 2, 4, 2, 2, *chunk), F32),
            pltpu.VMEM((2, 768, 256), BF16),
            pltpu.VMEM((2, 2, 2, LINES, 128), F32),
            pltpu.VMEM((2, 2, 2, LINES, 128), F32),
            pltpu.VMEM((512, 512), F32),
            pltpu.VMEM((512, 1536), BF16),
            pltpu.VMEM((2, 2, 2, LINES, 128), F32),
            pltpu.VMEM((2, 2, 2, LINES, 128), F32),
            pltpu.VMEM((2, 2, 4, 2, 2, *chunk), F32),
            pltpu.VMEM((2, 2, 4, 2, 2, *chunk), F32),
            pltpu.VMEM((2, 2, 2, 4, *chunk), F32),
            pltpu.VMEM((2, 2, 2, 4, *chunk), F32),
            pltpu.VMEM((4, *block), F32),
            pltpu.VMEM((256, 768), BF16),
            pltpu.VMEM((256, 768), BF16),
            pltpu.VMEM((512, 768), BF16),
            pltpu.VMEM((256, 1536), BF16),
            pltpu.VMEM((768, 512), BF16),
            pltpu.VMEM((1536, 256), BF16),
            sems((3,)),
            sems((2, 2, 2, 2)),
            sems((4, 2)),
            sems((4, 2)),
            sems((2, 2, 2, 4, 2)),
            sems((2, 2, 2, 4, 2)),
            sems((2, 2, 2)),
            sems((2, 2, 2)),
            sems((2, 2, 2, 2)),
        ],
        compiler_params=pltpu.CompilerParams(
            collective_id=0, has_side_effects=True, vmem_limit_bytes=56 * 1024 * 1024
        ),
        name="gradient",
    )(amplitude, displacement, support, miller, shift_kz, intensity.reshape(2048, 256))


def solution(mesh):
    placed = (
        P("slab", "refl", None),
        P(None, "slab", "refl", None),
        P("slab", None, None),
        P("refl", None),
        P("refl"),
        P("refl", None, "slab", None),
    )
    return jax.shard_map(
        body,
        mesh=mesh,
        in_specs=placed,
        out_specs=(P("slab", "refl", None), P(None, "slab", "refl", None)),
        check_vma=False,
    )
```

```python
import math

import jax
import jax.numpy as jnp
from jax import lax
from jax.experimental import pallas as pl
from jax.experimental.pallas import tpu as pltpu
from jax.sharding import PartitionSpec as P

MESH = pl.DeviceIdType.MESH
F32 = jnp.float32
BF16 = jnp.bfloat16
STRAIN_WEIGHT = 0.05
EDGE_WEIGHT = 0.05
SLABS = 32
ROWS = 4
WIDTH = 2
TEAM = SLABS // 2
GROUPS = 4
LINES = TEAM * 8
BLOCKS = ((0, 1), (1, 1), (1, 0))


def sine_turns(v):
    w = v * v
    total = jnp.full_like(v, -((2 * math.pi) ** 11) / math.factorial(11))
    for power in (9, 7, 5, 3, 1):
        sign = 1.0 if power % 4 == 1 else -1.0
        total = total * w + sign * (2 * math.pi) ** power / math.factorial(power)
    return total * v


def cos_sin_turns(t):
    t = t - jnp.floor(t + 0.5)
    size = jnp.abs(t)
    cosine = sine_turns(0.25 - size)
    sine = sine_turns(0.25 - jnp.abs(size - 0.25))
    return cosine, jnp.where(t < 0.0, -sine, sine)


def split(x):
    high = x.astype(BF16)
    low = (x - high.astype(F32)).astype(BF16)
    return high, low


def stacked(x):
    high, low = split(x)
    return jnp.concatenate([high, low, high], axis=0)


def abreast(x):
    high, low = split(x)
    return jnp.concatenate([high, low, high], axis=1)


def dot(a, b):
    return jnp.dot(a, b, preferred_element_type=F32)


def freq_plain(i):
    return i & 255, i >> 8


def place_plain(i):
    return i & 127, i >> 7


def fill_table(ref, shape, row_is_freq, freq, place, on_left):
    rows, cols = shape
    chunk = 32

    def step(j, carry):
        start = pl.multiple_of(j * chunk, chunk)
        row = lax.broadcasted_iota(jnp.int32, (chunk, cols), 0) + start
        col = lax.broadcasted_iota(jnp.int32, (chunk, cols), 1)
        if row_is_freq:
            k, kc = freq(row)
            n, nc = place(col)
        else:
            k, kc = freq(col)
            n, nc = place(row)
        turns = ((k * n + 64 * (kc - nc) + 128) & 255) - 128
        t = turns.astype(F32) * (1.0 / 256.0)
        high, low = split(sine_turns(0.25 - jnp.abs(t)) * (1.0 / 16.0))
        if on_left:
            ref[pl.ds(start, chunk), 0:cols] = high
            ref[pl.ds(start, chunk), cols : 2 * cols] = high
            ref[pl.ds(start, chunk), 2 * cols : 3 * cols] = low
        else:
            ref[pl.ds(start, chunk), :] = high
            ref[pl.ds(pl.multiple_of(rows + start, chunk), chunk), :] = high
            ref[pl.ds(pl.multiple_of(2 * rows + start, chunk), chunk), :] = low
        return carry

    lax.fori_loop(0, rows // chunk, step, 0)


def kernel(
    amp_hbm, disp_hbm, sup_hbm, miller_hbm, shift_hbm, int_hbm,
    amp_out, disp_out,
    amp, miller_ref, shift_ref, sup, inten, raw, mill, ey_send, ey_recv, ex_recv, trig, obj, obj_all, bcat,
    fwd_send, fwd_recv, zed, zedb, back_send, back_recv, ydone, ydone_all, part, part_recv, lapped,
    y_fwd, y_back, x_fwd, x_back, z_fwd, z_back,
    load_sem, raw_sem, mill_sem, edge_sem, peer_sem, peer_back_sem, slab_sem, slab_back_sem, part_sem,
):
    refl = lax.axis_index("refl")
    me = lax.axis_index("slab")
    zh = refl // 4
    yy = lax.rem(refl, 4)
    team = me // TEAM
    own = raw.at[0, 0]

    def peer_of(t):
        return {"refl": zh * 4 + lax.rem(yy + t, 4)}

    def across(b, q):
        return {"refl": lax.rem(refl + 4 * b, 8), "slab": lax.rem(me + TEAM * q, SLABS)}

    sup_copy = pltpu.make_async_copy(
        sup_hbm.at[:, pl.ds(pl.multiple_of(refl * 16, 16), 16), :], sup, load_sem.at[0]
    )
    first_copies = [
        pltpu.make_async_copy(miller_hbm, miller_ref, load_sem.at[3]),
        pltpu.make_async_copy(shift_hbm, shift_ref, load_sem.at[4]),
        sup_copy,
        pltpu.make_async_copy(amp_hbm, amp, load_sem.at[5]),
        pltpu.make_async_copy(disp_hbm, own.at[pl.ds(1, 3)], load_sem.at[6]),
    ]
    for copy in first_copies:
        copy.start()
    int_copies = [
        pltpu.make_async_copy(int_hbm.at[:, pl.ds(128 * j, 128)], inten.at[j], load_sem.at[1 + j])
        for j in range(2)
    ]

    barrier = pltpu.get_barrier_semaphore()

    def greet_slab(j, carry):
        pl.semaphore_signal(
            barrier, inc=1, device_id={"slab": lax.rem(me + j, SLABS)}, device_id_type=MESH
        )
        return carry

    def greet_refl(j, carry):
        pl.semaphore_signal(
            barrier, inc=1, device_id={"refl": lax.rem(refl + j, 8)}, device_id_type=MESH
        )
        return carry

    lax.fori_loop(1, 8, greet_refl, 0)
    lax.fori_loop(1, SLABS, greet_slab, 0)
    pl.semaphore_signal(barrier, inc=1, device_id=across(1, 1), device_id_type=MESH)

    for copy in first_copies:
        copy.wait()
    for copy in int_copies:
        copy.start()
    lane_row = lax.broadcasted_iota(jnp.int32, (8, 128), 0)
    tile = jnp.where(
        lane_row == 0,
        miller_ref[0, 0].astype(F32),
        jnp.where(
            lane_row == 1,
            miller_ref[0, 1].astype(F32),
            jnp.where(lane_row == 2, miller_ref[0, 2].astype(F32), shift_ref[0].astype(F32)),
        ),
    )
    mill[yy] = tile
    mask = sup[...].astype(F32)
    own[0] = mask * amp[...]
    for f in range(4):
        for x in range(ROWS):
            at = f * 4 + x
            ey_send[0, at : at + 1, :] = own[f, x, 0:1, :]
            ey_send[1, at : at + 1, :] = own[f, x, 15:16, :]

    pl.semaphore_wait(barrier, 39)

    def remote(src, dst, sems, target):
        return pltpu.make_async_remote_copy(
            src_ref=src,
            dst_ref=dst,
            send_sem=sems.at[0],
            recv_sem=sems.at[1],
            device_id=target,
            device_id_type=MESH,
        )

    def planes(p):
        return pl.ds(WIDTH * p, WIDTH)

    raw_copies = {
        (b, q, p): remote(
            raw.at[0, 0, :, planes(p)], raw.at[b, q, :, planes(p)], raw_sem.at[b, q, p], across(b, q)
        )
        for p in range(2)
        for b, q in BLOCKS
    }

    mill_copies = [
        remote(mill.at[yy], mill.at[yy], mill_sem.at[t], peer_of(t)) for t in (1, 2, 3)
    ]
    for copy in mill_copies + list(raw_copies.values()):
        copy.start()

    has = (refl > 0, refl < 7, me > 0, me < SLABS - 1)
    down_y = remote(ey_send.at[0], ey_recv.at[1], edge_sem.at[0], {"refl": lax.rem(refl + 7, 8)})
    up_y = remote(ey_send.at[1], ey_recv.at[0], edge_sem.at[1], {"refl": lax.rem(refl + 1, 8)})
    down_x = remote(own.at[:, 0], ex_recv.at[1], edge_sem.at[2], {"slab": lax.rem(me + SLABS - 1, SLABS)})
    up_x = remote(own.at[:, 3], ex_recv.at[0], edge_sem.at[3], {"slab": lax.rem(me + 1, SLABS)})
    edges = (down_y, up_y, down_x, up_x)
    for there, copy in zip(has, edges):
        pl.when(there)(copy.start)

    def nothing(ref, at):
        def fill():
            ref[at] = jnp.zeros(ref.shape[1:], F32)
        return fill

    for there, ref, at in zip(has, (ey_recv, ey_recv, ex_recv, ex_recv), (0, 1, 0, 1)):
        pl.when(jnp.logical_not(there))(nothing(ref, at))

    def place_y(i):
        side = ((i >> 5) & 1) + zh
        return ((side & 1) * 4 + (i >> 6)) * 16 + (i & 15), (i >> 4) & 1

    def freq_y(i):
        return 8 * (TEAM * team + ((i >> 1) & 15)) + 4 * (i >> 7) + ((i >> 5) & 3), i & 1

    def place_x(i):
        side = ((i >> 6) & 1) + team
        return 64 * (side & 1) + 4 * (i & 15) + 2 * ((i >> 5) & 1) + ((i >> 4) & 1), i >> 7

    fill_table(y_fwd, (256, 256), True, freq_y, place_y, True)
    for copy in mill_copies:
        copy.wait_recv()
    lane = lax.broadcasted_iota(jnp.int32, (1, 1, 128), 2).astype(F32)

    def objects(t, p, b, q, ref):
        coef = mill[lax.rem(yy + t, 4)]
        m0, m1, m2, s = [coef[j : j + 1][None] for j in range(4)]
        turn = s * lane * (1.0 / 256.0)
        turn = turn - jnp.floor(turn)
        weight, d0, d1, d2 = [raw[b, q, f, planes(p)] for f in range(4)]
        phase = m0 * d0 + m1 * d1 + m2 * d2
        cosine, sine = cos_sin_turns(phase * (1.0 / (2 * math.pi)) + turn)
        trig[t, 0, b, q, planes(p)] = cosine
        trig[t, 1, b, q, planes(p)] = sine
        ref[0] = weight * cosine
        ref[1] = weight * sine

    obj_copies = {}

    def object_block(p, b, q):
        for t in (2, 1, 3):
            objects(t, p, b, q, obj.at[t, p, q, b])
            copy = remote(
                obj.at[t, p, q, b], obj_all.at[p, q, yy, b], peer_sem.at[p, q, b, t], peer_of(t)
            )
            copy.start()
            obj_copies[p, q, b, t] = copy
        objects(0, p, b, q, obj_all.at[p, q, yy, b])

    for p in range(2):
        object_block(p, 0, 0)
    for p in range(2):
        for b, q in BLOCKS:
            raw_copies[b, q, p].wait_recv()
            object_block(p, b, q)

    whole = slice(None)
    fwd_groups = ((whole, 0), (0, 1), (1, 1), (2, 1), (3, 1))
    back_groups = ((0, whole), (1, whole), (2, whole), (3, 0), (3, 1))

    def slab_sends(src, dst, sems, at, g):
        def lines(i):
            return (*at, whole, pl.ds(pl.multiple_of(lax.rem(i, TEAM) * 8, 8), 8))

        def send(j, carry):
            to = TEAM * team + lax.rem(me + j, TEAM)
            pltpu.make_async_remote_copy(
                src_ref=src.at[lines(to)],
                dst_ref=dst.at[lines(me)],
                send_sem=sems.at[0, g],
                recv_sem=sems.at[1, g],
                device_id={"slab": to},
                device_id_type=MESH,
            ).start()
            return carry

        lax.fori_loop(1, TEAM, send, 0)
        pltpu.make_async_copy(src.at[lines(me)], dst.at[lines(me)], sems.at[1, g]).start()

    def wait_sent(src, dst, sems, at, g):
        most = (*at, whole, pl.ds(0, LINES - 8))
        pltpu.make_async_copy(src.at[most], dst.at[most], sems.at[0, g]).wait()

    def wait_arrived(dst, sems, at, g):
        pltpu.make_async_copy(dst.at[at], dst.at[at], sems.at[1, g]).wait()

    for p in range(2):
        for b, q in ((0, 0), *BLOCKS):
            for t in (1, 3, 2):
                obj_copies[p, q, b, t].wait_recv()
        for q in range(2):
            columns = [obj_all[p, q, :, :, :, j].reshape(256, 128) for j in range(WIDTH)]
            bcat[q] = stacked(jnp.concatenate(columns, axis=1))
        for h in range(2):
            for q in range(2):
                out = dot(y_fwd[128 * h : 128 * (h + 1), :], bcat[q])
                for k in range(4):
                    for j in range(WIDTH):
                        fwd_send[2 * h + k // 2, p, q, pl.ds(2 * j + k % 2, 32, stride=4), :] = out[
                            32 * k : 32 * (k + 1), 128 * j : 128 * (j + 1)
                        ]
            if p == 1:
                for g in (2 * h + 1, 2 * h + 2):
                    slab_sends(fwd_send, fwd_recv, slab_sem, fwd_groups[g], g)
        if p == 0:
            slab_sends(fwd_send, fwd_recv, slab_sem, fwd_groups[0], 0)

    fill_table(x_fwd, (512, 256), True, freq_plain, place_x, True)
    fill_table(z_fwd, (256, 512), False, freq_plain, place_plain, False)
    fill_table(x_back, (256, 512), False, freq_plain, place_x, True)
    fill_table(z_back, (512, 256), True, freq_plain, place_plain, False)
    fill_table(y_back, (256, 256), False, freq_y, place_y, True)
    for copy in int_copies:
        copy.wait()

    wait_arrived(fwd_recv, slab_sem, fwd_groups[0], 0)
    for h in range(GROUPS):
        wait_arrived(fwd_recv, slab_sem, fwd_groups[1 + h], 1 + h)
        sides = [
            jnp.concatenate(
                [
                    fwd_recv[h, p, q, pl.ds(c * 4 + 2 * j + k, 16, stride=8), :]
                    for k in range(2)
                    for q in range(2)
                    for p in range(2)
                    for j in range(WIDTH)
                ],
                axis=0,
            )
            for c in range(2)
        ]
        zed[h % 2] = dot(abreast(jnp.concatenate(sides, axis=1)), z_fwd[...])
        for k in range(2):
            lines = slice(128 * k, 128 * (k + 1))
            spec = dot(
                x_fwd[...],
                stacked(
                    jnp.concatenate([zed[h % 2, lines, :256], zed[h % 2, lines, 256:]], axis=0)
                ),
            )
            real, imag = spec[:256], spec[256:]
            measured = jnp.concatenate(
                [inten[j, pl.ds(2 * h + k, 256, stride=8), :] for j in range(2)], axis=1
            )
            excess = 4.0 * (real * real + imag * imag - measured)
            residual = jnp.concatenate([excess * real, excess * imag], axis=0)
            back = dot(x_back[...], stacked(residual))
            for c in range(2):
                high, low = split(back[128 * c : 128 * (c + 1)])
                zedb[h % 2, lines, 256 * c : 256 * (c + 1)] = high
                zedb[h % 2, lines, 512 + 256 * c : 512 + 256 * (c + 1)] = low
                zedb[h % 2, lines, 1024 + 256 * c : 1024 + 256 * (c + 1)] = high
        out = dot(zedb[h % 2], z_back[...])
        for k in range(2):
            for c in range(2):
                for at in range(8):
                    q, p, j = at // 4, at // 2 % 2, at % 2
                    first = 128 * k + 16 * at
                    back_send[h, p, q, pl.ds(c * 4 + 2 * j + k, 16, stride=8), :] = out[
                        first : first + 16, 128 * c : 128 * (c + 1)
                    ]
        for g in (h,) if h < GROUPS - 1 else (h, h + 1):
            slab_sends(back_send, back_recv, slab_back_sem, back_groups[g], g)

    for there, copy in ((has[0], up_y), (has[1], down_y), (has[2], up_x), (has[3], down_x)):
        pl.when(there)(copy.wait_recv)
    sub = lax.broadcasted_iota(jnp.int32, (ROWS, 16, 128), 1)
    last = lax.broadcasted_iota(jnp.int32, (ROWS, 16, 128), 2)
    for f in range(4):
        x = own[f]
        beside = jnp.concatenate([ex_recv[0, f][None], x[:3]], axis=0)
        beside = beside + jnp.concatenate([x[1:], ex_recv[1, f][None]], axis=0)
        low = ey_recv[0, 4 * f : 4 * f + 4, :][:, None, :]
        high = ey_recv[1, 4 * f : 4 * f + 4, :][:, None, :]
        beside = beside + jnp.where(sub == 0, low, pltpu.roll(x, 1, 1))
        beside = beside + jnp.where(sub == 15, high, pltpu.roll(x, 15, 1))
        beside = beside + jnp.where(last == 0, 0.0, pltpu.roll(x, 1, 2))
        beside = beside + jnp.where(last == 127, 0.0, pltpu.roll(x, 127, 2))
        lapped[f] = 2.0 * (EDGE_WEIGHT if f == 0 else STRAIN_WEIGHT) * (6.0 * x - beside)

    done_copies = {}

    def done_send(p, q, b):
        for t in (2, 1, 3):
            copy = remote(
                ydone.at[p, q, lax.rem(yy + t, 4), b],
                ydone_all.at[p, q, 4 - t, b],
                peer_back_sem.at[p, q, b, t],
                peer_of(t),
            )
            copy.start()
            done_copies[p, q, b, t] = copy

    for p in range(2):
        for g in ((0, 1, 2, 3), (4,))[p]:
            wait_arrived(back_recv, slab_back_sem, back_groups[g], g)
        for q in range(2):
            columns = [
                jnp.concatenate(
                    [
                        back_recv[h, p, q, pl.ds(2 * j + k, 32, stride=4), :]
                        for h in range(GROUPS)
                        for k in range(2)
                    ],
                    axis=0,
                )
                for j in range(WIDTH)
            ]
            out = dot(y_back[...], stacked(jnp.concatenate(columns, axis=1)))
            for j in range(WIDTH):
                ydone[p, q, :, :, :, j] = out[:, 128 * j : 128 * (j + 1)].reshape(4, 2, 2, 16, 128)
        for b, q in ((1, 0), (1, 1), (0, 1)):
            done_send(p, q, b)
    for p in range(2):
        done_send(p, 0, 0)

    def summed(b, q, p):
        for t in (1, 3, 2):
            done_copies[p, q, b, t].wait_recv()
        totals = [jnp.zeros((WIDTH, 16, 128), F32) for _ in range(4)]
        for t in range(4):
            if t == 0:
                real, imag = ydone[p, q, yy, b, 0], ydone[p, q, yy, b, 1]
            else:
                real, imag = ydone_all[p, q, t, b, 0], ydone_all[p, q, t, b, 1]
            cosine, sine = trig[t, 0, b, q, planes(p)], trig[t, 1, b, q, planes(p)]
            coef = mill[lax.rem(yy + t, 4)]
            across = imag * cosine - real * sine
            totals[0] = totals[0] + real * cosine + imag * sine
            for c in range(3):
                totals[1 + c] = totals[1 + c] + coef[c : c + 1][None] * across
        return totals

    part_copies = {}
    for p in range(2):
        for b, q in ((1, 0), (1, 1), (0, 1)):
            for f, total in enumerate(summed(b, q, p)):
                part[b, q, p, f] = total
            copy = remote(
                part.at[b, q, p], part_recv.at[b, q, p], part_sem.at[b, q, p], across(b, q)
            )
            copy.start()
            part_copies[b, q, p] = copy

    for p in range(2):
        sums = summed(0, 0, p)
        for b, q in BLOCKS:
            part_copies[b, q, p].wait_recv()
            sums = [sums[f] + part_recv[b, q, p, f] for f in range(4)]
        mask = sup[planes(p)].astype(F32)
        amp_out[planes(p)] = mask * (sums[0] + lapped[0, planes(p)])
        for c in range(3):
            disp_out[c, planes(p)] = (
                own[0, planes(p)] * sums[1 + c] + lapped[1 + c, planes(p)]
            )

    for copy in (*mill_copies, *raw_copies.values(), *part_copies.values()):
        copy.wait_send()
    for there, copy in zip(has, edges):
        pl.when(there)(copy.wait_send)
    for at in obj_copies:
        obj_copies[at].wait_send()
        done_copies[at].wait_send()
    for g in range(GROUPS + 1):
        wait_sent(fwd_send, fwd_recv, slab_sem, fwd_groups[g], g)
        wait_sent(back_send, back_recv, slab_back_sem, back_groups[g], g)


def body(amplitude, displacement, support, miller, shift_kz, intensity):
    vmem = pl.BlockSpec(memory_space=pltpu.VMEM)
    anywhere = pl.BlockSpec(memory_space=pl.ANY)
    block = (ROWS, 16, 128)
    chunk = (WIDTH, 16, 128)
    sems = pltpu.SemaphoreType.DMA
    return pl.pallas_call(
        kernel,
        out_shape=(
            jax.ShapeDtypeStruct(block, F32),
            jax.ShapeDtypeStruct((3, *block), F32),
        ),
        in_specs=[anywhere] * 6,
        out_specs=(vmem, vmem),
        scratch_shapes=[
            pltpu.VMEM(block, F32),
            pltpu.SMEM((1, 3), jnp.int32),
            pltpu.SMEM((1,), jnp.int32),
            pltpu.VMEM(block, jnp.int32),
            pltpu.VMEM((2, 2048, 128), F32),
            pltpu.VMEM((2, 2, 4, *block), F32),
            pltpu.VMEM((4, 8, 128), F32),
            pltpu.VMEM((2, 16, 128), F32),
            pltpu.VMEM((2, 16, 128), F32),
            pltpu.VMEM((2, 4, 16, 128), F32),
            pltpu.VMEM((4, 2, 2, 2, *block), F32),
            pltpu.VMEM((4, 2, 2, 2, 2, *chunk), F32),
            pltpu.VMEM((2, 2, 4, 2, 2, *chunk), F32),
            pltpu.VMEM((2, 768, 256), BF16),
            pltpu.VMEM((GROUPS, 2, 2, LINES, 128), F32),
            pltpu.VMEM((GROUPS, 2, 2, LINES, 128), F32),
            pltpu.VMEM((2, 256, 512), F32),
            pltpu.VMEM((2, 256, 1536), BF16),
            pltpu.VMEM((GROUPS, 2, 2, LINES, 128), F32),
            pltpu.VMEM((GROUPS, 2, 2, LINES, 128), F32),
            pltpu.VMEM((2, 2, 4, 2, 2, *chunk), F32),
            pltpu.VMEM((2, 2, 4, 2, 2, *chunk), F32),
            pltpu.VMEM((2, 2, 2, 4, *chunk), F32),
            pltpu.VMEM((2, 2, 2, 4, *chunk), F32),
            pltpu.VMEM((4, *block), F32),
            pltpu.VMEM((256, 768), BF16),
            pltpu.VMEM((256, 768), BF16),
            pltpu.VMEM((512, 768), BF16),
            pltpu.VMEM((256, 1536), BF16),
            pltpu.VMEM((768, 512), BF16),
            pltpu.VMEM((1536, 256), BF16),
            sems((7,)),
            sems((2, 2, 2, 2)),
            sems((4, 2)),
            sems((4, 2)),
            sems((2, 2, 2, 4, 2)),
            sems((2, 2, 2, 4, 2)),
            sems((2, GROUPS + 1)),
            sems((2, GROUPS + 1)),
            sems((2, 2, 2, 2)),
        ],
        compiler_params=pltpu.CompilerParams(
            collective_id=0, has_side_effects=True, vmem_limit_bytes=56 * 1024 * 1024
        ),
        name="gradient",
    )(amplitude, displacement, support, miller, shift_kz, intensity.reshape(2048, 256))


def solution(mesh):
    placed = (
        P("slab", "refl", None),
        P(None, "slab", "refl", None),
        P("slab", None, None),
        P("refl", None),
        P("refl"),
        P("refl", None, "slab", None),
    )
    return jax.shard_map(
        body,
        mesh=mesh,
        in_specs=placed,
        out_specs=(P("slab", "refl", None), P(None, "slab", "refl", None)),
        check_vma=False,
    )
```

```python
import math

import jax
import jax.numpy as jnp
from jax import lax
from jax.experimental import pallas as pl
from jax.experimental.pallas import tpu as pltpu
from jax.sharding import PartitionSpec as P

MESH = pl.DeviceIdType.MESH
F32 = jnp.float32
BF16 = jnp.bfloat16
STRAIN_WEIGHT = 0.05
EDGE_WEIGHT = 0.05
SLABS = 32
ROWS = 4
WIDTH = 2
TEAM = SLABS // 2
GROUPS = 4
LINES = TEAM * 8
BLOCKS = ((0, 1), (1, 1), (1, 0))


def sine_turns(v):
    w = v * v
    total = jnp.full_like(v, -((2 * math.pi) ** 11) / math.factorial(11))
    for power in (9, 7, 5, 3, 1):
        sign = 1.0 if power % 4 == 1 else -1.0
        total = total * w + sign * (2 * math.pi) ** power / math.factorial(power)
    return total * v


def cos_sin_turns(t):
    t = t - jnp.floor(t + 0.5)
    size = jnp.abs(t)
    cosine = sine_turns(0.25 - size)
    sine = sine_turns(0.25 - jnp.abs(size - 0.25))
    return cosine, jnp.where(t < 0.0, -sine, sine)


def split(x):
    high = x.astype(BF16)
    low = (x - high.astype(F32)).astype(BF16)
    return high, low


def stacked(x):
    high, low = split(x)
    return jnp.concatenate([high, low, high], axis=0)


def abreast(x):
    high, low = split(x)
    return jnp.concatenate([high, low, high], axis=1)


def dot(a, b):
    return jnp.dot(a, b, preferred_element_type=F32)


def freq_plain(i):
    return i & 255, i >> 8


def place_plain(i):
    return i & 127, i >> 7


def fill_table(ref, shape, row_is_freq, freq, place, on_left):
    rows, cols = shape
    chunk = 32

    def step(j, carry):
        start = pl.multiple_of(j * chunk, chunk)
        row = lax.broadcasted_iota(jnp.int32, (chunk, cols), 0) + start
        col = lax.broadcasted_iota(jnp.int32, (chunk, cols), 1)
        if row_is_freq:
            k, kc = freq(row)
            n, nc = place(col)
        else:
            k, kc = freq(col)
            n, nc = place(row)
        turns = ((k * n + 64 * (kc - nc) + 128) & 255) - 128
        t = turns.astype(F32) * (1.0 / 256.0)
        high, low = split(sine_turns(0.25 - jnp.abs(t)) * (1.0 / 16.0))
        if on_left:
            ref[pl.ds(start, chunk), 0:cols] = high
            ref[pl.ds(start, chunk), cols : 2 * cols] = high
            ref[pl.ds(start, chunk), 2 * cols : 3 * cols] = low
        else:
            ref[pl.ds(start, chunk), :] = high
            ref[pl.ds(pl.multiple_of(rows + start, chunk), chunk), :] = high
            ref[pl.ds(pl.multiple_of(2 * rows + start, chunk), chunk), :] = low
        return carry

    lax.fori_loop(0, rows // chunk, step, 0)


def kernel(
    amp_hbm, disp_hbm, sup_hbm, miller_hbm, shift_hbm, int_hbm,
    amp_out, disp_out,
    amp, miller_ref, shift_ref, sup, inten, raw, mill, ey_send, ey_recv, ex_recv, trig, obj, obj_all, bcat,
    fwd_send, fwd_recv, zed, zedb, back_send, back_recv, owner_send, owner_recv, ydone, ydone_all, part, part_recv, lapped,
    y_fwd, y_back, y_back_all, x_fwd, x_back, z_fwd, z_back,
    load_sem, raw_sem, mill_sem, edge_sem, peer_sem, peer_back_sem, slab_sem, slab_back_sem, owner_sem, part_sem,
):
    refl = lax.axis_index("refl")
    me = lax.axis_index("slab")
    zh = refl // 4
    yy = lax.rem(refl, 4)
    team = me // TEAM
    own = raw.at[0, 0]

    def peer_of(t):
        return {"refl": zh * 4 + lax.rem(yy + t, 4)}

    def across(b, q):
        return {"refl": lax.rem(refl + 4 * b, 8), "slab": lax.rem(me + TEAM * q, SLABS)}

    sup_copy = pltpu.make_async_copy(
        sup_hbm.at[:, pl.ds(pl.multiple_of(refl * 16, 16), 16), :], sup, load_sem.at[0]
    )
    first_copies = [
        pltpu.make_async_copy(miller_hbm, miller_ref, load_sem.at[3]),
        pltpu.make_async_copy(shift_hbm, shift_ref, load_sem.at[4]),
        sup_copy,
        pltpu.make_async_copy(amp_hbm, amp, load_sem.at[5]),
        pltpu.make_async_copy(disp_hbm, own.at[pl.ds(1, 3)], load_sem.at[6]),
    ]
    for copy in first_copies:
        copy.start()
    int_copies = [
        pltpu.make_async_copy(int_hbm.at[:, pl.ds(128 * j, 128)], inten.at[j], load_sem.at[1 + j])
        for j in range(2)
    ]

    barrier = pltpu.get_barrier_semaphore()

    def greet_slab(j, carry):
        pl.semaphore_signal(
            barrier, inc=1, device_id={"slab": lax.rem(me + j, SLABS)}, device_id_type=MESH
        )
        return carry

    def greet_refl(j, carry):
        pl.semaphore_signal(
            barrier, inc=1, device_id={"refl": lax.rem(refl + j, 8)}, device_id_type=MESH
        )
        return carry

    lax.fori_loop(1, 8, greet_refl, 0)
    lax.fori_loop(1, SLABS, greet_slab, 0)
    pl.semaphore_signal(barrier, inc=1, device_id=across(1, 1), device_id_type=MESH)

    for copy in first_copies:
        copy.wait()
    for copy in int_copies:
        copy.start()
    lane_row = lax.broadcasted_iota(jnp.int32, (8, 128), 0)
    tile = jnp.where(
        lane_row == 0,
        miller_ref[0, 0].astype(F32),
        jnp.where(
            lane_row == 1,
            miller_ref[0, 1].astype(F32),
            jnp.where(lane_row == 2, miller_ref[0, 2].astype(F32), shift_ref[0].astype(F32)),
        ),
    )
    mill[yy] = tile
    mask = sup[...].astype(F32)
    own[0] = mask * amp[...]
    for f in range(4):
        for x in range(ROWS):
            at = f * 4 + x
            ey_send[0, at : at + 1, :] = own[f, x, 0:1, :]
            ey_send[1, at : at + 1, :] = own[f, x, 15:16, :]

    pl.semaphore_wait(barrier, 39)

    def remote(src, dst, sems, target):
        return pltpu.make_async_remote_copy(
            src_ref=src,
            dst_ref=dst,
            send_sem=sems.at[0],
            recv_sem=sems.at[1],
            device_id=target,
            device_id_type=MESH,
        )

    def planes(p):
        return pl.ds(WIDTH * p, WIDTH)

    raw_copies = {
        (b, q, p): remote(
            raw.at[0, 0, :, planes(p)], raw.at[b, q, :, planes(p)], raw_sem.at[b, q, p], across(b, q)
        )
        for p in range(2)
        for b, q in BLOCKS
    }

    mill_copies = [
        remote(mill.at[yy], mill.at[yy], mill_sem.at[t], peer_of(t)) for t in (1, 2, 3)
    ]
    for copy in mill_copies + list(raw_copies.values()):
        copy.start()

    has = (refl > 0, refl < 7, me > 0, me < SLABS - 1)
    down_y = remote(ey_send.at[0], ey_recv.at[1], edge_sem.at[0], {"refl": lax.rem(refl + 7, 8)})
    up_y = remote(ey_send.at[1], ey_recv.at[0], edge_sem.at[1], {"refl": lax.rem(refl + 1, 8)})
    down_x = remote(own.at[:, 0], ex_recv.at[1], edge_sem.at[2], {"slab": lax.rem(me + SLABS - 1, SLABS)})
    up_x = remote(own.at[:, 3], ex_recv.at[0], edge_sem.at[3], {"slab": lax.rem(me + 1, SLABS)})
    edges = (down_y, up_y, down_x, up_x)
    for there, copy in zip(has, edges):
        pl.when(there)(copy.start)

    def nothing(ref, at):
        def fill():
            ref[at] = jnp.zeros(ref.shape[1:], F32)
        return fill

    for there, ref, at in zip(has, (ey_recv, ey_recv, ex_recv, ex_recv), (0, 1, 0, 1)):
        pl.when(jnp.logical_not(there))(nothing(ref, at))

    def place_y(i):
        side = ((i >> 5) & 1) + zh
        return ((side & 1) * 4 + (i >> 6)) * 16 + (i & 15), (i >> 4) & 1

    def freq_y(i):
        return 8 * (TEAM * team + ((i >> 1) & 15)) + 4 * (i >> 7) + ((i >> 5) & 3), i & 1

    def freq_y_all(i):
        return 8 * ((i >> 1) & 31) + 2 * (i >> 7) + ((i >> 6) & 1), i & 1

    def place_x(i):
        side = ((i >> 6) & 1) + team
        return 64 * (side & 1) + 4 * (i & 15) + 2 * ((i >> 5) & 1) + ((i >> 4) & 1), i >> 7

    fill_table(y_fwd, (256, 256), True, freq_y, place_y, True)
    for copy in mill_copies:
        copy.wait_recv()
    lane = lax.broadcasted_iota(jnp.int32, (1, 1, 128), 2).astype(F32)

    def objects(t, p, b, q, ref):
        coef = mill[lax.rem(yy + t, 4)]
        m0, m1, m2, s = [coef[j : j + 1][None] for j in range(4)]
        turn = s * lane * (1.0 / 256.0)
        turn = turn - jnp.floor(turn)
        weight, d0, d1, d2 = [raw[b, q, f, planes(p)] for f in range(4)]
        phase = m0 * d0 + m1 * d1 + m2 * d2
        cosine, sine = cos_sin_turns(phase * (1.0 / (2 * math.pi)) + turn)
        trig[t, 0, b, q, planes(p)] = cosine
        trig[t, 1, b, q, planes(p)] = sine
        ref[0] = weight * cosine
        ref[1] = weight * sine

    obj_copies = {}

    def object_block(p, b, q):
        for t in (2, 1, 3):
            objects(t, p, b, q, obj.at[t, p, q, b])
            copy = remote(
                obj.at[t, p, q, b], obj_all.at[p, q, yy, b], peer_sem.at[p, q, b, t], peer_of(t)
            )
            copy.start()
            obj_copies[p, q, b, t] = copy
        objects(0, p, b, q, obj_all.at[p, q, yy, b])

    for p in range(2):
        object_block(p, 0, 0)
    for p in range(2):
        for b, q in BLOCKS:
            raw_copies[b, q, p].wait_recv()
            object_block(p, b, q)

    whole = slice(None)
    fwd_groups = ((whole, 0), (0, 1), (1, 1), (2, 1), (3, 1))
    halves = (pl.ds(0, 2), pl.ds(2, 2))

    def slab_sends(src, dst, sems, at, g):
        def lines(i):
            return (*at, whole, pl.ds(pl.multiple_of(lax.rem(i, TEAM) * 8, 8), 8))

        def send(j, carry):
            to = TEAM * team + lax.rem(me + j, TEAM)
            pltpu.make_async_remote_copy(
                src_ref=src.at[lines(to)],
                dst_ref=dst.at[lines(me)],
                send_sem=sems.at[0, g],
                recv_sem=sems.at[1, g],
                device_id={"slab": to},
                device_id_type=MESH,
            ).start()
            return carry

        lax.fori_loop(1, TEAM, send, 0)
        pltpu.make_async_copy(src.at[lines(me)], dst.at[lines(me)], sems.at[1, g]).start()

    def owner_sends(g):
        def lines(i):
            return (halves[g], pl.ds(pl.multiple_of(i * 8, 8), 8))

        def send(j, carry):
            to = lax.rem(me + j, SLABS)
            pltpu.make_async_remote_copy(
                src_ref=owner_send.at[lines(to)],
                dst_ref=owner_recv.at[lines(me)],
                send_sem=owner_sem.at[0, g],
                recv_sem=owner_sem.at[1, g],
                device_id={"slab": to},
                device_id_type=MESH,
            ).start()
            return carry

        lax.fori_loop(1, SLABS, send, 0)
        pltpu.make_async_copy(
            owner_send.at[lines(me)], owner_recv.at[lines(me)], owner_sem.at[1, g]
        ).start()

    def wait_sent(src, dst, sems, at, g):
        most = (*at, whole, pl.ds(0, LINES - 8))
        pltpu.make_async_copy(src.at[most], dst.at[most], sems.at[0, g]).wait()

    def wait_arrived(dst, sems, at, g):
        pltpu.make_async_copy(dst.at[at], dst.at[at], sems.at[1, g]).wait()

    for p in range(2):
        for b, q in ((0, 0), *BLOCKS):
            for t in (1, 3, 2):
                obj_copies[p, q, b, t].wait_recv()
        for q in range(2):
            columns = [obj_all[p, q, :, :, :, j].reshape(256, 128) for j in range(WIDTH)]
            bcat[q] = stacked(jnp.concatenate(columns, axis=1))
        for h in range(2):
            for q in range(2):
                out = dot(y_fwd[128 * h : 128 * (h + 1), :], bcat[q])
                for k in range(4):
                    for j in range(WIDTH):
                        fwd_send[2 * h + k // 2, p, q, pl.ds(2 * j + k % 2, 32, stride=4), :] = out[
                            32 * k : 32 * (k + 1), 128 * j : 128 * (j + 1)
                        ]
            if p == 1:
                for g in (2 * h + 1, 2 * h + 2):
                    slab_sends(fwd_send, fwd_recv, slab_sem, fwd_groups[g], g)
        if p == 0:
            slab_sends(fwd_send, fwd_recv, slab_sem, fwd_groups[0], 0)

    fill_table(x_fwd, (512, 256), True, freq_plain, place_x, True)
    fill_table(z_fwd, (256, 512), False, freq_plain, place_plain, False)
    fill_table(x_back, (256, 512), False, freq_plain, place_x, True)
    fill_table(z_back, (512, 256), True, freq_plain, place_plain, False)
    fill_table(y_back, (256, 256), False, freq_y, place_y, True)
    fill_table(y_back_all, (256, 512), False, freq_y_all, place_y, True)
    for copy in int_copies:
        copy.wait()

    wait_arrived(fwd_recv, slab_sem, fwd_groups[0], 0)
    for h in range(GROUPS):
        wait_arrived(fwd_recv, slab_sem, fwd_groups[1 + h], 1 + h)
        sides = [
            jnp.concatenate(
                [
                    fwd_recv[h, p, q, pl.ds(c * 4 + 2 * j + k, 16, stride=8), :]
                    for k in range(2)
                    for q in range(2)
                    for p in range(2)
                    for j in range(WIDTH)
                ],
                axis=0,
            )
            for c in range(2)
        ]
        zed[h % 2] = dot(abreast(jnp.concatenate(sides, axis=1)), z_fwd[...])
        for k in range(2):
            lines = slice(128 * k, 128 * (k + 1))
            spec = dot(
                x_fwd[...],
                stacked(
                    jnp.concatenate([zed[h % 2, lines, :256], zed[h % 2, lines, 256:]], axis=0)
                ),
            )
            real, imag = spec[:256], spec[256:]
            measured = jnp.concatenate(
                [inten[j, pl.ds(2 * h + k, 256, stride=8), :] for j in range(2)], axis=1
            )
            excess = 4.0 * (real * real + imag * imag - measured)
            residual = jnp.concatenate([excess * real, excess * imag], axis=0)
            back = dot(x_back[...], stacked(residual))
            for c in range(2):
                high, low = split(back[128 * c : 128 * (c + 1)])
                zedb[h % 2, lines, 256 * c : 256 * (c + 1)] = high
                zedb[h % 2, lines, 512 + 256 * c : 512 + 256 * (c + 1)] = low
                zedb[h % 2, lines, 1024 + 256 * c : 1024 + 256 * (c + 1)] = high
        out = dot(zedb[h % 2], z_back[...])
        for k in range(2):
            for c in range(2):
                for at in range(8):
                    q, p, j = at // 4, at // 2 % 2, at % 2
                    first = 128 * k + 16 * at
                    value = out[first : first + 16, 128 * c : 128 * (c + 1)]
                    line = c * 4 + 2 * j + k
                    if p == 0:
                        back_send[h, q, pl.ds(line, 16, stride=8), :] = value
                    else:
                        line = LINES * lax.rem(q + team, 2) + line
                        owner_send[h, pl.ds(line, 16, stride=8), :] = value
        slab_sends(back_send, back_recv, slab_back_sem, (h,), h)
        if h % 2 == 1:
            owner_sends(h // 2)

    for there, copy in ((has[0], up_y), (has[1], down_y), (has[2], up_x), (has[3], down_x)):
        pl.when(there)(copy.wait_recv)
    sub = lax.broadcasted_iota(jnp.int32, (ROWS, 16, 128), 1)
    last = lax.broadcasted_iota(jnp.int32, (ROWS, 16, 128), 2)
    for f in range(4):
        x = own[f]
        beside = jnp.concatenate([ex_recv[0, f][None], x[:3]], axis=0)
        beside = beside + jnp.concatenate([x[1:], ex_recv[1, f][None]], axis=0)
        low = ey_recv[0, 4 * f : 4 * f + 4, :][:, None, :]
        high = ey_recv[1, 4 * f : 4 * f + 4, :][:, None, :]
        beside = beside + jnp.where(sub == 0, low, pltpu.roll(x, 1, 1))
        beside = beside + jnp.where(sub == 15, high, pltpu.roll(x, 15, 1))
        beside = beside + jnp.where(last == 0, 0.0, pltpu.roll(x, 1, 2))
        beside = beside + jnp.where(last == 127, 0.0, pltpu.roll(x, 127, 2))
        lapped[f] = 2.0 * (EDGE_WEIGHT if f == 0 else STRAIN_WEIGHT) * (6.0 * x - beside)

    done_copies = {}

    def done_send(p, q, b):
        for t in (2, 1, 3):
            copy = remote(
                ydone.at[p, q, lax.rem(yy + t, 4), b],
                ydone_all.at[p, q, 4 - t, b],
                peer_back_sem.at[p, q, b, t],
                peer_of(t),
            )
            copy.start()
            done_copies[p, q, b, t] = copy

    def why_back(p, q, table, load):
        columns = [
            jnp.concatenate(
                [load(h, 2 * j + k) for h in range(GROUPS) for k in range(2)], axis=0
            )
            for j in range(WIDTH)
        ]
        out = dot(table[...], stacked(jnp.concatenate(columns, axis=1)))
        for j in range(WIDTH):
            ydone[p, q, :, :, :, j] = out[:, 128 * j : 128 * (j + 1)].reshape(4, 2, 2, 16, 128)

    for g in range(GROUPS):
        wait_arrived(back_recv, slab_back_sem, (g,), g)
    for q in range(2):
        why_back(0, q, y_back, lambda h, line: back_recv[h, q, pl.ds(line, 32, stride=4), :])
    for b, q in ((1, 0), (1, 1), (0, 1)):
        done_send(0, q, b)
    for g in range(2):
        pltpu.make_async_copy(
            owner_recv.at[halves[g]], owner_recv.at[halves[g]], owner_sem.at[1, g]
        ).wait()
    why_back(1, 0, y_back_all, lambda h, line: owner_recv[h, pl.ds(line, 64, stride=4), :])
    done_send(1, 0, 1)
    done_send(0, 0, 0)
    done_send(1, 0, 0)

    def summed(b, q, p):
        for t in (1, 3, 2):
            done_copies[p, q, b, t].wait_recv()
        totals = [jnp.zeros((WIDTH, 16, 128), F32) for _ in range(4)]
        for t in range(4):
            if t == 0:
                real, imag = ydone[p, q, yy, b, 0], ydone[p, q, yy, b, 1]
            else:
                real, imag = ydone_all[p, q, t, b, 0], ydone_all[p, q, t, b, 1]
            cosine, sine = trig[t, 0, b, q, planes(p)], trig[t, 1, b, q, planes(p)]
            coef = mill[lax.rem(yy + t, 4)]
            across = imag * cosine - real * sine
            totals[0] = totals[0] + real * cosine + imag * sine
            for c in range(3):
                totals[1 + c] = totals[1 + c] + coef[c : c + 1][None] * across
        return totals

    part_copies = {}
    for b, q, p in ((1, 0, 0), (1, 1, 0), (0, 1, 0), (1, 0, 1)):
        for f, total in enumerate(summed(b, q, p)):
            part[b, q, p, f] = total
        copy = remote(part.at[b, q, p], part_recv.at[b, q, p], part_sem.at[b, q, p], across(b, q))
        copy.start()
        part_copies[b, q, p] = copy

    for p in range(2):
        sums = summed(0, 0, p)
        for b, q in BLOCKS if p == 0 else BLOCKS[2:]:
            part_copies[b, q, p].wait_recv()
            sums = [sums[f] + part_recv[b, q, p, f] for f in range(4)]
        mask = sup[planes(p)].astype(F32)
        amp_out[planes(p)] = mask * (sums[0] + lapped[0, planes(p)])
        for c in range(3):
            disp_out[c, planes(p)] = (
                own[0, planes(p)] * sums[1 + c] + lapped[1 + c, planes(p)]
            )

    for copy in (*mill_copies, *raw_copies.values(), *part_copies.values()):
        copy.wait_send()
    for there, copy in zip(has, edges):
        pl.when(there)(copy.wait_send)
    for copy in (*obj_copies.values(), *done_copies.values()):
        copy.wait_send()
    for g in range(GROUPS + 1):
        wait_sent(fwd_send, fwd_recv, slab_sem, fwd_groups[g], g)
    for g in range(GROUPS):
        wait_sent(back_send, back_recv, slab_back_sem, (g,), g)
    for g in range(2):
        most = (halves[g], pl.ds(0, 2 * LINES - 8))
        pltpu.make_async_copy(owner_send.at[most], owner_recv.at[most], owner_sem.at[0, g]).wait()


def body(amplitude, displacement, support, miller, shift_kz, intensity):
    vmem = pl.BlockSpec(memory_space=pltpu.VMEM)
    anywhere = pl.BlockSpec(memory_space=pl.ANY)
    block = (ROWS, 16, 128)
    chunk = (WIDTH, 16, 128)
    sems = pltpu.SemaphoreType.DMA
    return pl.pallas_call(
        kernel,
        out_shape=(
            jax.ShapeDtypeStruct(block, F32),
            jax.ShapeDtypeStruct((3, *block), F32),
        ),
        in_specs=[anywhere] * 6,
        out_specs=(vmem, vmem),
        scratch_shapes=[
            pltpu.VMEM(block, F32),
            pltpu.SMEM((1, 3), jnp.int32),
            pltpu.SMEM((1,), jnp.int32),
            pltpu.VMEM(block, jnp.int32),
            pltpu.VMEM((2, 2048, 128), F32),
            pltpu.VMEM((2, 2, 4, *block), F32),
            pltpu.VMEM((4, 8, 128), F32),
            pltpu.VMEM((2, 16, 128), F32),
            pltpu.VMEM((2, 16, 128), F32),
            pltpu.VMEM((2, 4, 16, 128), F32),
            pltpu.VMEM((4, 2, 2, 2, *block), F32),
            pltpu.VMEM((4, 2, 2, 2, 2, *chunk), F32),
            pltpu.VMEM((2, 2, 4, 2, 2, *chunk), F32),
            pltpu.VMEM((2, 768, 256), BF16),
            pltpu.VMEM((GROUPS, 2, 2, LINES, 128), F32),
            pltpu.VMEM((GROUPS, 2, 2, LINES, 128), F32),
            pltpu.VMEM((2, 256, 512), F32),
            pltpu.VMEM((2, 256, 1536), BF16),
            pltpu.VMEM((GROUPS, 2, LINES, 128), F32),
            pltpu.VMEM((GROUPS, 2, LINES, 128), F32),
            pltpu.VMEM((GROUPS, 2 * LINES, 128), F32),
            pltpu.VMEM((GROUPS, 2 * LINES, 128), F32),
            pltpu.VMEM((2, 2, 4, 2, 2, *chunk), F32),
            pltpu.VMEM((2, 2, 4, 2, 2, *chunk), F32),
            pltpu.VMEM((2, 2, 2, 4, *chunk), F32),
            pltpu.VMEM((2, 2, 2, 4, *chunk), F32),
            pltpu.VMEM((4, *block), F32),
            pltpu.VMEM((256, 768), BF16),
            pltpu.VMEM((256, 768), BF16),
            pltpu.VMEM((256, 1536), BF16),
            pltpu.VMEM((512, 768), BF16),
            pltpu.VMEM((256, 1536), BF16),
            pltpu.VMEM((768, 512), BF16),
            pltpu.VMEM((1536, 256), BF16),
            sems((7,)),
            sems((2, 2, 2, 2)),
            sems((4, 2)),
            sems((4, 2)),
            sems((2, 2, 2, 4, 2)),
            sems((2, 2, 2, 4, 2)),
            sems((2, GROUPS + 1)),
            sems((2, GROUPS)),
            sems((2, 2)),
            sems((2, 2, 2, 2)),
        ],
        compiler_params=pltpu.CompilerParams(
            collective_id=0, has_side_effects=True, vmem_limit_bytes=56 * 1024 * 1024
        ),
        name="gradient",
    )(amplitude, displacement, support, miller, shift_kz, intensity.reshape(2048, 256))


def solution(mesh):
    placed = (
        P("slab", "refl", None),
        P(None, "slab", "refl", None),
        P("slab", None, None),
        P("refl", None),
        P("refl"),
        P("refl", None, "slab", None),
    )
    return jax.shard_map(
        body,
        mesh=mesh,
        in_specs=placed,
        out_specs=(P("slab", "refl", None), P(None, "slab", "refl", None)),
        check_vma=False,
    )
```

```python
import math

import jax
import jax.numpy as jnp
from jax import lax
from jax.experimental import pallas as pl
from jax.experimental.pallas import tpu as pltpu
from jax.sharding import PartitionSpec as P

MESH = pl.DeviceIdType.MESH
F32 = jnp.float32
BF16 = jnp.bfloat16
STRAIN_WEIGHT = 0.05
EDGE_WEIGHT = 0.05
SLABS = 32
ROWS = 4
WIDTH = 2
TEAM = SLABS // 2
GROUPS = 4
LINES = TEAM * 8
BLOCKS = ((0, 1), (1, 1), (1, 0))


def sine_turns(v):
    w = v * v
    total = jnp.full_like(v, -((2 * math.pi) ** 11) / math.factorial(11))
    for power in (9, 7, 5, 3, 1):
        sign = 1.0 if power % 4 == 1 else -1.0
        total = total * w + sign * (2 * math.pi) ** power / math.factorial(power)
    return total * v


def cos_sin_turns(t):
    t = t - jnp.floor(t + 0.5)
    size = jnp.abs(t)
    cosine = sine_turns(0.25 - size)
    sine = sine_turns(0.25 - jnp.abs(size - 0.25))
    return cosine, jnp.where(t < 0.0, -sine, sine)


def split(x):
    high = x.astype(BF16)
    low = (x - high.astype(F32)).astype(BF16)
    return high, low


def stacked(x):
    high, low = split(x)
    return jnp.concatenate([high, low, high], axis=0)


def abreast(x):
    high, low = split(x)
    return jnp.concatenate([high, low, high], axis=1)


def dot(a, b):
    return jnp.dot(a, b, preferred_element_type=F32)


def freq_plain(i):
    return i & 255, i >> 8


def place_plain(i):
    return i & 127, i >> 7


def fill_table(ref, shape, row_is_freq, freq, place, on_left):
    rows, cols = shape
    chunk = 32

    def step(j, carry):
        start = pl.multiple_of(j * chunk, chunk)
        row = lax.broadcasted_iota(jnp.int32, (chunk, cols), 0) + start
        col = lax.broadcasted_iota(jnp.int32, (chunk, cols), 1)
        if row_is_freq:
            k, kc = freq(row)
            n, nc = place(col)
        else:
            k, kc = freq(col)
            n, nc = place(row)
        turns = ((k * n + 64 * (kc - nc) + 128) & 255) - 128
        t = turns.astype(F32) * (1.0 / 256.0)
        high, low = split(sine_turns(0.25 - jnp.abs(t)) * (1.0 / 16.0))
        if on_left:
            ref[pl.ds(start, chunk), 0:cols] = high
            ref[pl.ds(start, chunk), cols : 2 * cols] = high
            ref[pl.ds(start, chunk), 2 * cols : 3 * cols] = low
        else:
            ref[pl.ds(start, chunk), :] = high
            ref[pl.ds(pl.multiple_of(rows + start, chunk), chunk), :] = high
            ref[pl.ds(pl.multiple_of(2 * rows + start, chunk), chunk), :] = low
        return carry

    lax.fori_loop(0, rows // chunk, step, 0)


def kernel(
    amp_hbm, disp_hbm, sup_hbm, miller_hbm, shift_hbm, int_hbm,
    amp_out, disp_out,
    amp, miller_ref, shift_ref, sup, inten, raw, mill, ey_send, ey_recv, ex_recv, trig, obj, obj_all, bcat,
    fwd_send, fwd_recv, zed, zedb, back_send, back_recv, owner_send, owner_recv, ydone, ydone_all, part, part_recv, lapped,
    y_fwd, y_back, y_back_all, x_fwd, x_back, z_fwd, z_back,
    load_sem, raw_sem, mill_sem, edge_sem, peer_sem, peer_back_sem, slab_sem, slab_back_sem, owner_sem, part_sem,
):
    refl = lax.axis_index("refl")
    me = lax.axis_index("slab")
    zh = refl // 4
    yy = lax.rem(refl, 4)
    team = me // TEAM
    own = raw.at[0, 0]

    def peer_of(t):
        return {"refl": zh * 4 + lax.rem(yy + t, 4)}

    def across(b, q):
        return {"refl": lax.rem(refl + 4 * b, 8), "slab": lax.rem(me + TEAM * q, SLABS)}

    sup_copy = pltpu.make_async_copy(
        sup_hbm.at[:, pl.ds(pl.multiple_of(refl * 16, 16), 16), :], sup, load_sem.at[0]
    )
    first_copies = [
        pltpu.make_async_copy(miller_hbm, miller_ref, load_sem.at[3]),
        pltpu.make_async_copy(shift_hbm, shift_ref, load_sem.at[4]),
        sup_copy,
        pltpu.make_async_copy(amp_hbm, amp, load_sem.at[5]),
        pltpu.make_async_copy(disp_hbm, own.at[pl.ds(1, 3)], load_sem.at[6]),
    ]
    for copy in first_copies:
        copy.start()
    int_copies = [
        pltpu.make_async_copy(int_hbm.at[:, pl.ds(128 * j, 128)], inten.at[j], load_sem.at[1 + j])
        for j in range(2)
    ]

    barrier = pltpu.get_barrier_semaphore()

    def greet_slab(j, carry):
        pl.semaphore_signal(
            barrier, inc=1, device_id={"slab": lax.rem(me + j, SLABS)}, device_id_type=MESH
        )
        return carry

    def greet_refl(j, carry):
        pl.semaphore_signal(
            barrier, inc=1, device_id={"refl": lax.rem(refl + j, 8)}, device_id_type=MESH
        )
        return carry

    lax.fori_loop(1, 8, greet_refl, 0)
    lax.fori_loop(1, SLABS, greet_slab, 0)
    pl.semaphore_signal(barrier, inc=1, device_id=across(1, 1), device_id_type=MESH)

    for copy in first_copies:
        copy.wait()
    for copy in int_copies:
        copy.start()
    lane_row = lax.broadcasted_iota(jnp.int32, (8, 128), 0)
    tile = jnp.where(
        lane_row == 0,
        miller_ref[0, 0].astype(F32),
        jnp.where(
            lane_row == 1,
            miller_ref[0, 1].astype(F32),
            jnp.where(lane_row == 2, miller_ref[0, 2].astype(F32), shift_ref[0].astype(F32)),
        ),
    )
    mill[yy] = tile
    mask = sup[...].astype(F32)
    own[0] = mask * amp[...]
    for f in range(4):
        for x in range(ROWS):
            at = f * 4 + x
            ey_send[0, at : at + 1, :] = own[f, x, 0:1, :]
            ey_send[1, at : at + 1, :] = own[f, x, 15:16, :]

    pl.semaphore_wait(barrier, 39)

    def remote(src, dst, sems, target):
        return pltpu.make_async_remote_copy(
            src_ref=src,
            dst_ref=dst,
            send_sem=sems.at[0],
            recv_sem=sems.at[1],
            device_id=target,
            device_id_type=MESH,
        )

    def planes(p):
        return pl.ds(WIDTH * p, WIDTH)

    raw_copies = {
        (b, q, p): remote(
            raw.at[0, 0, :, planes(p)], raw.at[b, q, :, planes(p)], raw_sem.at[b, q, p], across(b, q)
        )
        for p in range(2)
        for b, q in BLOCKS
    }

    mill_copies = [
        remote(mill.at[yy], mill.at[yy], mill_sem.at[t], peer_of(t)) for t in (1, 2, 3)
    ]
    for copy in mill_copies + list(raw_copies.values()):
        copy.start()

    has = (refl > 0, refl < 7, me > 0, me < SLABS - 1)
    down_y = remote(ey_send.at[0], ey_recv.at[1], edge_sem.at[0], {"refl": lax.rem(refl + 7, 8)})
    up_y = remote(ey_send.at[1], ey_recv.at[0], edge_sem.at[1], {"refl": lax.rem(refl + 1, 8)})
    down_x = remote(own.at[:, 0], ex_recv.at[1], edge_sem.at[2], {"slab": lax.rem(me + SLABS - 1, SLABS)})
    up_x = remote(own.at[:, 3], ex_recv.at[0], edge_sem.at[3], {"slab": lax.rem(me + 1, SLABS)})
    edges = (down_y, up_y, down_x, up_x)
    for there, copy in zip(has, edges):
        pl.when(there)(copy.start)

    def nothing(ref, at):
        def fill():
            ref[at] = jnp.zeros(ref.shape[1:], F32)
        return fill

    for there, ref, at in zip(has, (ey_recv, ey_recv, ex_recv, ex_recv), (0, 1, 0, 1)):
        pl.when(jnp.logical_not(there))(nothing(ref, at))

    def place_y(i):
        side = ((i >> 5) & 1) + zh
        return ((side & 1) * 4 + (i >> 6)) * 16 + (i & 15), (i >> 4) & 1

    def freq_y(i):
        return 8 * (TEAM * team + ((i >> 1) & 15)) + 4 * (i >> 7) + ((i >> 5) & 3), i & 1

    def freq_y_all(i):
        return 8 * ((i >> 1) & 31) + 2 * (i >> 7) + ((i >> 6) & 1), i & 1

    def place_x(i):
        side = ((i >> 6) & 1) + team
        return 64 * (side & 1) + 4 * (i & 15) + 2 * ((i >> 5) & 1) + ((i >> 4) & 1), i >> 7

    fill_table(y_fwd, (256, 256), True, freq_y, place_y, True)
    for copy in mill_copies:
        copy.wait_recv()
    lane = lax.broadcasted_iota(jnp.int32, (1, 1, 128), 2).astype(F32)

    def objects(t, p, b, q, ref):
        coef = mill[lax.rem(yy + t, 4)]
        m0, m1, m2, s = [coef[j : j + 1][None] for j in range(4)]
        turn = s * lane * (1.0 / 256.0)
        turn = turn - jnp.floor(turn)
        weight, d0, d1, d2 = [raw[b, q, f, planes(p)] for f in range(4)]
        phase = m0 * d0 + m1 * d1 + m2 * d2
        cosine, sine = cos_sin_turns(phase * (1.0 / (2 * math.pi)) + turn)
        trig[t, 0, b, q, planes(p)] = cosine
        trig[t, 1, b, q, planes(p)] = sine
        ref[0] = weight * cosine
        ref[1] = weight * sine

    obj_copies = {}

    def object_block(p, b, q):
        for t in (2, 1, 3):
            objects(t, p, b, q, obj.at[t, p, q, b])
            copy = remote(
                obj.at[t, p, q, b], obj_all.at[p, q, yy, b], peer_sem.at[p, q, b, t], peer_of(t)
            )
            copy.start()
            obj_copies[p, q, b, t] = copy
        objects(0, p, b, q, obj_all.at[p, q, yy, b])

    for p in range(2):
        object_block(p, 0, 0)
    fill_table(x_fwd, (512, 256), True, freq_plain, place_x, True)
    fill_table(z_fwd, (256, 512), False, freq_plain, place_plain, False)
    fill_table(x_back, (256, 512), False, freq_plain, place_x, True)
    for p in range(2):
        for b, q in BLOCKS:
            raw_copies[b, q, p].wait_recv()
            object_block(p, b, q)

    whole = slice(None)
    fwd_groups = ((whole, 0), (0, 1), (1, 1), (2, 1), (3, 1))
    halves = (pl.ds(0, 2), pl.ds(2, 2))

    def slab_sends(src, dst, sems, at, g):
        def lines(i):
            return (*at, whole, pl.ds(pl.multiple_of(lax.rem(i, TEAM) * 8, 8), 8))

        def send(j, carry):
            to = TEAM * team + lax.rem(me + j, TEAM)
            pltpu.make_async_remote_copy(
                src_ref=src.at[lines(to)],
                dst_ref=dst.at[lines(me)],
                send_sem=sems.at[0, g],
                recv_sem=sems.at[1, g],
                device_id={"slab": to},
                device_id_type=MESH,
            ).start()
            return carry

        lax.fori_loop(1, TEAM, send, 0)
        pltpu.make_async_copy(src.at[lines(me)], dst.at[lines(me)], sems.at[1, g]).start()

    def owner_sends(g):
        def lines(i):
            return (halves[g], pl.ds(pl.multiple_of(i * 8, 8), 8))

        def send(j, carry):
            to = lax.rem(me + j, SLABS)
            pltpu.make_async_remote_copy(
                src_ref=owner_send.at[lines(to)],
                dst_ref=owner_recv.at[lines(me)],
                send_sem=owner_sem.at[0, g],
                recv_sem=owner_sem.at[1, g],
                device_id={"slab": to},
                device_id_type=MESH,
            ).start()
            return carry

        lax.fori_loop(1, SLABS, send, 0)
        pltpu.make_async_copy(
            owner_send.at[lines(me)], owner_recv.at[lines(me)], owner_sem.at[1, g]
        ).start()

    def wait_sent(src, dst, sems, at, g):
        most = (*at, whole, pl.ds(0, LINES - 8))
        pltpu.make_async_copy(src.at[most], dst.at[most], sems.at[0, g]).wait()

    def wait_arrived(dst, sems, at, g):
        pltpu.make_async_copy(dst.at[at], dst.at[at], sems.at[1, g]).wait()

    for p in range(2):
        for b, q in ((0, 0), *BLOCKS):
            for t in (1, 3, 2):
                obj_copies[p, q, b, t].wait_recv()
        for q in range(2):
            columns = [obj_all[p, q, :, :, :, j].reshape(256, 128) for j in range(WIDTH)]
            bcat[q] = stacked(jnp.concatenate(columns, axis=1))
        for h in range(2):
            for q in range(2):
                out = dot(y_fwd[128 * h : 128 * (h + 1), :], bcat[q])
                for k in range(4):
                    for j in range(WIDTH):
                        fwd_send[2 * h + k // 2, p, q, pl.ds(2 * j + k % 2, 32, stride=4), :] = out[
                            32 * k : 32 * (k + 1), 128 * j : 128 * (j + 1)
                        ]
            if p == 1:
                for g in (2 * h + 1, 2 * h + 2):
                    slab_sends(fwd_send, fwd_recv, slab_sem, fwd_groups[g], g)
        if p == 0:
            slab_sends(fwd_send, fwd_recv, slab_sem, fwd_groups[0], 0)

    fill_table(z_back, (512, 256), True, freq_plain, place_plain, False)
    fill_table(y_back, (256, 256), False, freq_y, place_y, True)
    fill_table(y_back_all, (256, 512), False, freq_y_all, place_y, True)
    for copy in int_copies:
        copy.wait()

    wait_arrived(fwd_recv, slab_sem, fwd_groups[0], 0)
    for h in range(GROUPS):
        wait_arrived(fwd_recv, slab_sem, fwd_groups[1 + h], 1 + h)
        sides = [
            jnp.concatenate(
                [
                    fwd_recv[h, p, q, pl.ds(c * 4 + 2 * j + k, 16, stride=8), :]
                    for k in range(2)
                    for q in range(2)
                    for p in range(2)
                    for j in range(WIDTH)
                ],
                axis=0,
            )
            for c in range(2)
        ]
        zed[h % 2] = dot(abreast(jnp.concatenate(sides, axis=1)), z_fwd[...])
        for k in range(2):
            lines = slice(128 * k, 128 * (k + 1))
            spec = dot(
                x_fwd[...],
                stacked(
                    jnp.concatenate([zed[h % 2, lines, :256], zed[h % 2, lines, 256:]], axis=0)
                ),
            )
            real, imag = spec[:256], spec[256:]
            measured = jnp.concatenate(
                [inten[j, pl.ds(2 * h + k, 256, stride=8), :] for j in range(2)], axis=1
            )
            excess = 4.0 * (real * real + imag * imag - measured)
            residual = jnp.concatenate([excess * real, excess * imag], axis=0)
            back = dot(x_back[...], stacked(residual))
            for c in range(2):
                high, low = split(back[128 * c : 128 * (c + 1)])
                zedb[h % 2, lines, 256 * c : 256 * (c + 1)] = high
                zedb[h % 2, lines, 512 + 256 * c : 512 + 256 * (c + 1)] = low
                zedb[h % 2, lines, 1024 + 256 * c : 1024 + 256 * (c + 1)] = high
        out = dot(zedb[h % 2], z_back[...])
        for k in range(2):
            for c in range(2):
                for at in range(8):
                    q, p, j = at // 4, at // 2 % 2, at % 2
                    first = 128 * k + 16 * at
                    value = out[first : first + 16, 128 * c : 128 * (c + 1)]
                    line = c * 4 + 2 * j + k
                    if p == 0:
                        back_send[h, q, pl.ds(line, 16, stride=8), :] = value
                    else:
                        line = LINES * lax.rem(q + team, 2) + line
                        owner_send[h, pl.ds(line, 16, stride=8), :] = value
        slab_sends(back_send, back_recv, slab_back_sem, (h,), h)
        if h % 2 == 1:
            owner_sends(h // 2)

    for there, copy in ((has[0], up_y), (has[1], down_y), (has[2], up_x), (has[3], down_x)):
        pl.when(there)(copy.wait_recv)
    sub = lax.broadcasted_iota(jnp.int32, (ROWS, 16, 128), 1)
    last = lax.broadcasted_iota(jnp.int32, (ROWS, 16, 128), 2)
    for f in range(4):
        x = own[f]
        beside = jnp.concatenate([ex_recv[0, f][None], x[:3]], axis=0)
        beside = beside + jnp.concatenate([x[1:], ex_recv[1, f][None]], axis=0)
        low = ey_recv[0, 4 * f : 4 * f + 4, :][:, None, :]
        high = ey_recv[1, 4 * f : 4 * f + 4, :][:, None, :]
        beside = beside + jnp.where(sub == 0, low, pltpu.roll(x, 1, 1))
        beside = beside + jnp.where(sub == 15, high, pltpu.roll(x, 15, 1))
        beside = beside + jnp.where(last == 0, 0.0, pltpu.roll(x, 1, 2))
        beside = beside + jnp.where(last == 127, 0.0, pltpu.roll(x, 127, 2))
        lapped[f] = 2.0 * (EDGE_WEIGHT if f == 0 else STRAIN_WEIGHT) * (6.0 * x - beside)

    done_copies = {}

    def done_send(p, q, b):
        for t in (2, 1, 3):
            copy = remote(
                ydone.at[p, q, lax.rem(yy + t, 4), b],
                ydone_all.at[p, q, 4 - t, b],
                peer_back_sem.at[p, q, b, t],
                peer_of(t),
            )
            copy.start()
            done_copies[p, q, b, t] = copy

    def why_back(p, q, table, load):
        columns = [
            jnp.concatenate(
                [load(h, 2 * j + k) for h in range(GROUPS) for k in range(2)], axis=0
            )
            for j in range(WIDTH)
        ]
        out = dot(table[...], stacked(jnp.concatenate(columns, axis=1)))
        for j in range(WIDTH):
            ydone[p, q, :, :, :, j] = out[:, 128 * j : 128 * (j + 1)].reshape(4, 2, 2, 16, 128)

    for g in range(GROUPS):
        wait_arrived(back_recv, slab_back_sem, (g,), g)
    for q in range(2):
        why_back(0, q, y_back, lambda h, line: back_recv[h, q, pl.ds(line, 32, stride=4), :])
    for b, q in ((1, 0), (1, 1), (0, 1)):
        done_send(0, q, b)
    done_send(0, 0, 0)
    for g in range(2):
        pltpu.make_async_copy(
            owner_recv.at[halves[g]], owner_recv.at[halves[g]], owner_sem.at[1, g]
        ).wait()
    why_back(1, 0, y_back_all, lambda h, line: owner_recv[h, pl.ds(line, 64, stride=4), :])
    done_send(1, 0, 1)
    done_send(1, 0, 0)

    def summed(b, q, p):
        for t in (1, 3, 2):
            done_copies[p, q, b, t].wait_recv()
        totals = [jnp.zeros((WIDTH, 16, 128), F32) for _ in range(4)]
        for t in range(4):
            if t == 0:
                real, imag = ydone[p, q, yy, b, 0], ydone[p, q, yy, b, 1]
            else:
                real, imag = ydone_all[p, q, t, b, 0], ydone_all[p, q, t, b, 1]
            cosine, sine = trig[t, 0, b, q, planes(p)], trig[t, 1, b, q, planes(p)]
            coef = mill[lax.rem(yy + t, 4)]
            across = imag * cosine - real * sine
            totals[0] = totals[0] + real * cosine + imag * sine
            for c in range(3):
                totals[1 + c] = totals[1 + c] + coef[c : c + 1][None] * across
        return totals

    part_copies = {}
    for b, q, p in ((1, 0, 0), (1, 1, 0), (0, 1, 0), (1, 0, 1)):
        for f, total in enumerate(summed(b, q, p)):
            part[b, q, p, f] = total
        copy = remote(part.at[b, q, p], part_recv.at[b, q, p], part_sem.at[b, q, p], across(b, q))
        copy.start()
        part_copies[b, q, p] = copy

    for p in range(2):
        sums = summed(0, 0, p)
        for b, q in BLOCKS if p == 0 else BLOCKS[2:]:
            part_copies[b, q, p].wait_recv()
            sums = [sums[f] + part_recv[b, q, p, f] for f in range(4)]
        mask = sup[planes(p)].astype(F32)
        amp_out[planes(p)] = mask * (sums[0] + lapped[0, planes(p)])
        for c in range(3):
            disp_out[c, planes(p)] = (
                own[0, planes(p)] * sums[1 + c] + lapped[1 + c, planes(p)]
            )

    for copy in (*mill_copies, *raw_copies.values(), *part_copies.values()):
        copy.wait_send()
    for there, copy in zip(has, edges):
        pl.when(there)(copy.wait_send)
    for copy in (*obj_copies.values(), *done_copies.values()):
        copy.wait_send()
    for g in range(GROUPS + 1):
        wait_sent(fwd_send, fwd_recv, slab_sem, fwd_groups[g], g)
    for g in range(GROUPS):
        wait_sent(back_send, back_recv, slab_back_sem, (g,), g)
    for g in range(2):
        most = (halves[g], pl.ds(0, 2 * LINES - 8))
        pltpu.make_async_copy(owner_send.at[most], owner_recv.at[most], owner_sem.at[0, g]).wait()


def body(amplitude, displacement, support, miller, shift_kz, intensity):
    vmem = pl.BlockSpec(memory_space=pltpu.VMEM)
    anywhere = pl.BlockSpec(memory_space=pl.ANY)
    block = (ROWS, 16, 128)
    chunk = (WIDTH, 16, 128)
    sems = pltpu.SemaphoreType.DMA
    return pl.pallas_call(
        kernel,
        out_shape=(
            jax.ShapeDtypeStruct(block, F32),
            jax.ShapeDtypeStruct((3, *block), F32),
        ),
        in_specs=[anywhere] * 6,
        out_specs=(vmem, vmem),
        scratch_shapes=[
            pltpu.VMEM(block, F32),
            pltpu.SMEM((1, 3), jnp.int32),
            pltpu.SMEM((1,), jnp.int32),
            pltpu.VMEM(block, jnp.int32),
            pltpu.VMEM((2, 2048, 128), F32),
            pltpu.VMEM((2, 2, 4, *block), F32),
            pltpu.VMEM((4, 8, 128), F32),
            pltpu.VMEM((2, 16, 128), F32),
            pltpu.VMEM((2, 16, 128), F32),
            pltpu.VMEM((2, 4, 16, 128), F32),
            pltpu.VMEM((4, 2, 2, 2, *block), F32),
            pltpu.VMEM((4, 2, 2, 2, 2, *chunk), F32),
            pltpu.VMEM((2, 2, 4, 2, 2, *chunk), F32),
            pltpu.VMEM((2, 768, 256), BF16),
            pltpu.VMEM((GROUPS, 2, 2, LINES, 128), F32),
            pltpu.VMEM((GROUPS, 2, 2, LINES, 128), F32),
            pltpu.VMEM((2, 256, 512), F32),
            pltpu.VMEM((2, 256, 1536), BF16),
            pltpu.VMEM((GROUPS, 2, LINES, 128), F32),
            pltpu.VMEM((GROUPS, 2, LINES, 128), F32),
            pltpu.VMEM((GROUPS, 2 * LINES, 128), F32),
            pltpu.VMEM((GROUPS, 2 * LINES, 128), F32),
            pltpu.VMEM((2, 2, 4, 2, 2, *chunk), F32),
            pltpu.VMEM((2, 2, 4, 2, 2, *chunk), F32),
            pltpu.VMEM((2, 2, 2, 4, *chunk), F32),
            pltpu.VMEM((2, 2, 2, 4, *chunk), F32),
            pltpu.VMEM((4, *block), F32),
            pltpu.VMEM((256, 768), BF16),
            pltpu.VMEM((256, 768), BF16),
            pltpu.VMEM((256, 1536), BF16),
            pltpu.VMEM((512, 768), BF16),
            pltpu.VMEM((256, 1536), BF16),
            pltpu.VMEM((768, 512), BF16),
            pltpu.VMEM((1536, 256), BF16),
            sems((7,)),
            sems((2, 2, 2, 2)),
            sems((4, 2)),
            sems((4, 2)),
            sems((2, 2, 2, 4, 2)),
            sems((2, 2, 2, 4, 2)),
            sems((2, GROUPS + 1)),
            sems((2, GROUPS)),
            sems((2, 2)),
            sems((2, 2, 2, 2)),
        ],
        compiler_params=pltpu.CompilerParams(
            collective_id=0, has_side_effects=True, vmem_limit_bytes=56 * 1024 * 1024
        ),
        name="gradient",
    )(amplitude, displacement, support, miller, shift_kz, intensity.reshape(2048, 256))


def solution(mesh):
    placed = (
        P("slab", "refl", None),
        P(None, "slab", "refl", None),
        P("slab", None, None),
        P("refl", None),
        P("refl"),
        P("refl", None, "slab", None),
    )
    return jax.shard_map(
        body,
        mesh=mesh,
        in_specs=placed,
        out_specs=(P("slab", "refl", None), P(None, "slab", "refl", None)),
        check_vma=False,
    )
```
